32 devices in a mesh: dp: 8 (over y, x, core), tensor: 4 (over z).
Axes of the slice: x: 2, y: 2, z: 4, core: 2. Of those that a mesh axis runs over, the one named last changes fastest.
Arguments:
- layer_input: bfloat16 [16384, 768], P(('dp', 'tensor')), may hold values from -6 to 6
- w_qkv: bfloat16 [2, 768, 2304], P(None, 'dp', 'tensor'), may hold values from -0.3125 to 0.3125
- w_out: bfloat16 [2, 768, 768], P(None, 'tensor', 'dp'), may hold values from -0.875 to 0.875
- w_up: bfloat16 [2, 768, 3072], P(None, 'dp', 'tensor'), may hold values from -0.21875 to 0.21875
- w_down: bfloat16 [2, 3072, 768], P(None, 'tensor', 'dp'), may hold values from -0.15625 to 0.15625
- attn_gain: float32 [2, 768], replicated, may hold values from 0.25 to 1.75
- attn_shift: float32 [2, 768], replicated, may hold values from -1.5 to 1.5
- ffn_gain: float32 [2, 768], replicated, may hold values from 0.25 to 1.75
- ffn_shift: float32 [2, 768], replicated, may hold values from -1.5 to 1.5
- out_grad: bfloat16 [16384, 768], P(('dp', 'tensor')), may hold values from -6 to 6
- doc_lengths: int32 [8, 4], P('dp'), may hold values from 1 to 16, 32 in all within a row
- block_deal: int32 [8, 32], P('dp'), may hold values from 0 to 31, each once within a row
- random_blocks: int32 [8, 12, 32, 3], P('dp', 'tensor'), may hold values from 0 to 4095
Outputs:
- layer_output: bfloat16 [16384, 768], P(('dp', 'tensor'))
- input_grad: float32 [16384, 768], P(('dp', 'tensor'))
- w_qkv_grad: float32 [2, 768, 2304], P(None, 'dp', 'tensor')
- w_out_grad: float32 [2, 768, 768], P(None, 'tensor', 'dp')
- w_up_grad: float32 [2, 768, 3072], P(None, 'dp', 'tensor')
- w_down_grad: float32 [2, 3072, 768], P(None, 'tensor', 'dp')
- attn_gain_grad: float32 [2, 768], replicated
- attn_shift_grad: float32 [2, 768], replicated
- ffn_gain_grad: float32 [2, 768], replicated
- ffn_shift_grad: float32 [2, 768], replicated
The draws below stay inside these ranges and needn't reach their ends.
Inputs may be any that keep to these rules, and one draw needn't show every extreme that they name: `doc_lengths`: each row sums to 32, and its largest entry is 16. `block_deal`: each row is a permutation of 0 to 31.
All inputs are finite; a program needn't handle non-finite values.
Results may differ from the reference program's by a relative error of at most 0.035.
The reference program's roundings to bfloat16 on the way count: a program that leaves them out, or rounds other values in their place, can miss the bound.
Values may be sent and summed in bfloat16 or wider, within the bound.
A program may use at most 192 MiB of HBM per device.

```python
import math
from functools import partial
import jax
import jax.numpy as jnp
import numpy as np
from jax import lax

D = 768
H = 12
HD = 64
FF = 3072
BLK = 64
RAND = 3
LAYERS = 2
QROWS = 512
GROUPS = 8
TOKENS = 16384
GROUP_BLOCKS = 32
DOCS = 4
LONGEST = 16


def place_ends(values, rng, low, top_value):
    longest = values.shape.index(max(values.shape))
    spots = []
    for shift in (0, 1):
        where = [jax.random.randint(jax.random.fold_in(rng, axis), (), 0, length) for axis, length in enumerate(values.shape)]
        where[longest] = (where[longest] + shift) % values.shape[longest]
        spots.append(tuple(where))
    return values.at[spots[0]].set(low).at[spots[1]].set(top_value)


def shard_levels(stream_key, extent, split, smallest, largest):
    def one(position, parts):
        draws = jax.random.uniform(jax.random.fold_in(jax.random.fold_in(stream_key, 6), position), (parts,), jnp.float32, smallest / len(split), largest / len(split))
        return jnp.repeat(jnp.exp(draws), extent[position] // parts).reshape((-1,) + (1,) * (len(extent) - position - 1))

    gain = one(*split[0])
    for cut in split[1:]:
        gain = gain * one(*cut)
    return gain


def length_profile(number_of, total, bound, slope):
    portions = [(1 << 20) // math.isqrt(standing ** slope) + 1 for standing in range(2, number_of + 1)]
    rest, counts = total - bound - (number_of - 1), [1] * (number_of - 1)
    while rest > 0:
        candidates = [i for i in range(number_of - 1) if counts[i] < bound]
        whole, budget = sum([portions[i] for i in candidates]), rest
        for i in candidates:
            extra = min(bound - counts[i], max(1, budget * portions[i] // whole), rest)
            counts[i] = counts[i] + extra
            rest = rest - extra
    return np.array([bound] + counts)


def uneven_parts(own_key, count, total, bound, skew):
    if count == 2:
        one = jax.random.randint(own_key, (), max(1, total - bound), min(bound, total - 1) + 1)
        return jnp.stack([one, total - one])
    lengths = jnp.asarray(length_profile(count, total, bound, skew), jnp.int32)
    twos = (count - 1) // 2
    donor, taker = lengths[1:1 + 2 * twos:2], lengths[2:2 + 2 * twos:2]
    room = jnp.minimum(donor - 1, bound - taker)
    passed = jax.random.randint(jax.random.fold_in(own_key, 1), (twos,), 0, 1 << 20) % (room + 1)
    lengths = lengths.at[1:1 + 2 * twos:2].set(donor - passed).at[2:2 + 2 * twos:2].set(taker + passed)
    return lengths[jax.random.permutation(jax.random.fold_in(own_key, 2), count)]


def noise(rng, shape, width, bound, cuts=(), kind=jnp.bfloat16):
    values = width * jax.random.normal(rng, shape, jnp.float32)
    if cuts:
        values = values * shard_levels(rng, shape, cuts, -0.22, 0.18)
    return jnp.clip(values, -bound, bound).astype(kind)


def setup_inputs(seed: int = 0) -> dict:
    key_of = jax.random.split(jax.random.key(seed), 14)
    return {
        "layer_input": noise(key_of[0], (TOKENS, D), 1.0, 6.0, ((0, 32),)),
        "w_qkv": noise(key_of[1], (LAYERS, D, 3 * D), (D // 2) ** -0.5, 0.3125, ((1, 8), (2, 4))),
        "w_out": noise(key_of[2], (LAYERS, D, D), (D // 16) ** -0.5, 0.875, ((1, 4), (2, 8))),
        "w_up": noise(key_of[3], (LAYERS, D, FF), D ** -0.5, 0.21875, ((1, 8), (2, 4))),
        "w_down": noise(key_of[4], (LAYERS, FF, D), (FF // 2) ** -0.5, 0.15625, ((1, 4), (2, 8))),
        "attn_gain": jnp.clip(1.0 + 0.15 * jax.random.normal(key_of[5], (LAYERS, D), jnp.float32), 0.25, 1.75),
        "attn_shift": noise(key_of[6], (LAYERS, D), 0.3, 1.5, (), jnp.float32),
        "ffn_gain": jnp.clip(1.0 + 0.15 * jax.random.normal(key_of[7], (LAYERS, D), jnp.float32), 0.25, 1.75),
        "ffn_shift": noise(key_of[8], (LAYERS, D), 0.3, 1.5, (), jnp.float32),
        "out_grad": noise(key_of[9], (TOKENS, D), 1.0, 6.0, ((0, 32),)),
        "doc_lengths": jax.vmap(lambda own: uneven_parts(own, DOCS, GROUP_BLOCKS, LONGEST, 2))(jax.random.split(key_of[10], GROUPS)).reshape((GROUPS, DOCS)).astype(jnp.int32),
        "block_deal": jax.vmap(lambda own: jax.random.permutation(own, GROUP_BLOCKS))(jax.random.split(key_of[11], GROUPS)).reshape((GROUPS, GROUP_BLOCKS)).astype(jnp.int32),
        "random_blocks": place_ends(jax.random.randint(key_of[12], (GROUPS, H, GROUP_BLOCKS, RAND), 0, 4096), jax.random.fold_in(key_of[12], 1), 0, 4095).astype(jnp.int32),
    }


@jax.custom_vjp
def low(v):
    return lax.optimization_barrier(v.astype(jnp.bfloat16)).astype(jnp.float32)

@jax.custom_vjp
def low_back(v):
    return v

def low_keep(v):
    return (low(v), None)

def low_pass(kept, grad):
    return (grad,)

def back_keep(v):
    return (v, None)

def back_low(kept, grad):
    return (low(grad),)
low.defvjp(low_keep, low_pass)
low_back.defvjp(back_keep, back_low)
NORM_EPSILON = 1e-12
MASK_VALUE = -1e+30
EXACT = lax.Precision.HIGHEST

def layer_norm(summed, norm_gain, norm_shift):
    row_mean = lax.optimization_barrier(jnp.mean(summed, axis=-1, keepdims=True))
    centred = summed - row_mean
    row_var = lax.optimization_barrier(jnp.mean(centred * centred, axis=-1, keepdims=True))
    return centred * lax.rsqrt(row_var + NORM_EPSILON) * norm_gain + norm_shift

def exact_dot(left, right):
    return jnp.dot(left, right, preferred_element_type=jnp.float32, precision=EXACT)

def block_mask(doc_lengths, block_deal, random_rows):
    doc_ends = jnp.cumsum(doc_lengths).astype(jnp.int32)
    doc_starts = doc_ends - doc_lengths
    doc_index = lax.optimization_barrier(jnp.sum((block_deal[:, None] >= doc_ends[None, :]).astype(jnp.int32), axis=1))
    doc_pick = (doc_index[:, None] == jnp.arange(doc_lengths.shape[0], dtype=jnp.int32)[None, :]).astype(jnp.int32)
    first_block = lax.optimization_barrier(jnp.sum(doc_pick * doc_starts[None, :], axis=1))
    doc_blocks = lax.optimization_barrier(jnp.sum(doc_pick * doc_lengths[None, :], axis=1))
    local_block = block_deal - first_block
    slot_pick = (block_deal[:, None] == jnp.arange(block_deal.shape[0], dtype=jnp.int32)[None, :]).astype(jnp.int32)
    random_picks = lax.optimization_barrier(jnp.sum(slot_pick[None, :, :, None] * random_rows[:, None, :, :], axis=2))
    random_local = jnp.remainder(random_picks, doc_blocks[None, :, None])
    random_hit = jnp.any(random_local[:, :, :, None] == local_block[None, None, None, :], axis=2)
    same_doc = doc_index[:, None] == doc_index[None, :]
    near_pair = jnp.abs(local_block[:, None] - local_block[None, :]) <= 1
    global_pair = (local_block[:, None] < 2) | (local_block[None, :] < 2)
    return same_doc[None] & ((near_pair | global_pair)[None] | random_hit)

def group_layer(stream, allowed, weights, norms):
    w_proj, w_back, w_expand, w_shrink = weights
    group_rows = stream.shape[0]
    inputs = low(stream)
    projected = low(low_back(exact_dot(inputs, w_proj))).reshape(group_rows, H, 3, HD)
    query_rows = projected[:, :, 0]
    key_rows = projected[:, :, 1]
    value_rows = projected[:, :, 2]
    block_count = group_rows // QROWS
    query_blocks = query_rows.reshape(block_count, QROWS, H, HD)
    mask_blocks = allowed.reshape(H, block_count, QROWS // BLK, group_rows // BLK).transpose(1, 0, 2, 3)
    score_scale = HD ** (-0.5)

    @jax.checkpoint
    def attend(pieces):
        query_block, mask_block = pieces
        raw_scores = jnp.einsum('qhe,khe->hqk', query_block, key_rows, precision=EXACT) * score_scale
        shaped = raw_scores.reshape(H, QROWS // BLK, BLK, group_rows // BLK, BLK)
        shaped = jnp.where(mask_block[:, :, None, :, None], shaped, MASK_VALUE)
        scores = low_back(shaped.reshape(H, QROWS, group_rows))
        prob_rows = low(jax.nn.softmax(scores, axis=2))
        return jnp.einsum('hqk,khe->qhe', prob_rows, value_rows, precision=EXACT)
    mixed_rows = lax.map(attend, (query_blocks, mask_blocks)).reshape(group_rows, H * HD)
    mixed_rows = low(low_back(mixed_rows))
    attended = low_back(exact_dot(mixed_rows, w_back))
    normed = layer_norm(stream + attended, norms[0], norms[1])
    ffn_in = low(normed)
    pre_act = low_back(exact_dot(ffn_in, w_expand))
    activated = low(jax.nn.gelu(pre_act, approximate=True))
    expanded = low_back(exact_dot(activated, w_shrink))
    return layer_norm(normed + expanded, norms[2], norms[3])

def run_group(pieces, weights, norms):
    return group_layer(pieces[0], pieces[1], weights, norms)

def forward(stream, w_proj, w_back, w_expand, w_shrink, gain_one, shift_one, gain_two, shift_two, allowed):
    for layer_index in range(LAYERS):
        weights = (w_proj[layer_index], w_back[layer_index], w_expand[layer_index], w_shrink[layer_index])
        norms = (gain_one[layer_index], shift_one[layer_index], gain_two[layer_index], shift_two[layer_index])
        stream = lax.map(partial(run_group, weights=weights, norms=norms), (stream, allowed))
    return stream

def reference(layer_input, w_qkv, w_out, w_up, w_down, attn_gain, attn_shift, ffn_gain, ffn_shift, out_grad, doc_lengths, block_deal, random_blocks):
    allowed = jax.vmap(block_mask)(doc_lengths, block_deal, random_blocks)
    group_count = doc_lengths.shape[0]
    start = layer_input.astype(jnp.float32).reshape(group_count, -1, D)

    def run_layers(stream, w_proj, w_back, w_expand, w_shrink, gain_one, shift_one, gain_two, shift_two):
        return forward(stream, w_proj, w_back, w_expand, w_shrink, gain_one, shift_one, gain_two, shift_two, allowed)
    result, pullback = jax.vjp(run_layers, start, w_qkv.astype(jnp.float32), w_out.astype(jnp.float32), w_up.astype(jnp.float32), w_down.astype(jnp.float32), attn_gain, attn_shift, ffn_gain, ffn_shift)
    grads = pullback(out_grad.astype(jnp.float32).reshape(result.shape))
    return (result.reshape(-1, D).astype(jnp.bfloat16), grads[0].reshape(-1, D), grads[1], grads[2], grads[3], grads[4], grads[5], grads[6], grads[7], grads[8])
```

```python
import jax
import jax.numpy as jnp
from jax import lax
from jax.experimental import pallas as pl
from jax.experimental.pallas import tpu as pltpu
from jax.sharding import PartitionSpec as P

HD = 64
BLK = 64
LAYERS = 2
LONGEST = 16
QUAD = 4
WIDE = QUAD * HD
STEP = 4
STEPS = LONGEST // STEP

NORM_EPSILON = 1e-12
MASK_VALUE = -1e30
BF = jnp.bfloat16
F32 = jnp.float32


def layer_norm(summed, norm_gain, norm_shift):
    row_mean = jnp.mean(summed, axis=-1, keepdims=True)
    centred = summed - row_mean
    row_var = jnp.mean(centred * centred, axis=-1, keepdims=True)
    return centred * lax.rsqrt(row_var + NORM_EPSILON) * norm_gain + norm_shift


def gelu_tanh(values):
    return jax.nn.gelu(values, approximate=True)


def dot(left, right):
    return jnp.dot(left, right, preferred_element_type=F32)


def dot_right_t(left, right):
    return lax.dot_general(left, right, (((1,), (1,)), ((), ())), preferred_element_type=F32)


def dot_left_t(left, right):
    return lax.dot_general(left, right, (((0,), (0,)), ((), ())), preferred_element_type=F32)


def head_diagonal(rows):
    lane_head = lax.broadcasted_iota(jnp.int32, rows.shape, 1) // HD
    return jnp.concatenate(
        [jnp.where(lane_head == h, rows, jnp.zeros_like(rows)) for h in range(QUAD)], axis=0
    )


def diagonal_rows(full):
    lane_head = lax.broadcasted_iota(jnp.int32, (HD, WIDE), 1) // HD
    out = full[:HD]
    for h in range(1, QUAD):
        out = jnp.where(lane_head == h, full[h * HD : (h + 1) * HD], out)
    return out


def forward_kernel(keys_at, steps_of, q_ref, k_ref, v_ref, bias_ref, out_ref, log_ref, score, peak, total, mix):
    def one_block(b, carry):
        rows = pl.ds(pl.multiple_of(b * BLK, BLK), BLK)
        query = head_diagonal(q_ref[rows, :])
        steps = steps_of[b]
        peak[...] = jnp.full(peak.shape, -jnp.inf, F32)
        total[...] = jnp.zeros_like(total)
        mix[...] = jnp.zeros_like(mix)

        def block_rows(ref, t):
            return jnp.concatenate(
                [
                    ref[pl.ds(pl.multiple_of(keys_at[b, t * STEP + j] * BLK, BLK), BLK), :]
                    for j in range(STEP)
                ],
                axis=0,
            )

        def scores(t, carry):
            raw = dot_right_t(query, block_rows(k_ref, t))
            bias = bias_ref[b, t]
            for h in range(QUAD):
                piece = raw[h * BLK : (h + 1) * BLK] + bias[h : h + 1, :]
                score[t, h * BLK : (h + 1) * BLK, :] = piece
                at = slice(h * BLK, (h + 1) * BLK)
                peak[at, :] = jnp.maximum(peak[at, :], jnp.maximum(piece[:, :128], piece[:, 128:]))
            return carry

        lax.fori_loop(0, steps, scores, 0)
        row_peak = jnp.max(peak[...], axis=1, keepdims=True)

        def mixes(t, carry):
            exponent = jnp.exp(score[t] - row_peak)
            total[...] += exponent[:, :128] + exponent[:, 128:]
            mix[...] += dot(exponent.astype(BF), block_rows(v_ref, t))
            return carry

        lax.fori_loop(0, steps, mixes, 0)
        row_total = jnp.sum(total[...], axis=1, keepdims=True)
        out_ref[rows, :] = diagonal_rows(mix[...] / row_total).astype(BF)
        logs = row_peak + jnp.log(row_total)
        log_ref[b] = jnp.transpose(jnp.broadcast_to(logs, (WIDE, 128)))[0:1, :]
        return carry

    lax.fori_loop(0, q_ref.shape[0] // BLK, one_block, 0)


def backward_kernel(
    keys_at, steps_of, q_ref, k_ref, v_ref, bias_ref, log_ref, d_ref, dq_ref, dk_ref, dv_ref, prob, dprob, inner, dquery, dkey, dvalue
):
    dkey[...] = jnp.zeros_like(dkey)
    dvalue[...] = jnp.zeros_like(dvalue)

    def one_block(b, carry):
        rows = pl.ds(pl.multiple_of(b * BLK, BLK), BLK)
        query = head_diagonal(q_ref[rows, :])
        d_mixed = head_diagonal(d_ref[rows, :])
        logs = log_ref[b]
        steps = steps_of[b]
        inner[...] = jnp.zeros_like(inner)
        dquery[...] = jnp.zeros_like(dquery)

        def places(t):
            return [
                pl.ds(pl.multiple_of(keys_at[b, t * STEP + j] * BLK, BLK), BLK) for j in range(STEP)
            ]

        def probs(t, carry):
            at = places(t)
            keys = jnp.concatenate([k_ref[p, :] for p in at], axis=0)
            values = jnp.concatenate([v_ref[p, :] for p in at], axis=0)
            raw = dot_right_t(keys, query)
            back = dot_right_t(values, d_mixed)
            bias = bias_ref[b, t]
            pieces = []
            for j in range(STEP):
                own = slice(j * BLK, (j + 1) * BLK)
                full = jnp.exp(raw[own] + (bias[j : j + 1, :] - logs))
                prob[t, own, :] = full
                product = full * back[own]
                inner[...] += jnp.sum(product.reshape(BLK // 8, 8, WIDE), axis=0)
                pieces.append(full.astype(BF))
            dprob[t] = back
            grad = dot(jnp.concatenate(pieces, axis=0), d_mixed)
            for j in range(STEP):
                dvalue[at[j], :] += grad[j * BLK : (j + 1) * BLK]
            return carry

        lax.fori_loop(0, steps, probs, 0)
        row_inner = jnp.sum(inner[...], axis=0, keepdims=True)

        def grads(t, carry):
            at = places(t)
            d_score = (prob[t] * (dprob[t] - row_inner)).astype(BF)
            grad = dot(d_score, query)
            for j in range(STEP):
                dkey[at[j], :] += grad[j * BLK : (j + 1) * BLK]
            keys = jnp.concatenate([k_ref[p, :] for p in at], axis=0)
            dquery[...] += dot_left_t(d_score, keys)
            return carry

        lax.fori_loop(0, steps, grads, 0)
        dq_ref[rows, :] = (diagonal_rows(dquery[...]) * (HD**-0.5)).astype(BF)
        return carry

    lax.fori_loop(0, q_ref.shape[0] // BLK, one_block, 0)
    dk_ref[...] = dkey[...].astype(BF)
    dv_ref[...] = dvalue[...].astype(BF)


def attend_forward(query, keyval, tables):
    keys_at, steps_of, bias_rows, bias_cols = tables
    own, width = query.shape
    quads = width // WIDE
    rows = keyval.shape[0]
    blocks = own // BLK
    return pl.pallas_call(
        forward_kernel,
        grid_spec=pltpu.PrefetchScalarGridSpec(
            num_scalar_prefetch=2,
            grid=(quads,),
            in_specs=[
                pl.BlockSpec((own, WIDE), lambda i, *_: (0, i)),
                pl.BlockSpec((rows, WIDE), lambda i, *_: (0, i)),
                pl.BlockSpec((rows, WIDE), lambda i, *_: (0, i + quads)),
                pl.BlockSpec((blocks, STEPS, None, QUAD, WIDE), lambda i, *_: (0, 0, i, 0, 0)),
            ],
            out_specs=[
                pl.BlockSpec((own, WIDE), lambda i, *_: (0, i)),
                pl.BlockSpec((blocks, 1, WIDE), lambda i, *_: (0, 0, i)),
            ],
            scratch_shapes=[
                pltpu.VMEM((STEPS, WIDE, WIDE), F32),
                pltpu.VMEM((WIDE, 128), F32),
                pltpu.VMEM((WIDE, 128), F32),
                pltpu.VMEM((WIDE, WIDE), F32),
            ],
        ),
        out_shape=[
            jax.ShapeDtypeStruct((own, width), BF),
            jax.ShapeDtypeStruct((blocks, 1, width), F32),
        ],
        cost_estimate=pl.CostEstimate(
            flops=2 * 2 * own * rows * width // 2 * 4,
            bytes_accessed=2 * (own * 2 + rows * 2) * width,
            transcendentals=own * rows * width // HD // 2,
        ),
        name="attend_forward",
    )(keys_at, steps_of, query, keyval, keyval, bias_rows)


def attend_backward(query, keyval, logs, d_mixed, tables):
    keys_at, steps_of, bias_rows, bias_cols = tables
    own, width = query.shape
    quads = width // WIDE
    rows = keyval.shape[0]
    blocks = own // BLK
    return pl.pallas_call(
        backward_kernel,
        grid_spec=pltpu.PrefetchScalarGridSpec(
            num_scalar_prefetch=2,
            grid=(quads,),
            in_specs=[
                pl.BlockSpec((own, WIDE), lambda i, *_: (0, i)),
                pl.BlockSpec((rows, WIDE), lambda i, *_: (0, i)),
                pl.BlockSpec((rows, WIDE), lambda i, *_: (0, i + quads)),
                pl.BlockSpec((blocks, STEPS, STEP, WIDE), lambda i, *_: (0, 0, 0, i)),
                pl.BlockSpec((blocks, 1, WIDE), lambda i, *_: (0, 0, i)),
                pl.BlockSpec((own, WIDE), lambda i, *_: (0, i)),
            ],
            out_specs=[
                pl.BlockSpec((own, WIDE), lambda i, *_: (0, i)),
                pl.BlockSpec((rows, WIDE), lambda i, *_: (0, i)),
                pl.BlockSpec((rows, WIDE), lambda i, *_: (0, i)),
            ],
            scratch_shapes=[
                pltpu.VMEM((STEPS, WIDE, WIDE), F32),
                pltpu.VMEM((STEPS, WIDE, WIDE), F32),
                pltpu.VMEM((8, WIDE), F32),
                pltpu.VMEM((WIDE, WIDE), F32),
                pltpu.VMEM((rows, WIDE), F32),
                pltpu.VMEM((rows, WIDE), F32),
            ],
        ),
        out_shape=[
            jax.ShapeDtypeStruct((own, width), BF),
            jax.ShapeDtypeStruct((rows, width), BF),
            jax.ShapeDtypeStruct((rows, width), BF),
        ],
        cost_estimate=pl.CostEstimate(
            flops=5 * 2 * own * rows * width // 2 * 4,
            bytes_accessed=2 * (own * 3 + rows * 4) * width,
            transcendentals=own * rows * width // HD // 2,
        ),
        name="attend_backward",
    )(keys_at, steps_of, query, keyval, keyval, bias_cols, logs, d_mixed)


def attention_tables(doc_lengths, block_deal, random_rows, own_blocks, first_own):
    blocks = block_deal.shape[0]
    doc_ends = jnp.cumsum(doc_lengths)
    doc_starts = doc_ends - doc_lengths
    place = jnp.arange(blocks, dtype=jnp.int32)
    stored_at = jnp.sum(
        jnp.where(block_deal[None, :] == place[:, None], place[None, :], 0), axis=1
    )
    own = lax.dynamic_slice(block_deal, (first_own,), (own_blocks,))
    doc_index = jnp.sum((own[:, None] >= doc_ends[None, :]).astype(jnp.int32), axis=1)
    doc_pick = (
        doc_index[:, None] == jnp.arange(doc_lengths.shape[0], dtype=jnp.int32)[None, :]
    ).astype(jnp.int32)
    first_block = jnp.sum(doc_pick * doc_starts[None, :], axis=1)
    doc_blocks = jnp.sum(doc_pick * doc_lengths[None, :], axis=1)
    local = own - first_block
    other = jnp.arange(LONGEST, dtype=jnp.int32)
    wanted = jnp.minimum(first_block[:, None] + other[None, :], blocks - 1)
    keys_at = jnp.sum(
        jnp.where(wanted[:, :, None] == place[None, None, :], stored_at[None, None, :], 0), axis=2
    )
    own_pick = (own[:, None] == place[None, :]).astype(jnp.int32)
    picks = jnp.sum(own_pick[None, :, :, None] * random_rows[:, None, :, :], axis=2)
    picks = jnp.remainder(picks, doc_blocks[None, :, None])
    random_hit = jnp.any(picks[:, :, :, None] == other[None, None, None, :], axis=2)
    inside = other[None, :] < doc_blocks[:, None]
    near = jnp.abs(local[:, None] - other[None, :]) <= 1
    everywhere = (local[:, None] < 2) | (other[None, :] < 2)
    allowed = inside[None] & ((near | everywhere)[None] | random_hit)
    bias = jnp.where(allowed, 0.0, MASK_VALUE).astype(F32)
    heads = bias.shape[0]
    bias_rows = bias.reshape(heads // QUAD, QUAD, own_blocks, STEPS, STEP).transpose(2, 3, 0, 1, 4)
    bias_rows = jnp.repeat(bias_rows, BLK, axis=4)
    bias_cols = bias.transpose(1, 2, 0).reshape(own_blocks, STEPS, STEP, heads)
    bias_cols = jnp.repeat(bias_cols, BLK, axis=3)
    steps_of = (doc_blocks + STEP - 1) // STEP
    return keys_at, steps_of, bias_rows, bias_cols


def gather_tensor(shard):
    return lax.all_gather(shard, "tensor", axis=0, tiled=True)


def local(
    layer_input,
    w_qkv,
    w_out,
    w_up,
    w_down,
    attn_gain,
    attn_shift,
    ffn_gain,
    ffn_shift,
    out_grad,
    doc_lengths,
    block_deal,
    random_blocks,
):
    own_rows, width = layer_input.shape
    tensor = lax.axis_size("tensor")
    slot = lax.axis_index("tensor")
    head_local = random_blocks.shape[1]
    chunk = head_local * HD
    depth = w_qkv.shape[1]
    hidden = w_up.shape[2]
    score_scale = HD ** (-0.5)

    attn_shards = jnp.concatenate(
        [
            w_qkv.reshape(LAYERS, depth, head_local, 3, HD)
            .transpose(0, 1, 3, 2, 4)
            .reshape(LAYERS, depth, 3 * chunk),
            w_out.transpose(0, 2, 1),
        ],
        axis=2,
    )
    ffn_shards = jnp.concatenate([w_up, w_down.transpose(0, 2, 1)], axis=2)

    def spread(shards, pieces):
        gathered = lax.all_gather(shards, "tensor", axis=0)
        gathered = gathered.reshape(tensor, LAYERS, depth, pieces, -1)
        return gathered.transpose(1, 2, 3, 0, 4).reshape(LAYERS, depth, -1)

    attn_rows = spread(attn_shards, 4)
    ffn_rows = spread(ffn_shards, 2)
    attn_full = [lax.all_gather(attn_rows[l], "dp", axis=0, tiled=True) for l in range(LAYERS)]
    ffn_full = [lax.all_gather(ffn_rows[l], "dp", axis=0, tiled=True) for l in range(LAYERS)]

    random_all = lax.all_gather(random_blocks[0], "tensor", axis=0, tiled=True)
    own_blocks = own_rows // BLK
    tables = attention_tables(
        doc_lengths[0], block_deal[0], random_all, own_blocks, slot * own_blocks
    )

    stream = layer_input.astype(F32)
    stored = []
    for layer in range(LAYERS):
        attn_w, ffn_w = attn_full[layer], ffn_full[layer]
        w_query = attn_w[:, :width]
        w_keyval = attn_w[:, width : 3 * width]
        w_back_t = attn_w[:, 3 * width :]
        w_expand = ffn_w[:, : hidden * tensor]
        w_shrink_t = ffn_w[:, hidden * tensor :]
        own_inputs = stream.astype(BF)
        inputs = gather_tensor(own_inputs)
        query = (dot(own_inputs, w_query).astype(BF).astype(F32) * score_scale).astype(BF)
        keyval = dot(inputs, w_keyval).astype(BF)
        mixed, logs = attend_forward(query, keyval, tables)
        summed_one = stream + dot_right_t(mixed, w_back_t)
        normed = layer_norm(summed_one, attn_gain[layer], attn_shift[layer])
        ffn_in = normed.astype(BF)
        pre_act = dot(ffn_in, w_expand)
        activated = gelu_tanh(pre_act).astype(BF)
        summed_two = normed + dot_right_t(activated, w_shrink_t)
        stored.append(
            (own_inputs, inputs, query, keyval, mixed, logs, summed_one, ffn_in, pre_act, activated, summed_two)
        )
        stream = layer_norm(summed_two, ffn_gain[layer], ffn_shift[layer])

    state_grad = out_grad.astype(F32)
    attn_grads = [None] * LAYERS
    ffn_grads = [None] * LAYERS
    norm_parts = [None] * LAYERS
    for layer in reversed(range(LAYERS)):
        (own_inputs, inputs, query, keyval, mixed, logs, summed_one, ffn_in, pre_act, activated, summed_two) = stored[layer]
        attn_w, ffn_w = attn_full[layer], ffn_full[layer]
        w_query = attn_w[:, :width]
        w_keyval = attn_w[:, width : 3 * width]
        w_back_t = attn_w[:, 3 * width :]
        w_expand = ffn_w[:, : hidden * tensor]
        w_shrink_t = ffn_w[:, hidden * tensor :]
        unused_two, ffn_back = jax.vjp(layer_norm, summed_two, ffn_gain[layer], ffn_shift[layer])
        d_two, ffn_gain_part, ffn_shift_part = ffn_back(state_grad)
        d_two_low = d_two.astype(BF)
        shrink_grad_t = dot_left_t(d_two_low, activated)
        unused_act, gelu_back = jax.vjp(gelu_tanh, pre_act)
        d_pre = gelu_back(dot(d_two_low, w_shrink_t))[0].astype(BF)
        expand_grad = dot_left_t(ffn_in, d_pre)
        ffn_part = jnp.concatenate([expand_grad.astype(BF), shrink_grad_t.astype(BF)], axis=1)
        ffn_grads[layer] = lax.psum_scatter(ffn_part, "dp", scatter_dimension=0, tiled=True)
        d_normed = d_two + dot_right_t(d_pre, w_expand)
        unused_one, attn_back = jax.vjp(layer_norm, summed_one, attn_gain[layer], attn_shift[layer])
        d_one, attn_gain_part, attn_shift_part = attn_back(d_normed)
        d_one_low = d_one.astype(BF)
        back_grad_t = dot_left_t(d_one_low, mixed)
        d_mixed = dot(d_one_low, w_back_t).astype(BF)
        d_query, d_key, d_value = attend_backward(query, keyval, logs, d_mixed, tables)
        others = dot_right_t(d_key, w_keyval[:, :width]) + dot_right_t(d_value, w_keyval[:, width:])
        summed = lax.psum_scatter(others.astype(BF), "tensor", scatter_dimension=0, tiled=True)
        attn_part = jnp.concatenate(
            [
                dot_left_t(own_inputs, d_query).astype(BF),
                dot_left_t(inputs, d_key).astype(BF),
                dot_left_t(inputs, d_value).astype(BF),
                back_grad_t.astype(BF),
            ],
            axis=1,
        )
        attn_grads[layer] = lax.psum_scatter(attn_part, "dp", scatter_dimension=0, tiled=True)
        state_grad = d_one + dot_right_t(d_query, w_query) + summed.astype(F32)
        norm_parts[layer] = (attn_gain_part, attn_shift_part, ffn_gain_part, ffn_shift_part)

    def collect(parts, pieces):
        grads = jnp.stack(parts).reshape(LAYERS, depth, pieces, tensor, -1).transpose(3, 0, 1, 2, 4)
        own = lax.psum_scatter(grads, "tensor", scatter_dimension=0, tiled=False)
        return own.astype(F32)

    attn_own = collect(attn_grads, 4)
    ffn_own = collect(ffn_grads, 2)
    qkv_grad = attn_own[:, :, :3].reshape(LAYERS, depth, 3, head_local, HD)
    qkv_grad = qkv_grad.transpose(0, 1, 3, 2, 4).reshape(LAYERS, depth, 3 * chunk)
    out_w_grad = attn_own[:, :, 3].transpose(0, 2, 1)
    up_grad = ffn_own[:, :, 0]
    down_grad = ffn_own[:, :, 1].transpose(0, 2, 1)
    norm_sums = lax.psum(
        tuple(jnp.stack([norm_parts[l][k] for l in range(LAYERS)]) for k in range(4)),
        ("dp", "tensor"),
    )
    return (stream.astype(BF), state_grad, qkv_grad, out_w_grad, up_grad, down_grad) + tuple(norm_sums)


def solution(mesh):
    placed = (
        P(("dp", "tensor"), None),
        P(None, "dp", "tensor"),
        P(None, "tensor", "dp"),
        P(None, "dp", "tensor"),
        P(None, "tensor", "dp"),
        P(),
        P(),
        P(),
        P(),
        P(("dp", "tensor"), None),
        P("dp", None),
        P("dp", None),
        P("dp", "tensor", None, None),
    )
    return jax.shard_map(
        local,
        mesh=mesh,
        in_specs=placed,
        out_specs=(
            P(("dp", "tensor"), None),
            P(("dp", "tensor"), None),
            P(None, "dp", "tensor"),
            P(None, "tensor", "dp"),
            P(None, "dp", "tensor"),
            P(None, "tensor", "dp"),
            P(),
            P(),
            P(),
            P(),
        ),
        check_vma=False,
    )
```

```python
import jax
import jax.numpy as jnp
from jax import lax
from jax.experimental import pallas as pl
from jax.experimental.pallas import tpu as pltpu
from jax.sharding import PartitionSpec as P

HD = 64
BLK = 64
LAYERS = 2
LONGEST = 16
QUAD = 4
WIDE = QUAD * HD
STEP = 4
STEPS = LONGEST // STEP

ROW = 2
DATA = ("hi", "row", "quad")
EVERY = DATA + ("tensor",)

NORM_EPSILON = 1e-12
MASK_VALUE = -1e30
BF = jnp.bfloat16
F32 = jnp.float32


def layer_norm(summed, norm_gain, norm_shift):
    row_mean = jnp.mean(summed, axis=-1, keepdims=True)
    centred = summed - row_mean
    row_var = jnp.mean(centred * centred, axis=-1, keepdims=True)
    return centred * lax.rsqrt(row_var + NORM_EPSILON) * norm_gain + norm_shift


def gelu_tanh(values):
    return jax.nn.gelu(values, approximate=True)


def dot(left, right):
    return jnp.dot(left, right, preferred_element_type=F32)


def dot_right_t(left, right):
    return lax.dot_general(left, right, (((1,), (1,)), ((), ())), preferred_element_type=F32)


def dot_left_t(left, right):
    return lax.dot_general(left, right, (((0,), (0,)), ((), ())), preferred_element_type=F32)


def head_diagonal(rows):
    lane_head = lax.broadcasted_iota(jnp.int32, rows.shape, 1) // HD
    return jnp.concatenate(
        [jnp.where(lane_head == h, rows, jnp.zeros_like(rows)) for h in range(QUAD)], axis=0
    )


def diagonal_rows(full):
    lane_head = lax.broadcasted_iota(jnp.int32, (HD, WIDE), 1) // HD
    out = full[:HD]
    for h in range(1, QUAD):
        out = jnp.where(lane_head == h, full[h * HD : (h + 1) * HD], out)
    return out


def forward_kernel(keys_at, steps_of, q_ref, k_ref, v_ref, bias_ref, out_ref, log_ref, score, peak, total, mix):
    def one_block(b, carry):
        rows = pl.ds(pl.multiple_of(b * BLK, BLK), BLK)
        query = head_diagonal(q_ref[rows, :])
        steps = steps_of[b]
        peak[...] = jnp.full(peak.shape, -jnp.inf, F32)
        total[...] = jnp.zeros_like(total)
        mix[...] = jnp.zeros_like(mix)

        def block_rows(ref, t):
            return jnp.concatenate(
                [
                    ref[pl.ds(pl.multiple_of(keys_at[b, t * STEP + j] * BLK, BLK), BLK), :]
                    for j in range(STEP)
                ],
                axis=0,
            )

        def scores(t, carry):
            raw = dot_right_t(query, block_rows(k_ref, t))
            bias = bias_ref[b, t]
            for h in range(QUAD):
                piece = raw[h * BLK : (h + 1) * BLK] + bias[h : h + 1, :]
                score[t, h * BLK : (h + 1) * BLK, :] = piece
                at = slice(h * BLK, (h + 1) * BLK)
                peak[at, :] = jnp.maximum(peak[at, :], jnp.maximum(piece[:, :128], piece[:, 128:]))
            return carry

        lax.fori_loop(0, steps, scores, 0)
        row_peak = jnp.max(peak[...], axis=1, keepdims=True)

        def mixes(t, carry):
            exponent = jnp.exp(score[t] - row_peak)
            total[...] += exponent[:, :128] + exponent[:, 128:]
            mix[...] += dot(exponent.astype(BF), block_rows(v_ref, t))
            return carry

        lax.fori_loop(0, steps, mixes, 0)
        row_total = jnp.sum(total[...], axis=1, keepdims=True)
        out_ref[rows, :] = diagonal_rows(mix[...] / row_total).astype(BF)
        logs = row_peak + jnp.log(row_total)
        log_ref[b] = jnp.transpose(jnp.broadcast_to(logs, (WIDE, 128)))[0:1, :]
        return carry

    lax.fori_loop(0, q_ref.shape[0] // BLK, one_block, 0)


def backward_kernel(
    keys_at, steps_of, q_ref, k_ref, v_ref, bias_ref, log_ref, d_ref, dq_ref, dk_ref, dv_ref, prob, dprob, inner, dquery, dkey, dvalue
):
    dkey[...] = jnp.zeros_like(dkey)
    dvalue[...] = jnp.zeros_like(dvalue)

    def one_block(b, carry):
        rows = pl.ds(pl.multiple_of(b * BLK, BLK), BLK)
        query = head_diagonal(q_ref[rows, :])
        d_mixed = head_diagonal(d_ref[rows, :])
        logs = log_ref[b]
        steps = steps_of[b]
        inner[...] = jnp.zeros_like(inner)
        dquery[...] = jnp.zeros_like(dquery)

        def places(t):
            return [
                pl.ds(pl.multiple_of(keys_at[b, t * STEP + j] * BLK, BLK), BLK) for j in range(STEP)
            ]

        def probs(t, carry):
            at = places(t)
            keys = jnp.concatenate([k_ref[p, :] for p in at], axis=0)
            values = jnp.concatenate([v_ref[p, :] for p in at], axis=0)
            raw = dot_right_t(keys, query)
            back = dot_right_t(values, d_mixed)
            bias = bias_ref[b, t]
            pieces = []
            for j in range(STEP):
                own = slice(j * BLK, (j + 1) * BLK)
                full = jnp.exp(raw[own] + (bias[j : j + 1, :] - logs))
                prob[t, own, :] = full
                product = full * back[own]
                inner[...] += jnp.sum(product.reshape(BLK // 8, 8, WIDE), axis=0)
                pieces.append(full.astype(BF))
            dprob[t] = back
            grad = dot(jnp.concatenate(pieces, axis=0), d_mixed)
            for j in range(STEP):
                dvalue[at[j], :] += grad[j * BLK : (j + 1) * BLK]
            return carry

        lax.fori_loop(0, steps, probs, 0)
        row_inner = jnp.sum(inner[...], axis=0, keepdims=True)

        def grads(t, carry):
            at = places(t)
            d_score = (prob[t] * (dprob[t] - row_inner)).astype(BF)
            grad = dot(d_score, query)
            for j in range(STEP):
                dkey[at[j], :] += grad[j * BLK : (j + 1) * BLK]
            keys = jnp.concatenate([k_ref[p, :] for p in at], axis=0)
            dquery[...] += dot_left_t(d_score, keys)
            return carry

        lax.fori_loop(0, steps, grads, 0)
        dq_ref[rows, :] = (diagonal_rows(dquery[...]) * (HD**-0.5)).astype(BF)
        return carry

    lax.fori_loop(0, q_ref.shape[0] // BLK, one_block, 0)
    dk_ref[...] = dkey[...].astype(BF)
    dv_ref[...] = dvalue[...].astype(BF)


def attend_forward(query, keyval, tables):
    keys_at, steps_of, bias_rows, bias_cols = tables
    own, width = query.shape
    quads = width // WIDE
    rows = keyval.shape[0]
    blocks = own // BLK
    return pl.pallas_call(
        forward_kernel,
        grid_spec=pltpu.PrefetchScalarGridSpec(
            num_scalar_prefetch=2,
            grid=(quads,),
            in_specs=[
                pl.BlockSpec((own, WIDE), lambda i, *_: (0, i)),
                pl.BlockSpec((rows, WIDE), lambda i, *_: (0, i)),
                pl.BlockSpec((rows, WIDE), lambda i, *_: (0, i + quads)),
                pl.BlockSpec((blocks, STEPS, None, QUAD, WIDE), lambda i, *_: (0, 0, i, 0, 0)),
            ],
            out_specs=[
                pl.BlockSpec((own, WIDE), lambda i, *_: (0, i)),
                pl.BlockSpec((blocks, 1, WIDE), lambda i, *_: (0, 0, i)),
            ],
            scratch_shapes=[
                pltpu.VMEM((STEPS, WIDE, WIDE), F32),
                pltpu.VMEM((WIDE, 128), F32),
                pltpu.VMEM((WIDE, 128), F32),
                pltpu.VMEM((WIDE, WIDE), F32),
            ],
        ),
        out_shape=[
            jax.ShapeDtypeStruct((own, width), BF),
            jax.ShapeDtypeStruct((blocks, 1, width), F32),
        ],
        cost_estimate=pl.CostEstimate(
            flops=2 * 2 * own * rows * width // 2 * 4,
            bytes_accessed=2 * (own * 2 + rows * 2) * width,
            transcendentals=own * rows * width // HD // 2,
        ),
        name="attend_forward",
    )(keys_at, steps_of, query, keyval, keyval, bias_rows)


def attend_backward(query, keyval, logs, d_mixed, tables):
    keys_at, steps_of, bias_rows, bias_cols = tables
    own, width = query.shape
    quads = width // WIDE
    rows = keyval.shape[0]
    blocks = own // BLK
    return pl.pallas_call(
        backward_kernel,
        grid_spec=pltpu.PrefetchScalarGridSpec(
            num_scalar_prefetch=2,
            grid=(quads,),
            in_specs=[
                pl.BlockSpec((own, WIDE), lambda i, *_: (0, i)),
                pl.BlockSpec((rows, WIDE), lambda i, *_: (0, i)),
                pl.BlockSpec((rows, WIDE), lambda i, *_: (0, i + quads)),
                pl.BlockSpec((blocks, STEPS, STEP, WIDE), lambda i, *_: (0, 0, 0, i)),
                pl.BlockSpec((blocks, 1, WIDE), lambda i, *_: (0, 0, i)),
                pl.BlockSpec((own, WIDE), lambda i, *_: (0, i)),
            ],
            out_specs=[
                pl.BlockSpec((own, WIDE), lambda i, *_: (0, i)),
                pl.BlockSpec((rows, WIDE), lambda i, *_: (0, i)),
                pl.BlockSpec((rows, WIDE), lambda i, *_: (0, i)),
            ],
            scratch_shapes=[
                pltpu.VMEM((STEPS, WIDE, WIDE), F32),
                pltpu.VMEM((STEPS, WIDE, WIDE), F32),
                pltpu.VMEM((8, WIDE), F32),
                pltpu.VMEM((WIDE, WIDE), F32),
                pltpu.VMEM((rows, WIDE), F32),
                pltpu.VMEM((rows, WIDE), F32),
            ],
        ),
        out_shape=[
            jax.ShapeDtypeStruct((own, width), BF),
            jax.ShapeDtypeStruct((rows, width), BF),
            jax.ShapeDtypeStruct((rows, width), BF),
        ],
        cost_estimate=pl.CostEstimate(
            flops=5 * 2 * own * rows * width // 2 * 4,
            bytes_accessed=2 * (own * 3 + rows * 4) * width,
            transcendentals=own * rows * width // HD // 2,
        ),
        name="attend_backward",
    )(keys_at, steps_of, query, keyval, keyval, bias_cols, logs, d_mixed)


def attention_tables(doc_lengths, block_deal, random_rows, own_blocks, first_own):
    blocks = block_deal.shape[0]
    doc_ends = jnp.cumsum(doc_lengths)
    doc_starts = doc_ends - doc_lengths
    place = jnp.arange(blocks, dtype=jnp.int32)
    stored_at = jnp.sum(
        jnp.where(block_deal[None, :] == place[:, None], place[None, :], 0), axis=1
    )
    own = lax.dynamic_slice(block_deal, (first_own,), (own_blocks,))
    doc_index = jnp.sum((own[:, None] >= doc_ends[None, :]).astype(jnp.int32), axis=1)
    doc_pick = (
        doc_index[:, None] == jnp.arange(doc_lengths.shape[0], dtype=jnp.int32)[None, :]
    ).astype(jnp.int32)
    first_block = jnp.sum(doc_pick * doc_starts[None, :], axis=1)
    doc_blocks = jnp.sum(doc_pick * doc_lengths[None, :], axis=1)
    local = own - first_block
    other = jnp.arange(LONGEST, dtype=jnp.int32)
    wanted = jnp.minimum(first_block[:, None] + other[None, :], blocks - 1)
    keys_at = jnp.sum(
        jnp.where(wanted[:, :, None] == place[None, None, :], stored_at[None, None, :], 0), axis=2
    )
    own_pick = (own[:, None] == place[None, :]).astype(jnp.int32)
    picks = jnp.sum(own_pick[None, :, :, None] * random_rows[:, None, :, :], axis=2)
    picks = jnp.remainder(picks, doc_blocks[None, :, None])
    random_hit = jnp.any(picks[:, :, :, None] == other[None, None, None, :], axis=2)
    inside = other[None, :] < doc_blocks[:, None]
    near = jnp.abs(local[:, None] - other[None, :]) <= 1
    everywhere = (local[:, None] < 2) | (other[None, :] < 2)
    allowed = inside[None] & ((near | everywhere)[None] | random_hit)
    bias = jnp.where(allowed, 0.0, MASK_VALUE).astype(F32)
    heads = bias.shape[0]
    bias_rows = bias.reshape(heads // QUAD, QUAD, own_blocks, STEPS, STEP).transpose(2, 3, 0, 1, 4)
    bias_rows = jnp.repeat(bias_rows, BLK, axis=4)
    bias_cols = bias.transpose(1, 2, 0).reshape(own_blocks, STEPS, STEP, heads)
    bias_cols = jnp.repeat(bias_cols, BLK, axis=3)
    steps_of = (doc_blocks + STEP - 1) // STEP
    return keys_at, steps_of, bias_rows, bias_cols


def to_home(steps, parts):
    pairs = []
    for hi in range(steps):
        for row in range(ROW):
            for quad in range(QUAD):
                side, core = quad // 2, quad % 2
                plane = parts - 1 - side if core else side
                for part in range(parts):
                    source = ((hi * ROW + row) * QUAD + quad) * parts + part
                    target = ((hi * ROW + row) * QUAD + part) * parts + plane
                    pairs.append((source, target))
    return pairs


def local(
    layer_input,
    w_qkv,
    w_out,
    w_up,
    w_down,
    attn_gain,
    attn_shift,
    ffn_gain,
    ffn_shift,
    out_grad,
    doc_lengths,
    block_deal,
    random_blocks,
):
    own_rows, width = layer_input.shape
    tensor = lax.axis_size("tensor")
    slot = lax.axis_index("quad")
    plane = lax.axis_index("tensor")
    head_local = random_blocks.shape[1]
    chunk = head_local * HD
    depth = w_qkv.shape[1]
    hidden = w_up.shape[2]
    score_scale = HD ** (-0.5)
    moves = to_home(lax.axis_size("hi"), tensor)
    moves_back = [(b, a) for a, b in moves]

    def shifted(x, by):
        return lax.ppermute(x, "tensor", [(i, (i + by) % tensor) for i in range(tensor)])

    def spread(shard):
        return [shard] + [shifted(shard, by) for by in range(1, tensor)]

    def attn_rows(qkv, back):
        qkv = qkv.reshape(depth, head_local, 3, HD).transpose(0, 2, 1, 3)
        shard = jnp.concatenate([qkv.reshape(depth, 3 * chunk), back.T], axis=1)
        parts = spread(shard)
        return jnp.concatenate(
            [part[:, p * chunk : (p + 1) * chunk] for p in range(4) for part in parts], axis=1
        )

    def ffn_rows(up, down):
        parts = spread(jnp.concatenate([up, down.T], axis=1))
        return jnp.concatenate(
            [part[:, p * hidden : (p + 1) * hidden] for p in range(2) for part in parts], axis=1
        )

    def over_data(rows):
        return lax.all_gather(rows, DATA, axis=0, tiled=True)

    random_all = lax.all_gather(random_blocks[0], "tensor", axis=0, tiled=True)
    own_tokens = lax.ppermute(layer_input, EVERY, moves)
    docs, group_blocks = doc_lengths.shape[1], block_deal.shape[1]
    numbers = jnp.concatenate([doc_lengths[0], block_deal[0], random_all.reshape(-1)])
    numbers = lax.ppermute(numbers, EVERY, moves)
    attn_full = [over_data(attn_rows(w_qkv[0], w_out[0]))]
    own_tokens, up_0, down_0 = lax.optimization_barrier((own_tokens, w_up[0], w_down[0]))
    ffn_full = [over_data(ffn_rows(up_0, down_0))]

    random_home = numbers[docs + group_blocks :].reshape(tensor, head_local, group_blocks, -1)
    part_of = (plane - jnp.arange(tensor, dtype=jnp.int32)) % tensor
    part_pick = (part_of[:, None] == jnp.arange(tensor, dtype=jnp.int32)[None, :]).astype(jnp.int32)
    random_home = jnp.sum(part_pick[:, :, None, None, None] * random_home[None], axis=1)
    random_home = random_home.reshape(tensor * head_local, group_blocks, -1)
    own_blocks = own_rows // BLK
    tables = attention_tables(
        numbers[:docs],
        numbers[docs : docs + group_blocks],
        random_home,
        own_blocks,
        slot * own_blocks,
    )

    stream = own_tokens.astype(F32)
    stored = []
    for layer in range(LAYERS):
        attn_w, ffn_w = attn_full[layer], ffn_full[layer]
        w_query = attn_w[:, :width]
        w_keyval = attn_w[:, width : 3 * width]
        w_back_t = attn_w[:, 3 * width :]
        w_expand = ffn_w[:, : hidden * tensor]
        w_shrink_t = ffn_w[:, hidden * tensor :]
        own_inputs = stream.astype(BF)
        inputs = lax.all_gather(own_inputs, "quad", axis=0, tiled=True)
        query = (dot(own_inputs, w_query).astype(BF).astype(F32) * score_scale).astype(BF)
        keyval = dot(inputs, w_keyval).astype(BF)
        if layer == 0:
            query, later = lax.optimization_barrier((query, (out_grad, w_qkv, w_out, w_up, w_down)))
            for other in range(1, LAYERS):
                attn_full.append(over_data(attn_rows(later[1][other], later[2][other])))
                ffn_full.append(over_data(ffn_rows(later[3][other], later[4][other])))
            own_grad = lax.ppermute(later[0], EVERY, moves)
        mixed, logs = attend_forward(query, keyval, tables)
        summed_one = stream + dot_right_t(mixed, w_back_t)
        normed = layer_norm(summed_one, attn_gain[layer], attn_shift[layer])
        ffn_in = normed.astype(BF)
        pre_act = dot(ffn_in, w_expand)
        activated = gelu_tanh(pre_act).astype(BF)
        summed_two = normed + dot_right_t(activated, w_shrink_t)
        stored.append(
            (own_inputs, inputs, query, keyval, mixed, logs, summed_one, ffn_in, pre_act, activated, summed_two)
        )
        stream = layer_norm(summed_two, ffn_gain[layer], ffn_shift[layer])
    layer_output = lax.ppermute(stream.astype(BF), EVERY, moves_back)

    def sum_parts(rows, pieces):
        parts = rows.reshape(depth, pieces, tensor, -1)
        total = parts[:, :, 0].astype(F32)
        for by in range(1, tensor):
            total = total + shifted(parts[:, :, by].reshape(depth, -1), tensor - by).reshape(
                depth, pieces, -1
            ).astype(F32)
        return total

    def sum_data(part):
        return lax.psum_scatter(part, DATA, scatter_dimension=0, tiled=True)

    state_grad = own_grad.astype(F32)
    attn_grads = [None] * LAYERS
    ffn_grads = [None] * LAYERS
    norm_parts = [None] * LAYERS
    for layer in reversed(range(LAYERS)):
        (own_inputs, inputs, query, keyval, mixed, logs, summed_one, ffn_in, pre_act, activated, summed_two) = stored[layer]
        attn_w, ffn_w = attn_full[layer], ffn_full[layer]
        w_query = attn_w[:, :width]
        w_keyval = attn_w[:, width : 3 * width]
        w_back_t = attn_w[:, 3 * width :]
        w_expand = ffn_w[:, : hidden * tensor]
        w_shrink_t = ffn_w[:, hidden * tensor :]
        unused_two, ffn_back = jax.vjp(layer_norm, summed_two, ffn_gain[layer], ffn_shift[layer])
        d_two, ffn_gain_part, ffn_shift_part = ffn_back(state_grad)
        d_two_low = d_two.astype(BF)
        shrink_grad_t = dot_left_t(d_two_low, activated)
        unused_act, gelu_back = jax.vjp(gelu_tanh, pre_act)
        d_pre = gelu_back(dot(d_two_low, w_shrink_t))[0].astype(BF)
        expand_grad = dot_left_t(ffn_in, d_pre)
        ffn_part = jnp.concatenate([expand_grad.astype(BF), shrink_grad_t.astype(BF)], axis=1)
        d_pre, ffn_part = lax.optimization_barrier((d_pre, ffn_part))
        ffn_sum = sum_data(ffn_part)
        d_normed = d_two + dot_right_t(d_pre, w_expand)
        unused_one, attn_back = jax.vjp(layer_norm, summed_one, attn_gain[layer], attn_shift[layer])
        d_one, attn_gain_part, attn_shift_part = attn_back(d_normed)
        d_one_low = d_one.astype(BF)
        d_mixed = dot(d_one_low, w_back_t).astype(BF)
        if layer < LAYERS - 1:
            d_mixed, attn_sum, ffn_grads[layer + 1] = lax.optimization_barrier(
                (d_mixed, attn_sum, ffn_grads[layer + 1])
            )
            attn_grads[layer + 1] = sum_parts(attn_sum, 4)
        d_query, d_key, d_value = attend_backward(query, keyval, logs, d_mixed, tables)
        (d_query, d_key, d_value), ffn_sum, attn_grads, layer_output = lax.optimization_barrier(
            ((d_query, d_key, d_value), ffn_sum, attn_grads, layer_output)
        )
        ffn_grads[layer] = sum_parts(ffn_sum, 2)
        others = dot_right_t(d_key, w_keyval[:, :width]) + dot_right_t(d_value, w_keyval[:, width:])
        others = others.astype(BF)
        d_query, d_key, d_value, others = lax.optimization_barrier((d_query, d_key, d_value, others))
        summed = lax.psum_scatter(others, "quad", scatter_dimension=0, tiled=True)
        attn_part = jnp.concatenate(
            [
                dot_left_t(own_inputs, d_query).astype(BF),
                dot_left_t(inputs, d_key).astype(BF),
                dot_left_t(inputs, d_value).astype(BF),
                dot_left_t(d_one_low, mixed).astype(BF),
            ],
            axis=1,
        )
        summed, attn_part = lax.optimization_barrier((summed, attn_part))
        attn_sum = sum_data(attn_part)
        state_grad = d_one + dot_right_t(d_query, w_query) + summed.astype(F32)
        norm_parts[layer] = (attn_gain_part, attn_shift_part, ffn_gain_part, ffn_shift_part)
    norm_sums = lax.psum(
        tuple(jnp.stack([norm_parts[l][k] for l in range(LAYERS)]) for k in range(4)), EVERY
    )
    attn_sum, ffn_grads, norm_sums = lax.optimization_barrier((attn_sum, ffn_grads, norm_sums))
    attn_grads[0] = sum_parts(attn_sum, 4)
    input_grad = lax.ppermute(state_grad.astype(BF), EVERY, moves_back).astype(F32)

    attn_own = jnp.stack(attn_grads)
    ffn_own = jnp.stack(ffn_grads)
    qkv_grad = attn_own[:, :, :3].reshape(LAYERS, depth, 3, head_local, HD)
    qkv_grad = qkv_grad.transpose(0, 1, 3, 2, 4).reshape(LAYERS, depth, 3 * chunk)
    out_w_grad = attn_own[:, :, 3].transpose(0, 2, 1)
    up_grad = ffn_own[:, :, 0]
    down_grad = ffn_own[:, :, 1].transpose(0, 2, 1)
    return (layer_output, input_grad, qkv_grad, out_w_grad, up_grad, down_grad) + tuple(norm_sums)


def solution(mesh):
    devices = mesh.devices
    tensor = devices.shape[1]
    split = jax.sharding.Mesh(
        devices.reshape(devices.shape[0] // (ROW * QUAD), ROW, QUAD, tensor), EVERY
    )
    placed = (
        P(EVERY, None),
        P(None, DATA, "tensor"),
        P(None, "tensor", DATA),
        P(None, DATA, "tensor"),
        P(None, "tensor", DATA),
        P(),
        P(),
        P(),
        P(),
        P(EVERY, None),
        P(DATA, None),
        P(DATA, None),
        P(DATA, "tensor", None, None),
    )
    return jax.shard_map(
        local,
        mesh=split,
        in_specs=placed,
        out_specs=(
            P(EVERY, None),
            P(EVERY, None),
            P(None, DATA, "tensor"),
            P(None, "tensor", DATA),
            P(None, DATA, "tensor"),
            P(None, "tensor", DATA),
            P(),
            P(),
            P(),
            P(),
        ),
        check_vma=False,
    )
```

```python
import functools

import jax
import jax.numpy as jnp
from jax import lax
from jax.experimental import pallas as pl
from jax.experimental.pallas import tpu as pltpu
from jax.sharding import PartitionSpec as P

HD = 64
BLK = 64
LAYERS = 2
LONGEST = 16
QUAD = 4
WIDE = QUAD * HD
STEP = 4
STEPS = LONGEST // STEP

ROW = 2
DATA = ("hi", "row", "quad")
EVERY = DATA + ("tensor",)

NORM_EPSILON = 1e-12
MASK_VALUE = -1e30
BF = jnp.bfloat16
F32 = jnp.float32


def layer_norm(summed, norm_gain, norm_shift):
    row_mean = jnp.mean(summed, axis=-1, keepdims=True)
    centred = summed - row_mean
    row_var = jnp.mean(centred * centred, axis=-1, keepdims=True)
    return centred * lax.rsqrt(row_var + NORM_EPSILON) * norm_gain + norm_shift


def gelu_tanh(values):
    return jax.nn.gelu(values, approximate=True)


def dot(left, right):
    return jnp.dot(left, right, preferred_element_type=F32)


def dot_right_t(left, right):
    return lax.dot_general(left, right, (((1,), (1,)), ((), ())), preferred_element_type=F32)


def dot_left_t(left, right):
    return lax.dot_general(left, right, (((0,), (0,)), ((), ())), preferred_element_type=F32)


def head_diagonal(rows):
    lane_head = lax.broadcasted_iota(jnp.int32, rows.shape, 1) // HD
    return jnp.concatenate(
        [jnp.where(lane_head == h, rows, jnp.zeros_like(rows)) for h in range(QUAD)], axis=0
    )


def diagonal_rows(full):
    lane_head = lax.broadcasted_iota(jnp.int32, (HD, WIDE), 1) // HD
    out = full[:HD]
    for h in range(1, QUAD):
        out = jnp.where(lane_head == h, full[h * HD : (h + 1) * HD], out)
    return out


def key_rows(keys_at, b, count):
    return [pl.ds(pl.multiple_of(keys_at[b, i] * BLK, BLK), BLK) for i in range(count)]


def stacked(ref, places):
    return jnp.concatenate([ref[p, :] for p in places], axis=0)


def row_sums(x):
    return jnp.sum(x.reshape(x.shape[0] // 8, 8, WIDE), axis=0)


def for_steps(steps, body):
    for n in range(1, STEPS + 1):
        pl.when(steps == n)(functools.partial(body, n * STEP))


def forward_kernel(keys_at, steps_of, q_ref, k_ref, v_ref, bias_ref, out_ref, log_ref):
    def one_block(b, carry):
        rows = pl.ds(pl.multiple_of(b * BLK, BLK), BLK)

        def attend(count):
            places = key_rows(keys_at, b, count)
            query = head_diagonal(q_ref[rows, :])
            raw = dot_right_t(stacked(k_ref, places), query)
            scores, peak = [], None
            for i in range(count):
                piece = raw[i * BLK : (i + 1) * BLK] + bias_ref[b, i : i + 1, :]
                scores.append(piece)
                high = jnp.max(piece.reshape(BLK // 8, 8, WIDE), axis=0)
                peak = high if peak is None else jnp.maximum(peak, high)
            peak = jnp.max(peak, axis=0, keepdims=True)
            total, weights = None, []
            for piece in scores:
                exponent = jnp.exp(piece - peak)
                part = row_sums(exponent)
                total = part if total is None else total + part
                weights.append(exponent.astype(BF))
            total = jnp.sum(total, axis=0, keepdims=True)
            mix = dot_left_t(jnp.concatenate(weights, axis=0), stacked(v_ref, places))
            column = jnp.transpose(jnp.broadcast_to(total, (128, WIDE)))
            mix = mix / jnp.concatenate([column, column], axis=1)
            out_ref[rows, :] = diagonal_rows(mix).astype(BF)
            log_ref[b] = peak + jnp.log(total)

        for_steps(steps_of[b], attend)
        return carry

    lax.fori_loop(0, q_ref.shape[0] // BLK, one_block, 0)


def backward_kernel(
    keys_at, steps_of, q_ref, k_ref, v_ref, bias_ref, log_ref, d_ref, dq_ref, dk_ref, dv_ref, dkey, dvalue
):
    dkey[...] = jnp.zeros_like(dkey)
    dvalue[...] = jnp.zeros_like(dvalue)

    def one_block(b, carry):
        rows = pl.ds(pl.multiple_of(b * BLK, BLK), BLK)

        def attend(count):
            places = key_rows(keys_at, b, count)
            query = head_diagonal(q_ref[rows, :])
            d_mixed = head_diagonal(d_ref[rows, :])
            logs = log_ref[b]
            keys = stacked(k_ref, places)
            raw = dot_right_t(keys, query)
            back = dot_right_t(stacked(v_ref, places), d_mixed)
            probs, inner = [], None
            for i in range(count):
                at = slice(i * BLK, (i + 1) * BLK)
                prob = jnp.exp(raw[at] + (bias_ref[b, i : i + 1, :] - logs))
                probs.append(prob)
                part = row_sums(prob * back[at])
                inner = part if inner is None else inner + part
            grad = dot(jnp.concatenate([p.astype(BF) for p in probs], axis=0), d_mixed)
            for i, p in enumerate(places):
                dvalue[p, :] += grad[i * BLK : (i + 1) * BLK]
            inner = jnp.sum(inner, axis=0, keepdims=True)
            d_score = jnp.concatenate(
                [
                    (prob * (back[i * BLK : (i + 1) * BLK] - inner)).astype(BF)
                    for i, prob in enumerate(probs)
                ],
                axis=0,
            )
            grad = dot(d_score, query)
            for i, p in enumerate(places):
                dkey[p, :] += grad[i * BLK : (i + 1) * BLK]
            d_query = dot_left_t(d_score, keys)
            dq_ref[rows, :] = (diagonal_rows(d_query) * (HD**-0.5)).astype(BF)

        for_steps(steps_of[b], attend)
        return carry

    lax.fori_loop(0, q_ref.shape[0] // BLK, one_block, 0)
    dk_ref[...] = dkey[...].astype(BF)
    dv_ref[...] = dvalue[...].astype(BF)


SHORT = pl.CostEstimate(flops=1_000_000, bytes_accessed=1_000_000, transcendentals=0)
MESH_ID = pl.DeviceIdType.MESH
CALL_GATHER_FIRST, CALL_GATHER, CALL_REDUCE, CALL_NORMS = range(4)


def quad_places():
    me = lax.axis_index("quad")
    mate = me + 1 - 2 * (me % 2)
    return me, mate, (me + 2) % QUAD, (mate + 2) % QUAD


def greet(*peers):
    barrier = pltpu.get_barrier_semaphore()
    for peer in peers:
        pl.semaphore_signal(barrier, inc=1, device_id=peer, device_id_type=MESH_ID)
    pl.semaphore_wait(barrier, len(peers))


def block_at(block, size, start=0, rows=None):
    return pl.ds(pl.multiple_of(block * size + start, 16), size if rows is None else rows)


def gather_kernel(pieces, *refs):
    count = len(pieces)
    owns, outs = refs[:count], refs[count : 2 * count]
    keep_sem, mate_send, mate_recv, far_send, far_recv, on_send, on_recv = refs[2 * count :]
    me, mate, far, cross = quad_places()
    greet({"quad": mate}, {"quad": far})

    def send(source, target, sends, recvs, at, peer):
        return pltpu.make_async_remote_copy(
            src_ref=source,
            dst_ref=target,
            send_sem=sends.at[at],
            recv_sem=recvs.at[at],
            device_id={"quad": peer},
            device_id_type=MESH_ID,
        )

    parts = []
    for n in range(count):
        size = owns[n].shape[0]
        step = size // pieces[n]
        for p in range(pieces[n]):
            parts.append((n, size, p * step, step))
    to_far = [
        send(owns[n].at[pl.ds(start, step)], outs[n].at[block_at(me, size, start, step)], far_send, far_recv, i, far)
        for i, (n, size, start, step) in enumerate(parts)
    ]
    for copy in to_far:
        copy.start()
    to_mate = [
        send(owns[n], outs[n].at[block_at(me, owns[n].shape[0])], mate_send, mate_recv, n, mate)
        for n in range(count)
    ]
    for copy in to_mate:
        copy.start()
    kept = [
        pltpu.make_async_copy(owns[n], outs[n].at[block_at(me, owns[n].shape[0])], keep_sem.at[n])
        for n in range(count)
    ]
    for copy in kept:
        copy.start()
    onward = []
    for i, (n, size, start, step) in enumerate(parts):
        to_far[i].wait_recv()
        came = outs[n].at[block_at(far, size, start, step)]
        copy = send(came, came, on_send, on_recv, i, mate)
        copy.start()
        onward.append(copy)
    for copy in to_mate + onward:
        copy.wait()
    for copy in to_far:
        copy.wait_send()
    for copy in kept:
        copy.wait()


def quad_gather(arrays, pieces, call):
    count, total = len(arrays), sum(pieces)
    sems = [pltpu.SemaphoreType.DMA((k,)) for k in (count, count, count, total, total, total, total)]
    return pl.pallas_call(
        functools.partial(gather_kernel, pieces),
        out_shape=[jax.ShapeDtypeStruct((QUAD * x.shape[0],) + x.shape[1:], x.dtype) for x in arrays],
        in_specs=[pl.BlockSpec(memory_space=pltpu.VMEM)] * count,
        out_specs=[pl.BlockSpec(memory_space=pl.ANY)] * count,
        scratch_shapes=sems,
        compiler_params=pltpu.CompilerParams(collective_id=call, has_side_effects=True),
        cost_estimate=SHORT,
        name="quad_gather",
    )(*arrays)


REDUCE_PIECES = 4


def reduce_kernel(
    parts_ref, out_ref, near, relay, beyond, mate_send, mate_recv, own_send, own_recv, far_send, far_recv
):
    me, mate, far, cross = quad_places()
    greet({"quad": mate}, {"quad": far})
    size = out_ref.shape[0]
    step = size // REDUCE_PIECES

    def send(source, target, send_sem, recv_sem, peer):
        copy = pltpu.make_async_remote_copy(
            src_ref=source,
            dst_ref=target,
            send_sem=send_sem,
            recv_sem=recv_sem,
            device_id={"quad": peer},
            device_id_type=MESH_ID,
        )
        copy.start()
        return copy

    to_mate = [
        send(
            parts_ref.at[block_at(cross, size, p * step, step)],
            near.at[1, pl.ds(p * step, step)],
            mate_send.at[p],
            mate_recv.at[p],
            mate,
        )
        for p in range(REDUCE_PIECES)
    ]
    own = send(parts_ref.at[block_at(mate, size)], near.at[0], own_send, own_recv, mate)
    to_far = []
    for p in range(REDUCE_PIECES):
        rows = pl.ds(p * step, step)
        to_mate[p].wait_recv()
        mine = parts_ref[block_at(far, size, p * step, step), :].astype(F32)
        relay[rows, :] = (mine + near[1, rows, :].astype(F32)).astype(BF)
        to_far.append(send(relay.at[rows], beyond.at[rows], far_send.at[p], far_recv.at[p], far))
    own.wait_recv()
    for p in range(REDUCE_PIECES):
        rows = pl.ds(p * step, step)
        to_far[p].wait_recv()
        mine = parts_ref[block_at(me, size, p * step, step), :].astype(F32)
        out_ref[rows, :] = mine + near[0, rows, :].astype(F32) + beyond[rows, :].astype(F32)
    for copy in to_mate + [own] + to_far:
        copy.wait_send()


def quad_reduce(parts):
    rows, width = parts.shape[0] // QUAD, parts.shape[1]
    dma = pltpu.SemaphoreType.DMA
    return pl.pallas_call(
        reduce_kernel,
        out_shape=jax.ShapeDtypeStruct((rows, width), F32),
        in_specs=[pl.BlockSpec(memory_space=pltpu.VMEM)],
        out_specs=pl.BlockSpec(memory_space=pltpu.VMEM),
        scratch_shapes=[
            pltpu.VMEM((2, rows, width), BF),
            pltpu.VMEM((rows, width), BF),
            pltpu.VMEM((rows, width), BF),
            dma((REDUCE_PIECES,)),
            dma((REDUCE_PIECES,)),
            dma,
            dma,
            dma((REDUCE_PIECES,)),
            dma((REDUCE_PIECES,)),
        ],
        compiler_params=pltpu.CompilerParams(collective_id=CALL_REDUCE, has_side_effects=True),
        cost_estimate=SHORT,
        name="quad_reduce",
    )(parts)


def norms_kernel(hops, x_ref, out_ref, held, came, send_sem, recv_sem):
    peers = []
    for axis, bit in hops:
        at = lax.axis_index(axis)
        peers.append({axis: at + bit - 2 * bit * ((at // bit) % 2)})
    greet(*peers)
    for n, peer in enumerate(peers):
        source = x_ref if n == 0 else held.at[n]
        copy = pltpu.make_async_remote_copy(
            src_ref=source,
            dst_ref=came.at[n],
            send_sem=send_sem.at[n],
            recv_sem=recv_sem.at[n],
            device_id=peer,
            device_id_type=MESH_ID,
        )
        copy.start()
        copy.wait()
        total = source[...] + came[n]
        if n == len(peers) - 1:
            out_ref[...] = total
        else:
            held[n + 1] = total


def sum_everywhere(x):
    hops = []
    for axis in ("quad", "row", "tensor", "hi"):
        bit = 1
        while bit < lax.axis_size(axis):
            hops.append((axis, bit))
            bit *= 2
    vmem = pltpu.VMEM((len(hops),) + x.shape, x.dtype)
    return pl.pallas_call(
        functools.partial(norms_kernel, tuple(hops)),
        out_shape=jax.ShapeDtypeStruct(x.shape, x.dtype),
        in_specs=[pl.BlockSpec(memory_space=pltpu.VMEM)],
        out_specs=pl.BlockSpec(memory_space=pltpu.VMEM),
        scratch_shapes=[
            vmem,
            vmem,
            pltpu.SemaphoreType.DMA((len(hops),)),
            pltpu.SemaphoreType.DMA((len(hops),)),
        ],
        compiler_params=pltpu.CompilerParams(collective_id=CALL_NORMS, has_side_effects=True),
        cost_estimate=SHORT,
        name="sum_everywhere",
    )(x)


def attend_forward(query, keyval, tables):
    keys_at, steps_of, bias = tables
    own, width = query.shape
    quads = width // WIDE
    rows = keyval.shape[0]
    blocks = own // BLK
    return pl.pallas_call(
        forward_kernel,
        grid_spec=pltpu.PrefetchScalarGridSpec(
            num_scalar_prefetch=2,
            grid=(quads,),
            in_specs=[
                pl.BlockSpec((own, WIDE), lambda i, *_: (0, i)),
                pl.BlockSpec((rows, WIDE), lambda i, *_: (0, i)),
                pl.BlockSpec((rows, WIDE), lambda i, *_: (0, i + quads)),
                pl.BlockSpec((blocks, LONGEST, WIDE), lambda i, *_: (0, 0, i)),
            ],
            out_specs=[
                pl.BlockSpec((own, WIDE), lambda i, *_: (0, i)),
                pl.BlockSpec((blocks, 1, WIDE), lambda i, *_: (0, 0, i)),
            ],
        ),
        out_shape=[
            jax.ShapeDtypeStruct((own, width), BF),
            jax.ShapeDtypeStruct((blocks, 1, width), F32),
        ],
        cost_estimate=SHORT,
        name="attend_forward",
    )(keys_at, steps_of, query, keyval, keyval, bias)


def attend_backward(query, keyval, logs, d_mixed, tables):
    keys_at, steps_of, bias = tables
    own, width = query.shape
    quads = width // WIDE
    rows = keyval.shape[0]
    blocks = own // BLK
    return pl.pallas_call(
        backward_kernel,
        grid_spec=pltpu.PrefetchScalarGridSpec(
            num_scalar_prefetch=2,
            grid=(quads,),
            in_specs=[
                pl.BlockSpec((own, WIDE), lambda i, *_: (0, i)),
                pl.BlockSpec((rows, WIDE), lambda i, *_: (0, i)),
                pl.BlockSpec((rows, WIDE), lambda i, *_: (0, i + quads)),
                pl.BlockSpec((blocks, LONGEST, WIDE), lambda i, *_: (0, 0, i)),
                pl.BlockSpec((blocks, 1, WIDE), lambda i, *_: (0, 0, i)),
                pl.BlockSpec((own, WIDE), lambda i, *_: (0, i)),
            ],
            out_specs=[
                pl.BlockSpec((own, WIDE), lambda i, *_: (0, i)),
                pl.BlockSpec((rows, WIDE), lambda i, *_: (0, i)),
                pl.BlockSpec((rows, WIDE), lambda i, *_: (0, i)),
            ],
            scratch_shapes=[
                pltpu.VMEM((rows, WIDE), F32),
                pltpu.VMEM((rows, WIDE), F32),
            ],
        ),
        out_shape=[
            jax.ShapeDtypeStruct((own, width), BF),
            jax.ShapeDtypeStruct((rows, width), BF),
            jax.ShapeDtypeStruct((rows, width), BF),
        ],
        cost_estimate=SHORT,
        name="attend_backward",
    )(keys_at, steps_of, query, keyval, keyval, bias, logs, d_mixed)


def attention_tables(doc_lengths, block_deal, random_rows, own_blocks, first_own):
    blocks = block_deal.shape[0]
    doc_ends = jnp.cumsum(doc_lengths)
    doc_starts = doc_ends - doc_lengths
    place = jnp.arange(blocks, dtype=jnp.int32)
    stored_at = jnp.sum(
        jnp.where(block_deal[None, :] == place[:, None], place[None, :], 0), axis=1
    )
    own = lax.dynamic_slice(block_deal, (first_own,), (own_blocks,))
    doc_index = jnp.sum((own[:, None] >= doc_ends[None, :]).astype(jnp.int32), axis=1)
    doc_pick = (
        doc_index[:, None] == jnp.arange(doc_lengths.shape[0], dtype=jnp.int32)[None, :]
    ).astype(jnp.int32)
    first_block = jnp.sum(doc_pick * doc_starts[None, :], axis=1)
    doc_blocks = jnp.sum(doc_pick * doc_lengths[None, :], axis=1)
    local = own - first_block
    other = jnp.arange(LONGEST, dtype=jnp.int32)
    wanted = jnp.minimum(first_block[:, None] + other[None, :], blocks - 1)
    keys_at = jnp.sum(
        jnp.where(wanted[:, :, None] == place[None, None, :], stored_at[None, None, :], 0), axis=2
    )
    own_pick = (own[:, None] == place[None, :]).astype(jnp.int32)
    picks = jnp.sum(own_pick[None, :, :, None] * random_rows[:, None, :, :], axis=2)
    picks = jnp.remainder(picks, doc_blocks[None, :, None])
    random_hit = jnp.any(picks[:, :, :, None] == other[None, None, None, :], axis=2)
    inside = other[None, :] < doc_blocks[:, None]
    near = jnp.abs(local[:, None] - other[None, :]) <= 1
    everywhere = (local[:, None] < 2) | (other[None, :] < 2)
    allowed = inside[None] & ((near | everywhere)[None] | random_hit)
    bias = jnp.where(allowed, 0.0, MASK_VALUE).astype(F32)
    bias = jnp.repeat(bias.transpose(1, 2, 0), BLK, axis=2)
    steps_of = (doc_blocks + STEP - 1) // STEP
    return keys_at, steps_of, bias


def to_home(steps, parts):
    pairs = []
    for hi in range(steps):
        for row in range(ROW):
            for quad in range(QUAD):
                side, core = quad // 2, quad % 2
                plane = parts - 1 - side if core else side
                for part in range(parts):
                    source = ((hi * ROW + row) * QUAD + quad) * parts + part
                    target = ((hi * ROW + row) * QUAD + part) * parts + plane
                    pairs.append((source, target))
    return pairs


def local(
    layer_input,
    w_qkv,
    w_out,
    w_up,
    w_down,
    attn_gain,
    attn_shift,
    ffn_gain,
    ffn_shift,
    out_grad,
    doc_lengths,
    block_deal,
    random_blocks,
):
    own_rows, width = layer_input.shape
    tensor = lax.axis_size("tensor")
    slot = lax.axis_index("quad")
    plane = lax.axis_index("tensor")
    head_local = random_blocks.shape[1]
    chunk = head_local * HD
    depth = w_qkv.shape[1]
    hidden = w_up.shape[2]
    score_scale = HD ** (-0.5)
    moves = to_home(lax.axis_size("hi"), tensor)
    moves_back = [(b, a) for a, b in moves]

    def shifted(x, by):
        return lax.ppermute(x, "tensor", [(i, (i + by) % tensor) for i in range(tensor)])

    def spread(shard):
        return [shard] + [shifted(shard, by) for by in range(1, tensor)]

    def attn_rows(qkv, back):
        qkv = qkv.reshape(depth, head_local, 3, HD).transpose(0, 2, 1, 3)
        shard = jnp.concatenate([qkv.reshape(depth, 3 * chunk), back.T], axis=1)
        parts = spread(shard)
        return jnp.concatenate(
            [part[:, p * chunk : (p + 1) * chunk] for p in range(4) for part in parts], axis=1
        )

    def ffn_rows(up, down):
        parts = spread(jnp.concatenate([up, down.T], axis=1))
        return jnp.concatenate(
            [part[:, p * hidden : (p + 1) * hidden] for p in range(2) for part in parts], axis=1
        )

    def over_data(rows):
        return lax.all_gather(rows, DATA, axis=0, tiled=True)

    docs, group_blocks = doc_lengths.shape[1], block_deal.shape[1]
    numbers = jnp.concatenate([doc_lengths[0], block_deal[0], random_blocks[0].reshape(-1)])
    numbers = jnp.stack([numbers // BLK, numbers % BLK]).astype(BF)
    numbers = jnp.pad(numbers, ((0, 14), (0, width - numbers.shape[1])))
    own_numbers = lax.ppermute(numbers, EVERY, moves)
    own_tokens = lax.ppermute(layer_input, EVERY, moves)
    attn_full = [over_data(attn_rows(w_qkv[0], w_out[0]))]
    own_tokens, own_numbers, up_0, down_0 = lax.optimization_barrier(
        (own_tokens, own_numbers, w_up[0], w_down[0])
    )
    ffn_full = [over_data(ffn_rows(up_0, down_0))]

    inputs, numbers = quad_gather([own_tokens, own_numbers], [4, 1], CALL_GATHER_FIRST)
    numbers = numbers.reshape(QUAD, 16, width)[:, :2].astype(jnp.int32)
    numbers = numbers[:, 0] * BLK + numbers[:, 1]
    lengths, deal = numbers[0, :docs], numbers[0, docs : docs + group_blocks]
    random_home = numbers[:, docs + group_blocks :][:, : random_blocks.size]
    random_home = random_home.reshape(tensor, head_local, group_blocks, -1)
    part_of = (plane - jnp.arange(tensor, dtype=jnp.int32)) % tensor
    part_pick = (part_of[:, None] == jnp.arange(tensor, dtype=jnp.int32)[None, :]).astype(jnp.int32)
    random_home = jnp.sum(part_pick[:, :, None, None, None] * random_home[None], axis=1)
    random_home = random_home.reshape(tensor * head_local, group_blocks, -1)
    own_blocks = own_rows // BLK
    tables = attention_tables(
        lengths,
        deal,
        random_home,
        own_blocks,
        slot * own_blocks,
    )

    stream = own_tokens.astype(F32)
    stored = []
    for layer in range(LAYERS):
        attn_w, ffn_w = attn_full[layer], ffn_full[layer]
        w_query = attn_w[:, :width]
        w_keyval = attn_w[:, width : 3 * width]
        w_back_t = attn_w[:, 3 * width :]
        w_expand = ffn_w[:, : hidden * tensor]
        w_shrink_t = ffn_w[:, hidden * tensor :]
        own_inputs = stream.astype(BF)
        if layer > 0:
            (inputs,) = quad_gather([own_inputs], [4], CALL_GATHER)
        query = (dot(own_inputs, w_query).astype(BF).astype(F32) * score_scale).astype(BF)
        keyval = dot(inputs, w_keyval).astype(BF)
        if layer == 0:
            keyval, later = lax.optimization_barrier((keyval, (w_qkv, w_out, w_up, w_down)))
            later_rows = [
                (attn_rows(later[0][other], later[1][other]), ffn_rows(later[2][other], later[3][other]))
                for other in range(1, LAYERS)
            ]
        mixed, logs = attend_forward(query, keyval, tables)
        if layer == 0:
            mixed, later_rows, own_grad = lax.optimization_barrier((mixed, later_rows, out_grad))
            for attn_later, ffn_later in later_rows:
                attn_full.append(over_data(attn_later))
                ffn_full.append(over_data(ffn_later))
            own_grad = lax.ppermute(own_grad, EVERY, moves)
        summed_one = stream + dot_right_t(mixed, w_back_t)
        normed = layer_norm(summed_one, attn_gain[layer], attn_shift[layer])
        ffn_in = normed.astype(BF)
        pre_act = dot(ffn_in, w_expand)
        activated = gelu_tanh(pre_act).astype(BF)
        summed_two = normed + dot_right_t(activated, w_shrink_t)
        stored.append(
            (own_inputs, inputs, query, keyval, mixed, logs, summed_one, ffn_in, pre_act, activated, summed_two)
        )
        stream = layer_norm(summed_two, ffn_gain[layer], ffn_shift[layer])
    layer_output = lax.ppermute(stream.astype(BF), EVERY, moves_back)

    def sum_parts(rows, sizes):
        pieces, start = [], 0
        for size in sizes:
            pieces.append(rows[:, start : start + tensor * size].reshape(depth, tensor, size))
            start += tensor * size
        total = jnp.concatenate([p[:, 0] for p in pieces], axis=1).astype(F32)
        for by in range(1, tensor):
            part = jnp.concatenate([p[:, by] for p in pieces], axis=1)
            total = total + shifted(part, tensor - by).astype(F32)
        return total

    def sum_data(part):
        return lax.psum_scatter(part, DATA, scatter_dimension=0, tiled=True)

    state_grad = own_grad.astype(F32)
    attn_grads = [None] * LAYERS
    ffn_grads = [None] * LAYERS
    norm_parts = [None] * LAYERS
    for layer in reversed(range(LAYERS)):
        (own_inputs, inputs, query, keyval, mixed, logs, summed_one, ffn_in, pre_act, activated, summed_two) = stored[layer]
        attn_w, ffn_w = attn_full[layer], ffn_full[layer]
        w_query = attn_w[:, :width]
        w_keyval = attn_w[:, width : 3 * width]
        w_back_t = attn_w[:, 3 * width :]
        w_expand = ffn_w[:, : hidden * tensor]
        w_shrink_t = ffn_w[:, hidden * tensor :]
        unused_two, ffn_back = jax.vjp(layer_norm, summed_two, ffn_gain[layer], ffn_shift[layer])
        d_two, ffn_gain_part, ffn_shift_part = ffn_back(state_grad)
        d_two_low = d_two.astype(BF)
        shrink_grad_t = dot_left_t(d_two_low, activated)
        unused_act, gelu_back = jax.vjp(gelu_tanh, pre_act)
        d_pre = gelu_back(dot(d_two_low, w_shrink_t))[0].astype(BF)
        expand_grad = dot_left_t(ffn_in, d_pre)
        d_normed = d_two + dot_right_t(d_pre, w_expand)
        unused_one, attn_back = jax.vjp(layer_norm, summed_one, attn_gain[layer], attn_shift[layer])
        d_one, attn_gain_part, attn_shift_part = attn_back(d_normed)
        norm_parts[layer] = (attn_gain_part, attn_shift_part, ffn_gain_part, ffn_shift_part)
        d_one_low = d_one.astype(BF)
        ffn_part = jnp.concatenate(
            [
                expand_grad.astype(BF),
                shrink_grad_t.astype(BF),
                dot_left_t(d_one_low, mixed).astype(BF),
            ],
            axis=1,
        )
        d_one_low, ffn_part = lax.optimization_barrier((d_one_low, ffn_part))
        ffn_sum = sum_data(ffn_part)
        d_mixed = dot(d_one_low, w_back_t).astype(BF)
        if layer < LAYERS - 1:
            d_mixed, attn_sum, ffn_grads[layer + 1] = lax.optimization_barrier(
                (d_mixed, attn_sum, ffn_grads[layer + 1])
            )
            attn_grads[layer + 1] = sum_parts(attn_sum, (chunk,) * 3)
        if layer == 0:
            norm_sums = sum_everywhere(
                jnp.stack([norm_parts[l][k] for k in range(4) for l in range(LAYERS)])
            )
            d_mixed, norm_sums = lax.optimization_barrier((d_mixed, norm_sums))
        d_query, d_key, d_value = attend_backward(query, keyval, logs, d_mixed, tables)
        (d_query, d_key, d_value), ffn_sum, attn_grads, layer_output = lax.optimization_barrier(
            ((d_query, d_key, d_value), ffn_sum, attn_grads, layer_output)
        )
        ffn_grads[layer] = sum_parts(ffn_sum, (hidden, hidden, chunk))
        others = dot_right_t(d_key, w_keyval[:, :width]) + dot_right_t(d_value, w_keyval[:, width:])
        others = others.astype(BF)
        d_query, d_key, d_value, others = lax.optimization_barrier((d_query, d_key, d_value, others))
        attn_part = jnp.concatenate(
            [
                dot_left_t(own_inputs, d_query).astype(BF),
                dot_left_t(inputs, d_key).astype(BF),
                dot_left_t(inputs, d_value).astype(BF),
            ],
            axis=1,
        )
        others, attn_part = lax.optimization_barrier((others, attn_part))
        attn_sum = sum_data(attn_part)
        summed = quad_reduce(others)
        state_grad = d_one + dot_right_t(d_query, w_query) + summed
    attn_sum, ffn_grads = lax.optimization_barrier((attn_sum, ffn_grads))
    attn_grads[0] = sum_parts(attn_sum, (chunk,) * 3)
    input_grad = lax.ppermute(state_grad.astype(BF), EVERY, moves_back).astype(F32)

    qkv_grad = jnp.stack(attn_grads).reshape(LAYERS, depth, 3, head_local, HD)
    qkv_grad = qkv_grad.transpose(0, 1, 3, 2, 4).reshape(LAYERS, depth, 3 * chunk)
    ffn_own = jnp.stack(ffn_grads)
    up_grad = ffn_own[:, :, :hidden]
    down_grad = ffn_own[:, :, hidden : 2 * hidden].transpose(0, 2, 1)
    out_w_grad = ffn_own[:, :, 2 * hidden :].transpose(0, 2, 1)
    return (layer_output, input_grad, qkv_grad, out_w_grad, up_grad, down_grad) + tuple(
        norm_sums[k * LAYERS : (k + 1) * LAYERS] for k in range(4)
    )


def solution(mesh):
    devices = mesh.devices
    tensor = devices.shape[1]
    split = jax.sharding.Mesh(
        devices.reshape(devices.shape[0] // (ROW * QUAD), ROW, QUAD, tensor), EVERY
    )
    placed = (
        P(EVERY, None),
        P(None, DATA, "tensor"),
        P(None, "tensor", DATA),
        P(None, DATA, "tensor"),
        P(None, "tensor", DATA),
        P(),
        P(),
        P(),
        P(),
        P(EVERY, None),
        P(DATA, None),
        P(DATA, None),
        P(DATA, "tensor", None, None),
    )
    return jax.shard_map(
        local,
        mesh=split,
        in_specs=placed,
        out_specs=(
            P(EVERY, None),
            P(EVERY, None),
            P(None, DATA, "tensor"),
            P(None, "tensor", DATA),
            P(None, DATA, "tensor"),
            P(None, "tensor", DATA),
            P(),
            P(),
            P(),
            P(),
        ),
        check_vma=False,
    )
```

```python
import functools

import jax
import jax.numpy as jnp
from jax import lax
from jax.experimental import pallas as pl
from jax.experimental.pallas import tpu as pltpu
from jax.sharding import PartitionSpec as P

HD = 64
BLK = 64
LAYERS = 2
LONGEST = 16
QUAD = 4
WIDE = QUAD * HD
STEP = 4
STEPS = LONGEST // STEP

ROW = 2
DATA = ("hi", "row", "quad")
EVERY = DATA + ("tensor",)

NORM_EPSILON = 1e-12
MASK_VALUE = -1e30
BF = jnp.bfloat16
F32 = jnp.float32


def layer_norm(summed, norm_gain, norm_shift):
    row_mean = jnp.mean(summed, axis=-1, keepdims=True)
    centred = summed - row_mean
    row_var = jnp.mean(centred * centred, axis=-1, keepdims=True)
    return centred * lax.rsqrt(row_var + NORM_EPSILON) * norm_gain + norm_shift


def gelu_tanh(values):
    return jax.nn.gelu(values, approximate=True)


def dot(left, right):
    return jnp.dot(left, right, preferred_element_type=F32)


def dot_right_t(left, right):
    return lax.dot_general(left, right, (((1,), (1,)), ((), ())), preferred_element_type=F32)


def dot_left_t(left, right):
    return lax.dot_general(left, right, (((0,), (0,)), ((), ())), preferred_element_type=F32)


def head_diagonal(rows):
    lane_head = lax.broadcasted_iota(jnp.int32, rows.shape, 1) // HD
    return jnp.concatenate(
        [jnp.where(lane_head == h, rows, jnp.zeros_like(rows)) for h in range(QUAD)], axis=0
    )


def diagonal_rows(full):
    lane_head = lax.broadcasted_iota(jnp.int32, (HD, WIDE), 1) // HD
    out = full[:HD]
    for h in range(1, QUAD):
        out = jnp.where(lane_head == h, full[h * HD : (h + 1) * HD], out)
    return out


def key_rows(keys_at, b, count):
    return [pl.ds(pl.multiple_of(keys_at[b, i] * BLK, BLK), BLK) for i in range(count)]


def stacked(ref, places):
    return jnp.concatenate([ref[p, :] for p in places], axis=0)


def row_sums(x):
    return jnp.sum(x.reshape(x.shape[0] // 8, 8, WIDE), axis=0)


def for_steps(steps, body):
    for n in range(1, STEPS + 1):
        pl.when(steps == n)(functools.partial(body, n * STEP))


def forward_kernel(keys_at, steps_of, q_ref, k_ref, v_ref, bias_ref, out_ref, log_ref):
    def one_block(b, carry):
        rows = pl.ds(pl.multiple_of(b * BLK, BLK), BLK)

        def attend(count):
            places = key_rows(keys_at, b, count)
            query = head_diagonal(q_ref[rows, :])
            raw = dot_right_t(stacked(k_ref, places), query)
            scores, peak = [], None
            for i in range(count):
                piece = raw[i * BLK : (i + 1) * BLK] + bias_ref[b, i : i + 1, :]
                scores.append(piece)
                high = jnp.max(piece.reshape(BLK // 8, 8, WIDE), axis=0)
                peak = high if peak is None else jnp.maximum(peak, high)
            peak = jnp.max(peak, axis=0, keepdims=True)
            total, weights = None, []
            for piece in scores:
                exponent = jnp.exp(piece - peak)
                part = row_sums(exponent)
                total = part if total is None else total + part
                weights.append(exponent.astype(BF))
            total = jnp.sum(total, axis=0, keepdims=True)
            mix = dot_left_t(jnp.concatenate(weights, axis=0), stacked(v_ref, places))
            column = jnp.transpose(jnp.broadcast_to(total, (128, WIDE)))
            mix = mix / jnp.concatenate([column, column], axis=1)
            out_ref[rows, :] = diagonal_rows(mix).astype(BF)
            log_ref[b] = peak + jnp.log(total)

        for_steps(steps_of[b], attend)
        return carry

    lax.fori_loop(0, q_ref.shape[0] // BLK, one_block, 0)


def backward_kernel(
    keys_at,
    steps_of,
    q_ref,
    k_ref,
    v_ref,
    bias_ref,
    log_ref,
    d_ref,
    own_ref,
    in_ref,
    wk_ref,
    wv_ref,
    dq_ref,
    others_ref,
    grad_ref,
    dkey,
    dvalue,
    low,
    back_sum,
):
    dkey[...] = jnp.zeros_like(dkey)
    dvalue[...] = jnp.zeros_like(dvalue)

    def one_block(b, carry):
        rows = pl.ds(pl.multiple_of(b * BLK, BLK), BLK)

        def attend(count):
            places = key_rows(keys_at, b, count)
            query = head_diagonal(q_ref[rows, :])
            d_mixed = head_diagonal(d_ref[rows, :])
            logs = log_ref[b]
            keys = stacked(k_ref, places)
            raw = dot_right_t(keys, query)
            back = dot_right_t(stacked(v_ref, places), d_mixed)
            probs, inner = [], None
            for i in range(count):
                at = slice(i * BLK, (i + 1) * BLK)
                prob = jnp.exp(raw[at] + (bias_ref[b, i : i + 1, :] - logs))
                probs.append(prob)
                part = row_sums(prob * back[at])
                inner = part if inner is None else inner + part
            grad = dot(jnp.concatenate([p.astype(BF) for p in probs], axis=0), d_mixed)
            for i, p in enumerate(places):
                dvalue[p, :] += grad[i * BLK : (i + 1) * BLK]
            inner = jnp.sum(inner, axis=0, keepdims=True)
            d_score = jnp.concatenate(
                [
                    (prob * (back[i * BLK : (i + 1) * BLK] - inner)).astype(BF)
                    for i, prob in enumerate(probs)
                ],
                axis=0,
            )
            grad = dot(d_score, query)
            for i, p in enumerate(places):
                dkey[p, :] += grad[i * BLK : (i + 1) * BLK]
            d_query = dot_left_t(d_score, keys)
            dq_ref[rows, :] = (diagonal_rows(d_query) * (HD**-0.5)).astype(BF)

        for_steps(steps_of[b], attend)
        return carry

    lax.fori_loop(0, q_ref.shape[0] // BLK, one_block, 0)

    low[0] = dkey[...].astype(BF)
    low[1] = dvalue[...].astype(BF)
    grad_ref[:, :WIDE] = dot_left_t(own_ref[...], dq_ref[...]).astype(BF)
    grad_ref[:, WIDE : 2 * WIDE] = dot_left_t(in_ref[...], low[0]).astype(BF)
    grad_ref[:, 2 * WIDE :] = dot_left_t(in_ref[...], low[1]).astype(BF)
    quad = pl.program_id(0)

    def others(r, carry):
        at = pl.ds(pl.multiple_of(r * WIDE, WIDE), WIDE)
        part = dot_right_t(low[0, at, :], wk_ref[...]) + dot_right_t(low[1, at, :], wv_ref[...])
        so_far = jnp.where(quad == 0, jnp.zeros_like(part), back_sum[at, :]) + part
        back_sum[at, :] = so_far
        others_ref[at, :] = so_far.astype(BF)
        return carry

    lax.fori_loop(0, in_ref.shape[0] // WIDE, others, 0)


SHORT = pl.CostEstimate(flops=1_000_000, bytes_accessed=1_000_000, transcendentals=0)
MESH_ID = pl.DeviceIdType.MESH
CALL_GATHER_FIRST, CALL_GATHER, CALL_REDUCE, CALL_NORMS, CALL_ROWS, CALL_LINE_FFN, CALL_LINE_ATTN, CALL_BOTH = range(8)


def quad_places():
    me = lax.axis_index("quad")
    mate = me + 1 - 2 * (me % 2)
    return me, mate, (me + 2) % QUAD, (mate + 2) % QUAD


def greet(*peers):
    barrier = pltpu.get_barrier_semaphore()
    for peer in peers:
        pl.semaphore_signal(barrier, inc=1, device_id=peer, device_id_type=MESH_ID)
    pl.semaphore_wait(barrier, len(peers))


def block_at(block, size, start=0, rows=None):
    return pl.ds(pl.multiple_of(block * size + start, 16), size if rows is None else rows)


def gather_kernel(pieces, *refs):
    count = len(pieces)
    owns, outs = refs[:count], refs[count : 2 * count]
    keep_sem, mate_send, mate_recv, far_send, far_recv, on_send, on_recv = refs[2 * count :]
    me, mate, far, cross = quad_places()
    greet({"quad": mate}, {"quad": far})

    def send(source, target, sends, recvs, at, peer):
        return pltpu.make_async_remote_copy(
            src_ref=source,
            dst_ref=target,
            send_sem=sends.at[at],
            recv_sem=recvs.at[at],
            device_id={"quad": peer},
            device_id_type=MESH_ID,
        )

    parts = []
    for n in range(count):
        size = owns[n].shape[0]
        step = size // pieces[n]
        for p in range(pieces[n]):
            parts.append((n, size, p * step, step))
    to_far = [
        send(owns[n].at[pl.ds(start, step)], outs[n].at[block_at(me, size, start, step)], far_send, far_recv, i, far)
        for i, (n, size, start, step) in enumerate(parts)
    ]
    for copy in to_far:
        copy.start()
    to_mate = [
        send(owns[n], outs[n].at[block_at(me, owns[n].shape[0])], mate_send, mate_recv, n, mate)
        for n in range(count)
    ]
    for copy in to_mate:
        copy.start()
    kept = [
        pltpu.make_async_copy(owns[n], outs[n].at[block_at(me, owns[n].shape[0])], keep_sem.at[n])
        for n in range(count)
    ]
    for copy in kept:
        copy.start()
    onward = []
    for i, (n, size, start, step) in enumerate(parts):
        to_far[i].wait_recv()
        came = outs[n].at[block_at(far, size, start, step)]
        copy = send(came, came, on_send, on_recv, i, mate)
        copy.start()
        onward.append(copy)
    for copy in to_mate + onward:
        copy.wait()
    for copy in to_far:
        copy.wait_send()
    for copy in kept:
        copy.wait()


def quad_gather(arrays, pieces, call):
    count, total = len(arrays), sum(pieces)
    sems = [pltpu.SemaphoreType.DMA((k,)) for k in (count, count, count, total, total, total, total)]
    return pl.pallas_call(
        functools.partial(gather_kernel, pieces),
        out_shape=[jax.ShapeDtypeStruct((QUAD * x.shape[0],) + x.shape[1:], x.dtype) for x in arrays],
        in_specs=[pl.BlockSpec(memory_space=pltpu.VMEM)] * count,
        out_specs=[pl.BlockSpec(memory_space=pl.ANY)] * count,
        scratch_shapes=sems,
        compiler_params=pltpu.CompilerParams(collective_id=call, has_side_effects=True),
        cost_estimate=SHORT,
        name="quad_gather",
    )(*arrays)


REDUCE_PIECES = 4


def reduce_kernel(
    parts_ref,
    out_ref,
    near,
    relay,
    beyond,
    mate_send,
    mate_recv,
    own_send,
    own_recv,
    far_send,
    far_recv,
    greeted=False,
):
    me, mate, far, cross = quad_places()
    if not greeted:
        greet({"quad": mate}, {"quad": far})
    size = out_ref.shape[0]
    step = size // REDUCE_PIECES

    def send(source, target, send_sem, recv_sem, peer):
        copy = pltpu.make_async_remote_copy(
            src_ref=source,
            dst_ref=target,
            send_sem=send_sem,
            recv_sem=recv_sem,
            device_id={"quad": peer},
            device_id_type=MESH_ID,
        )
        copy.start()
        return copy

    to_mate = [
        send(
            parts_ref.at[block_at(cross, size, p * step, step)],
            near.at[1, pl.ds(p * step, step)],
            mate_send.at[p],
            mate_recv.at[p],
            mate,
        )
        for p in range(REDUCE_PIECES)
    ]
    own = send(parts_ref.at[block_at(mate, size)], near.at[0], own_send, own_recv, mate)
    to_far = []
    for p in range(REDUCE_PIECES):
        rows = pl.ds(p * step, step)
        to_mate[p].wait_recv()
        mine = parts_ref[block_at(far, size, p * step, step), :].astype(F32)
        relay[rows, :] = (mine + near[1, rows, :].astype(F32)).astype(BF)
        to_far.append(send(relay.at[rows], beyond.at[rows], far_send.at[p], far_recv.at[p], far))
    own.wait_recv()
    for p in range(REDUCE_PIECES):
        rows = pl.ds(p * step, step)
        to_far[p].wait_recv()
        mine = parts_ref[block_at(me, size, p * step, step), :].astype(F32)
        out_ref[rows, :] = mine + near[0, rows, :].astype(F32) + beyond[rows, :].astype(F32)
    for copy in to_mate + [own] + to_far:
        copy.wait_send()


def reduce_scratch(rows, width):
    one, each = pltpu.SemaphoreType.DMA, pltpu.SemaphoreType.DMA((REDUCE_PIECES,))
    low = pltpu.VMEM((rows, width), BF)
    return [pltpu.VMEM((2, rows, width), BF), low, low, each, each, one, one, each, each]


def quad_reduce(parts):
    rows, width = parts.shape[0] // QUAD, parts.shape[1]
    return pl.pallas_call(
        reduce_kernel,
        out_shape=jax.ShapeDtypeStruct((rows, width), F32),
        in_specs=[pl.BlockSpec(memory_space=pltpu.VMEM)],
        out_specs=pl.BlockSpec(memory_space=pltpu.VMEM),
        scratch_shapes=reduce_scratch(rows, width),
        compiler_params=pltpu.CompilerParams(collective_id=CALL_REDUCE, has_side_effects=True),
        cost_estimate=SHORT,
        name="quad_reduce",
    )(parts)


def both_kernel(sizes, planes, parts_ref, x_ref, out_ref, line_ref, *scratch):
    me, mate, far, cross = quad_places()
    greet({"quad": mate}, {"quad": far}, *line_peers(planes))
    held, came, send_sem, recv_sem = scratch[:4]
    copies = line_start(sizes, planes, x_ref, held, came, send_sem, recv_sem)
    reduce_kernel(parts_ref, out_ref, *scratch[4:], greeted=True)
    line_finish(sizes, planes, x_ref, line_ref, came, copies)


def quad_reduce_and_line(parts, lines, sizes, planes):
    rows, width = parts.shape[0] // QUAD, parts.shape[1]
    shape = (lines.shape[0], sum(sizes))
    vmem = pl.BlockSpec(memory_space=pltpu.VMEM)
    return pl.pallas_call(
        functools.partial(both_kernel, sizes, planes),
        out_shape=[jax.ShapeDtypeStruct((rows, width), F32), jax.ShapeDtypeStruct(shape, F32)],
        in_specs=[vmem, vmem],
        out_specs=[vmem, vmem],
        scratch_shapes=line_scratch(shape, planes) + reduce_scratch(rows, width),
        compiler_params=pltpu.CompilerParams(collective_id=CALL_BOTH, has_side_effects=True),
        cost_estimate=SHORT,
        name="quad_reduce_and_line",
    )(parts, lines)


def norms_kernel(hops, x_ref, out_ref, held, came, send_sem, recv_sem):
    peers = []
    for axis, bit in hops:
        at = lax.axis_index(axis)
        peers.append({axis: at + bit - 2 * bit * ((at // bit) % 2)})
    greet(*peers)
    for n, peer in enumerate(peers):
        source = x_ref if n == 0 else held.at[n]
        copy = pltpu.make_async_remote_copy(
            src_ref=source,
            dst_ref=came.at[n],
            send_sem=send_sem.at[n],
            recv_sem=recv_sem.at[n],
            device_id=peer,
            device_id_type=MESH_ID,
        )
        copy.start()
        copy.wait()
        total = source[...] + came[n]
        if n == len(peers) - 1:
            out_ref[...] = total
        else:
            held[n + 1] = total


def sum_everywhere(x):
    hops = []
    for axis in ("quad", "row", "tensor", "hi"):
        bit = 1
        while bit < lax.axis_size(axis):
            hops.append((axis, bit))
            bit *= 2
    vmem = pltpu.VMEM((len(hops),) + x.shape, x.dtype)
    return pl.pallas_call(
        functools.partial(norms_kernel, tuple(hops)),
        out_shape=jax.ShapeDtypeStruct(x.shape, x.dtype),
        in_specs=[pl.BlockSpec(memory_space=pltpu.VMEM)],
        out_specs=pl.BlockSpec(memory_space=pltpu.VMEM),
        scratch_shapes=[
            vmem,
            vmem,
            pltpu.SemaphoreType.DMA((len(hops),)),
            pltpu.SemaphoreType.DMA((len(hops),)),
        ],
        compiler_params=pltpu.CompilerParams(collective_id=CALL_NORMS, has_side_effects=True),
        cost_estimate=SHORT,
        name="sum_everywhere",
    )(x)


def rows_kernel(parts, own_ref, out_ref, keep_sem, line_send, line_recv, send_sem, recv_sem):
    me, mate, far, cross = quad_places()
    row, plane = lax.axis_index("row"), lax.axis_index("tensor")
    other = 1 - row
    line = [{"tensor": (plane + by) % parts} for by in range(1, parts)]
    to_x, to_y, to_mate = {"quad": far}, {"row": other}, {"quad": mate}
    greet(*line, to_x, to_y, to_mate)
    size, width = own_ref.shape

    def block(at_row, at_quad, part):
        return out_ref.at[block_at(at_row * QUAD + at_quad, size), pl.ds(part * width, width)]

    used = []

    def send(source, target, peer, n):
        copy = pltpu.make_async_remote_copy(
            src_ref=source,
            dst_ref=target,
            send_sem=send_sem.at[n],
            recv_sem=recv_sem.at[n],
            device_id=peer,
            device_id_type=MESH_ID,
        )
        copy.start()
        used.append(copy)
        return copy

    along = []
    for by in range(1, parts):
        copy = pltpu.make_async_remote_copy(
            src_ref=own_ref,
            dst_ref=block(row, me, by),
            send_sem=line_send.at[by - 1],
            recv_sem=line_recv.at[by - 1],
            device_id=line[by - 1],
            device_id_type=MESH_ID,
        )
        copy.start()
        along.append(copy)
    keep = pltpu.make_async_copy(own_ref, block(row, me, 0), keep_sem)
    keep.start()
    near_x, near_y, beyond, mates = [], [], [], []
    for part in range(parts + 1):
        if part < parts:
            if part:
                along[part - 1].wait_recv()
            source = own_ref if part == 0 else block(row, me, part)
            target = block(row, me, part)
            near_x.append(send(source, target, to_x, part))
            near_y.append(send(source, target, to_y, parts + part))
            mates.append(send(source, target, to_mate, 2 * parts + part))
        if part:
            done = part - 1
            from_x, from_y = block(row, far, done), block(other, me, done)
            near_x[done].wait_recv()
            near_y[done].wait_recv()
            if done % 2:
                beyond.append(send(from_y, from_y, to_x, 3 * parts + done))
            else:
                beyond.append(send(from_x, from_x, to_y, 3 * parts + done))
            mates.append(send(from_x, from_x, to_mate, 4 * parts + done))
            mates.append(send(from_y, from_y, to_mate, 5 * parts + done))
    for part in range(parts):
        beyond[part].wait_recv()
        came = block(other, far, part)
        mates.append(send(came, came, to_mate, 6 * parts + part))
    for copy in mates:
        copy.wait_recv()
    for copy in along + used:
        copy.wait_send()
    keep.wait()


def gather_rows(rows, parts):
    size, width = rows.shape
    dma = pltpu.SemaphoreType.DMA
    return pl.pallas_call(
        functools.partial(rows_kernel, parts),
        out_shape=jax.ShapeDtypeStruct((ROW * QUAD * size, parts * width), rows.dtype),
        in_specs=[pl.BlockSpec(memory_space=pltpu.VMEM)],
        out_specs=pl.BlockSpec(memory_space=pl.ANY),
        scratch_shapes=[dma, dma((parts - 1,)), dma((parts - 1,)), dma((7 * parts,)), dma((7 * parts,))],
        compiler_params=pltpu.CompilerParams(collective_id=CALL_ROWS, has_side_effects=True),
        cost_estimate=SHORT,
        name="gather_rows",
    )(rows)


def regroup_kernel(parts, kinds, x_ref, out_ref):
    size = x_ref.shape[1] // (parts * kinds)
    for kind in range(kinds):
        for part in range(parts):
            to, at = (kind * parts + part) * size, (part * kinds + kind) * size
            out_ref[:, to : to + size] = x_ref[:, at : at + size]


def regroup(rows, parts, kinds):
    block = pl.BlockSpec((rows.shape[0] // 4, rows.shape[1]), lambda i: (i, 0))
    return pl.pallas_call(
        functools.partial(regroup_kernel, parts, kinds),
        out_shape=jax.ShapeDtypeStruct(rows.shape, rows.dtype),
        grid=(4,),
        in_specs=[block],
        out_specs=block,
        cost_estimate=SHORT,
        name="regroup",
    )(rows)


def line_peers(parts):
    plane = lax.axis_index("tensor")
    return [{"tensor": (plane + by) % parts} for by in range(1, parts)]


def line_pick(sizes, parts, x_ref, part):
    columns, start = [], 0
    for size in sizes:
        columns.append(x_ref[:, start + part * size : start + (part + 1) * size])
        start += parts * size
    return jnp.concatenate(columns, axis=1)


def line_start(sizes, parts, x_ref, held, came, send_sem, recv_sem):
    plane = lax.axis_index("tensor")
    copies = []
    for by in range(1, parts):
        held[by - 1] = line_pick(sizes, parts, x_ref, by)
        copy = pltpu.make_async_remote_copy(
            src_ref=held.at[by - 1],
            dst_ref=came.at[by - 1],
            send_sem=send_sem.at[by - 1],
            recv_sem=recv_sem.at[by - 1],
            device_id={"tensor": (plane + parts - by) % parts},
            device_id_type=MESH_ID,
        )
        copy.start()
        copies.append(copy)
    return copies


def line_finish(sizes, parts, x_ref, out_ref, came, copies):
    total = line_pick(sizes, parts, x_ref, 0).astype(F32)
    for by in range(1, parts):
        copies[by - 1].wait_recv()
        total = total + came[by - 1].astype(F32)
    out_ref[...] = total
    for copy in copies:
        copy.wait_send()


def line_scratch(shape, parts):
    dma = pltpu.SemaphoreType.DMA((parts - 1,))
    return [pltpu.VMEM((parts - 1,) + shape, BF), pltpu.VMEM((parts - 1,) + shape, BF), dma, dma]


def parts_kernel(sizes, parts, x_ref, out_ref, held, came, send_sem, recv_sem):
    greet(*line_peers(parts))
    copies = line_start(sizes, parts, x_ref, held, came, send_sem, recv_sem)
    line_finish(sizes, parts, x_ref, out_ref, came, copies)


def sum_line(rows, sizes, parts, call):
    shape = (rows.shape[0], sum(sizes))
    return pl.pallas_call(
        functools.partial(parts_kernel, sizes, parts),
        out_shape=jax.ShapeDtypeStruct(shape, F32),
        in_specs=[pl.BlockSpec(memory_space=pltpu.VMEM)],
        out_specs=pl.BlockSpec(memory_space=pltpu.VMEM),
        scratch_shapes=line_scratch(shape, parts),
        compiler_params=pltpu.CompilerParams(collective_id=call, has_side_effects=True),
        cost_estimate=SHORT,
        name="sum_line",
    )(rows)


def attend_forward(query, keyval, tables):
    keys_at, steps_of, bias = tables
    own, width = query.shape
    quads = width // WIDE
    rows = keyval.shape[0]
    blocks = own // BLK
    return pl.pallas_call(
        forward_kernel,
        grid_spec=pltpu.PrefetchScalarGridSpec(
            num_scalar_prefetch=2,
            grid=(quads,),
            in_specs=[
                pl.BlockSpec((own, WIDE), lambda i, *_: (0, i)),
                pl.BlockSpec((rows, WIDE), lambda i, *_: (0, i)),
                pl.BlockSpec((rows, WIDE), lambda i, *_: (0, i + quads)),
                pl.BlockSpec((blocks, LONGEST, WIDE), lambda i, *_: (0, 0, i)),
            ],
            out_specs=[
                pl.BlockSpec((own, WIDE), lambda i, *_: (0, i)),
                pl.BlockSpec((blocks, 1, WIDE), lambda i, *_: (0, 0, i)),
            ],
        ),
        out_shape=[
            jax.ShapeDtypeStruct((own, width), BF),
            jax.ShapeDtypeStruct((blocks, 1, width), F32),
        ],
        cost_estimate=SHORT,
        name="attend_forward",
    )(keys_at, steps_of, query, keyval, keyval, bias)


def attend_backward(query, keyval, logs, d_mixed, tables, own_inputs, inputs, w_keyval):
    keys_at, steps_of, bias = tables
    own, width = query.shape
    quads = width // WIDE
    rows, depth = inputs.shape
    blocks = own // BLK
    once = pl.Buffered(1)
    return pl.pallas_call(
        backward_kernel,
        grid_spec=pltpu.PrefetchScalarGridSpec(
            num_scalar_prefetch=2,
            grid=(quads,),
            in_specs=[
                pl.BlockSpec((own, WIDE), lambda i, *_: (0, i)),
                pl.BlockSpec((rows, WIDE), lambda i, *_: (0, i)),
                pl.BlockSpec((rows, WIDE), lambda i, *_: (0, i + quads)),
                pl.BlockSpec((blocks, LONGEST, WIDE), lambda i, *_: (0, 0, i)),
                pl.BlockSpec((blocks, 1, WIDE), lambda i, *_: (0, 0, i)),
                pl.BlockSpec((own, WIDE), lambda i, *_: (0, i)),
                pl.BlockSpec((own, depth), lambda i, *_: (0, 0), pipeline_mode=once),
                pl.BlockSpec((rows, depth), lambda i, *_: (0, 0), pipeline_mode=once),
                pl.BlockSpec((depth, WIDE), lambda i, *_: (0, i)),
                pl.BlockSpec((depth, WIDE), lambda i, *_: (0, i + quads)),
            ],
            out_specs=[
                pl.BlockSpec((own, WIDE), lambda i, *_: (0, i)),
                pl.BlockSpec((rows, depth), lambda i, *_: (0, 0)),
                pl.BlockSpec((depth, 3 * WIDE), lambda i, *_: (0, i)),
            ],
            scratch_shapes=[
                pltpu.VMEM((rows, WIDE), F32),
                pltpu.VMEM((rows, WIDE), F32),
                pltpu.VMEM((2, rows, WIDE), BF),
                pltpu.VMEM((rows, depth), F32),
            ],
        ),
        out_shape=[
            jax.ShapeDtypeStruct((own, width), BF),
            jax.ShapeDtypeStruct((rows, depth), BF),
            jax.ShapeDtypeStruct((depth, 3 * width), BF),
        ],
        cost_estimate=SHORT,
        name="attend_backward",
    )(keys_at, steps_of, query, keyval, keyval, bias, logs, d_mixed, own_inputs, inputs, w_keyval, w_keyval)


def attention_tables(doc_lengths, block_deal, random_rows, own_blocks, first_own):
    blocks = block_deal.shape[0]
    doc_ends = jnp.cumsum(doc_lengths)
    doc_starts = doc_ends - doc_lengths
    place = jnp.arange(blocks, dtype=jnp.int32)
    stored_at = jnp.sum(
        jnp.where(block_deal[None, :] == place[:, None], place[None, :], 0), axis=1
    )
    own = lax.dynamic_slice(block_deal, (first_own,), (own_blocks,))
    doc_index = jnp.sum((own[:, None] >= doc_ends[None, :]).astype(jnp.int32), axis=1)
    doc_pick = (
        doc_index[:, None] == jnp.arange(doc_lengths.shape[0], dtype=jnp.int32)[None, :]
    ).astype(jnp.int32)
    first_block = jnp.sum(doc_pick * doc_starts[None, :], axis=1)
    doc_blocks = jnp.sum(doc_pick * doc_lengths[None, :], axis=1)
    local = own - first_block
    other = jnp.arange(LONGEST, dtype=jnp.int32)
    wanted = jnp.minimum(first_block[:, None] + other[None, :], blocks - 1)
    keys_at = jnp.sum(
        jnp.where(wanted[:, :, None] == place[None, None, :], stored_at[None, None, :], 0), axis=2
    )
    own_pick = (own[:, None] == place[None, :]).astype(jnp.int32)
    picks = jnp.sum(own_pick[None, :, :, None] * random_rows[:, None, :, :], axis=2)
    picks = jnp.remainder(picks, doc_blocks[None, :, None])
    random_hit = jnp.any(picks[:, :, :, None] == other[None, None, None, :], axis=2)
    inside = other[None, :] < doc_blocks[:, None]
    near = jnp.abs(local[:, None] - other[None, :]) <= 1
    everywhere = (local[:, None] < 2) | (other[None, :] < 2)
    allowed = inside[None] & ((near | everywhere)[None] | random_hit)
    bias = jnp.where(allowed, 0.0, MASK_VALUE).astype(F32)
    bias = jnp.repeat(bias.transpose(1, 2, 0), BLK, axis=2)
    steps_of = (doc_blocks + STEP - 1) // STEP
    return keys_at, steps_of, bias


def to_home(steps, parts):
    pairs = []
    for hi in range(steps):
        for row in range(ROW):
            for quad in range(QUAD):
                side, core = quad // 2, quad % 2
                plane = parts - 1 - side if core else side
                for part in range(parts):
                    source = ((hi * ROW + row) * QUAD + quad) * parts + part
                    target = ((hi * ROW + row) * QUAD + part) * parts + plane
                    pairs.append((source, target))
    return pairs


def local(
    layer_input,
    w_qkv,
    w_out,
    w_up,
    w_down,
    attn_gain,
    attn_shift,
    ffn_gain,
    ffn_shift,
    out_grad,
    doc_lengths,
    block_deal,
    random_blocks,
):
    own_rows, width = layer_input.shape
    tensor = lax.axis_size("tensor")
    slot = lax.axis_index("quad")
    plane = lax.axis_index("tensor")
    head_local = random_blocks.shape[1]
    chunk = head_local * HD
    depth = w_qkv.shape[1]
    hidden = w_up.shape[2]
    score_scale = HD ** (-0.5)
    moves = to_home(lax.axis_size("hi"), tensor)
    moves_back = [(b, a) for a, b in moves]

    def shifted(x, by):
        return lax.ppermute(x, "tensor", [(i, (i + by) % tensor) for i in range(tensor)])

    def spread(shard):
        return [shard] + [shifted(shard, by) for by in range(1, tensor)]

    def by_kind(parts, kinds):
        rows = jnp.stack([part.reshape(depth, kinds, -1) for part in parts], axis=2)
        return rows.reshape(depth, -1)

    def attn_shard(qkv, back):
        qkv = qkv.reshape(depth, head_local, 3, HD).transpose(0, 2, 1, 3)
        return jnp.concatenate([qkv.reshape(depth, 3 * chunk), back.T], axis=1)

    def attn_rows(qkv, back):
        return by_kind(spread(attn_shard(qkv, back)), 4)

    def ffn_rows(up, down):
        return by_kind(spread(jnp.concatenate([up, down.T], axis=1)), 2)

    def over_data(rows):
        return lax.all_gather(rows, DATA, axis=0, tiled=True)

    docs, group_blocks = doc_lengths.shape[1], block_deal.shape[1]
    numbers = jnp.concatenate([doc_lengths[0], block_deal[0], random_blocks[0].reshape(-1)])
    numbers = jnp.stack([numbers // BLK, numbers % BLK]).astype(BF)
    numbers = jnp.pad(numbers, ((0, 14), (0, width - numbers.shape[1])))
    own_numbers = lax.ppermute(numbers, EVERY, moves)
    own_tokens = lax.ppermute(layer_input, EVERY, moves)
    if lax.axis_size("hi") == 1:
        rows = gather_rows(attn_shard(w_qkv[0], w_out[0]), tensor)
        rows, own_tokens, own_numbers, up_0, down_0 = lax.optimization_barrier(
            (rows, own_tokens, own_numbers, w_up[0], w_down[0])
        )
        attn_full = [regroup(rows, tensor, 4)]
    else:
        attn_full = [over_data(attn_rows(w_qkv[0], w_out[0]))]
        own_tokens, own_numbers, up_0, down_0 = lax.optimization_barrier(
            (own_tokens, own_numbers, w_up[0], w_down[0])
        )
    first_rows = ffn_rows(up_0, down_0)

    inputs, numbers = quad_gather([own_tokens, own_numbers], [4, 1], CALL_GATHER_FIRST)
    inputs, first_rows = lax.optimization_barrier((inputs, first_rows))
    ffn_full = [over_data(first_rows)]
    numbers = numbers.reshape(QUAD, 16, width)[:, :2].astype(jnp.int32)
    numbers = numbers[:, 0] * BLK + numbers[:, 1]
    lengths, deal = numbers[0, :docs], numbers[0, docs : docs + group_blocks]
    random_home = numbers[:, docs + group_blocks :][:, : random_blocks.size]
    random_home = random_home.reshape(tensor, head_local, group_blocks, -1)
    part_of = (plane - jnp.arange(tensor, dtype=jnp.int32)) % tensor
    part_pick = (part_of[:, None] == jnp.arange(tensor, dtype=jnp.int32)[None, :]).astype(jnp.int32)
    random_home = jnp.sum(part_pick[:, :, None, None, None] * random_home[None], axis=1)
    random_home = random_home.reshape(tensor * head_local, group_blocks, -1)
    own_blocks = own_rows // BLK
    tables = attention_tables(
        lengths,
        deal,
        random_home,
        own_blocks,
        slot * own_blocks,
    )

    stream = own_tokens.astype(F32)
    stored = []
    for layer in range(LAYERS):
        attn_w, ffn_w = attn_full[layer], ffn_full[layer]
        w_query = attn_w[:, :width]
        w_keyval = attn_w[:, width : 3 * width]
        w_back_t = attn_w[:, 3 * width :]
        w_expand = ffn_w[:, : hidden * tensor]
        w_shrink_t = ffn_w[:, hidden * tensor :]
        own_inputs = stream.astype(BF)
        if layer > 0:
            (inputs,) = quad_gather([own_inputs], [4], CALL_GATHER)
        query = (dot(own_inputs, w_query).astype(BF).astype(F32) * score_scale).astype(BF)
        keyval = dot(inputs, w_keyval).astype(BF)
        if layer < LAYERS - 1:
            keyval, following = lax.optimization_barrier(
                (keyval, [w[layer + 1] for w in (w_qkv, w_out, w_up, w_down)])
            )
            attn_next, ffn_next = attn_rows(*following[:2]), ffn_rows(*following[2:])
        mixed, logs = attend_forward(query, keyval, tables)
        if layer < LAYERS - 1:
            mixed, attn_next = lax.optimization_barrier((mixed, attn_next))
            attn_full.append(over_data(attn_next))
        if layer == 0:
            mixed, own_grad = lax.optimization_barrier((mixed, out_grad))
            own_grad = lax.ppermute(own_grad, EVERY, moves)
        summed_one = stream + dot_right_t(mixed, w_back_t)
        normed = layer_norm(summed_one, attn_gain[layer], attn_shift[layer])
        ffn_in = normed.astype(BF)
        pre_act = dot(ffn_in, w_expand)
        activated = gelu_tanh(pre_act).astype(BF)
        summed_two = normed + dot_right_t(activated, w_shrink_t)
        if layer < LAYERS - 1:
            summed_two, ffn_next = lax.optimization_barrier((summed_two, ffn_next))
            ffn_full.append(over_data(ffn_next))
        stored.append(
            (own_inputs, inputs, query, keyval, mixed, logs, summed_one, ffn_in, pre_act, activated, summed_two)
        )
        stream = layer_norm(summed_two, ffn_gain[layer], ffn_shift[layer])
    layer_output = lax.ppermute(stream.astype(BF), EVERY, moves_back)

    def by_piece(rows):
        rows = rows.reshape(depth, -1, 3, WIDE).transpose(0, 2, 1, 3)
        return rows.reshape(depth, 3 * width)

    def sum_data(part):
        return lax.psum_scatter(part, DATA, scatter_dimension=0, tiled=True)

    state_grad = own_grad.astype(F32)
    attn_sums = [None] * LAYERS
    attn_grads = [None] * LAYERS
    ffn_grads = [None] * LAYERS
    norm_parts = [None] * LAYERS
    for layer in reversed(range(LAYERS)):
        (own_inputs, inputs, query, keyval, mixed, logs, summed_one, ffn_in, pre_act, activated, summed_two) = stored[layer]
        attn_w, ffn_w = attn_full[layer], ffn_full[layer]
        w_query = attn_w[:, :width]
        w_keyval = attn_w[:, width : 3 * width]
        w_back_t = attn_w[:, 3 * width :]
        w_expand = ffn_w[:, : hidden * tensor]
        w_shrink_t = ffn_w[:, hidden * tensor :]
        unused_two, ffn_back = jax.vjp(layer_norm, summed_two, ffn_gain[layer], ffn_shift[layer])
        d_two, ffn_gain_part, ffn_shift_part = ffn_back(state_grad)
        d_two_low = d_two.astype(BF)
        shrink_grad_t = dot_left_t(d_two_low, activated)
        unused_act, gelu_back = jax.vjp(gelu_tanh, pre_act)
        d_pre = gelu_back(dot(d_two_low, w_shrink_t))[0].astype(BF)
        expand_grad = dot_left_t(ffn_in, d_pre)
        d_normed = d_two + dot_right_t(d_pre, w_expand)
        unused_one, attn_back = jax.vjp(layer_norm, summed_one, attn_gain[layer], attn_shift[layer])
        d_one, attn_gain_part, attn_shift_part = attn_back(d_normed)
        norm_parts[layer] = (attn_gain_part, attn_shift_part, ffn_gain_part, ffn_shift_part)
        d_one_low = d_one.astype(BF)
        ffn_part = jnp.concatenate(
            [
                expand_grad.astype(BF),
                shrink_grad_t.astype(BF),
                dot_left_t(d_one_low, mixed).astype(BF),
            ],
            axis=1,
        )
        d_one_low, ffn_part = lax.optimization_barrier((d_one_low, ffn_part))
        ffn_sum = sum_data(ffn_part)
        d_mixed = dot(d_one_low, w_back_t).astype(BF)
        if layer < LAYERS - 1:
            d_mixed, attn_sums[layer + 1] = lax.optimization_barrier((d_mixed, attn_sums[layer + 1]))
        d_query, others, attn_part = attend_backward(
            query, keyval, logs, d_mixed, tables, own_inputs, inputs, w_keyval
        )
        if layer == 0:
            norms = jnp.stack([norm_parts[l][k] for k in range(4) for l in range(LAYERS)])
            norms, others = lax.optimization_barrier((norms, others))
            norm_sums = sum_everywhere(norms)
            norm_sums, ffn_last = lax.optimization_barrier((norm_sums, ffn_last))
            ffn_grads[1] = sum_line(ffn_last, (hidden, hidden, chunk), tensor, CALL_LINE_FFN)
            others, ffn_sum, attn_part, norm_sums, ffn_grads[1] = lax.optimization_barrier(
                (others, ffn_sum, attn_part, norm_sums, ffn_grads[1])
            )
        else:
            others, layer_output = lax.optimization_barrier((others, layer_output))
        if layer == 0:
            summed, ffn_grads[0] = quad_reduce_and_line(others, ffn_sum, (hidden, hidden, chunk), tensor)
        else:
            summed = quad_reduce(others)
            summed, ffn_sum, attn_part = lax.optimization_barrier((summed, ffn_sum, attn_part))
        ffn_last = ffn_sum
        attn_sums[layer] = sum_data(attn_part)
        state_grad = d_one + dot_right_t(d_query, w_query) + summed
    input_grad = lax.ppermute(state_grad.astype(BF), EVERY, moves_back).astype(F32)
    for layer in reversed(range(LAYERS)):
        attn_sums[layer], ffn_grads, attn_grads = lax.optimization_barrier(
            (attn_sums[layer], ffn_grads, attn_grads)
        )
        attn_grads[layer] = sum_line(by_piece(attn_sums[layer]), (chunk,) * 3, tensor, CALL_LINE_ATTN)

    qkv_grad = jnp.stack(attn_grads).reshape(LAYERS, depth, 3, head_local, HD)
    qkv_grad = qkv_grad.transpose(0, 1, 3, 2, 4).reshape(LAYERS, depth, 3 * chunk)
    ffn_own = jnp.stack(ffn_grads)
    up_grad = ffn_own[:, :, :hidden]
    down_grad = ffn_own[:, :, hidden : 2 * hidden].transpose(0, 2, 1)
    out_w_grad = ffn_own[:, :, 2 * hidden :].transpose(0, 2, 1)
    return (layer_output, input_grad, qkv_grad, out_w_grad, up_grad, down_grad) + tuple(
        norm_sums[k * LAYERS : (k + 1) * LAYERS] for k in range(4)
    )


def solution(mesh):
    devices = mesh.devices
    tensor = devices.shape[1]
    split = jax.sharding.Mesh(
        devices.reshape(devices.shape[0] // (ROW * QUAD), ROW, QUAD, tensor), EVERY
    )
    placed = (
        P(EVERY, None),
        P(None, DATA, "tensor"),
        P(None, "tensor", DATA),
        P(None, DATA, "tensor"),
        P(None, "tensor", DATA),
        P(),
        P(),
        P(),
        P(),
        P(EVERY, None),
        P(DATA, None),
        P(DATA, None),
        P(DATA, "tensor", None, None),
    )
    return jax.shard_map(
        local,
        mesh=split,
        in_specs=placed,
        out_specs=(
            P(EVERY, None),
            P(EVERY, None),
            P(None, DATA, "tensor"),
            P(None, "tensor", DATA),
            P(None, DATA, "tensor"),
            P(None, "tensor", DATA),
            P(),
            P(),
            P(),
            P(),
        ),
        check_vma=False,
    )
```

```python
import functools

import jax
import jax.numpy as jnp
from jax import lax
from jax.experimental import pallas as pl
from jax.experimental.pallas import tpu as pltpu
from jax.sharding import PartitionSpec as P

HD = 64
BLK = 64
LAYERS = 2
LONGEST = 16
QUAD = 4
WIDE = QUAD * HD
STEP = 4
STEPS = LONGEST // STEP

ROW = 2
DATA = ("hi", "row", "quad")
EVERY = DATA + ("tensor",)

NORM_EPSILON = 1e-12
MASK_VALUE = -1e30
BF = jnp.bfloat16
F32 = jnp.float32


def layer_norm(summed, norm_gain, norm_shift):
    row_mean = jnp.mean(summed, axis=-1, keepdims=True)
    centred = summed - row_mean
    row_var = jnp.mean(centred * centred, axis=-1, keepdims=True)
    return centred * lax.rsqrt(row_var + NORM_EPSILON) * norm_gain + norm_shift


def gelu_tanh(values):
    return jax.nn.gelu(values, approximate=True)


def dot(left, right):
    return jnp.dot(left, right, preferred_element_type=F32)


def dot_right_t(left, right):
    return lax.dot_general(left, right, (((1,), (1,)), ((), ())), preferred_element_type=F32)


def dot_left_t(left, right):
    return lax.dot_general(left, right, (((0,), (0,)), ((), ())), preferred_element_type=F32)


def head_diagonal(rows):
    lane_head = lax.broadcasted_iota(jnp.int32, rows.shape, 1) // HD
    return jnp.concatenate(
        [jnp.where(lane_head == h, rows, jnp.zeros_like(rows)) for h in range(QUAD)], axis=0
    )


def diagonal_rows(full):
    lane_head = lax.broadcasted_iota(jnp.int32, (HD, WIDE), 1) // HD
    out = full[:HD]
    for h in range(1, QUAD):
        out = jnp.where(lane_head == h, full[h * HD : (h + 1) * HD], out)
    return out


def key_rows(keys_at, b, count):
    return [pl.ds(pl.multiple_of(keys_at[b, i] * BLK, BLK), BLK) for i in range(count)]


def stacked(ref, places):
    return jnp.concatenate([ref[p, :] for p in places], axis=0)


def row_sums(x):
    return jnp.sum(x.reshape(x.shape[0] // 8, 8, WIDE), axis=0)


def for_steps(steps, body):
    for n in range(1, STEPS + 1):
        pl.when(steps == n)(functools.partial(body, n * STEP))


def forward_kernel(keys_at, steps_of, q_ref, k_ref, v_ref, bias_ref, out_ref, log_ref):
    def one_block(b, carry):
        rows = pl.ds(pl.multiple_of(b * BLK, BLK), BLK)

        def attend(count):
            places = key_rows(keys_at, b, count)
            query = head_diagonal(q_ref[rows, :])
            raw = dot_right_t(stacked(k_ref, places), query)
            scores, peak = [], None
            for i in range(count):
                piece = raw[i * BLK : (i + 1) * BLK] + bias_ref[b, i : i + 1, :]
                scores.append(piece)
                high = jnp.max(piece.reshape(BLK // 8, 8, WIDE), axis=0)
                peak = high if peak is None else jnp.maximum(peak, high)
            peak = jnp.max(peak, axis=0, keepdims=True)
            total, weights = None, []
            for piece in scores:
                exponent = jnp.exp(piece - peak)
                part = row_sums(exponent)
                total = part if total is None else total + part
                weights.append(exponent.astype(BF))
            total = jnp.sum(total, axis=0, keepdims=True)
            mix = dot_left_t(jnp.concatenate(weights, axis=0), stacked(v_ref, places))
            column = jnp.transpose(jnp.broadcast_to(total, (128, WIDE)))
            mix = mix / jnp.concatenate([column, column], axis=1)
            out_ref[rows, :] = diagonal_rows(mix).astype(BF)
            log_ref[b] = peak + jnp.log(total)

        for_steps(steps_of[b], attend)
        return carry

    lax.fori_loop(0, q_ref.shape[0] // BLK, one_block, 0)


def backward_kernel(
    keys_at,
    steps_of,
    q_ref,
    k_ref,
    v_ref,
    bias_ref,
    log_ref,
    d_ref,
    own_ref,
    in_ref,
    wk_ref,
    wv_ref,
    dq_ref,
    others_ref,
    grad_ref,
    dkey,
    dvalue,
    low,
    back_sum,
):
    dkey[...] = jnp.zeros_like(dkey)
    dvalue[...] = jnp.zeros_like(dvalue)

    def one_block(b, carry):
        rows = pl.ds(pl.multiple_of(b * BLK, BLK), BLK)

        def attend(count):
            places = key_rows(keys_at, b, count)
            query = head_diagonal(q_ref[rows, :])
            d_mixed = head_diagonal(d_ref[rows, :])
            logs = log_ref[b]
            keys = stacked(k_ref, places)
            raw = dot_right_t(keys, query)
            back = dot_right_t(stacked(v_ref, places), d_mixed)
            probs, inner = [], None
            for i in range(count):
                at = slice(i * BLK, (i + 1) * BLK)
                prob = jnp.exp(raw[at] + (bias_ref[b, i : i + 1, :] - logs))
                probs.append(prob)
                part = row_sums(prob * back[at])
                inner = part if inner is None else inner + part
            grad = dot(jnp.concatenate([p.astype(BF) for p in probs], axis=0), d_mixed)
            for i, p in enumerate(places):
                dvalue[p, :] += grad[i * BLK : (i + 1) * BLK]
            inner = jnp.sum(inner, axis=0, keepdims=True)
            d_score = jnp.concatenate(
                [
                    (prob * (back[i * BLK : (i + 1) * BLK] - inner)).astype(BF)
                    for i, prob in enumerate(probs)
                ],
                axis=0,
            )
            grad = dot(d_score, query)
            for i, p in enumerate(places):
                dkey[p, :] += grad[i * BLK : (i + 1) * BLK]
            d_query = dot_left_t(d_score, keys)
            dq_ref[rows, :] = (diagonal_rows(d_query) * (HD**-0.5)).astype(BF)

        for_steps(steps_of[b], attend)
        return carry

    lax.fori_loop(0, q_ref.shape[0] // BLK, one_block, 0)

    low[0] = dkey[...].astype(BF)
    low[1] = dvalue[...].astype(BF)
    grad_ref[:, :WIDE] = dot_left_t(own_ref[...], dq_ref[...]).astype(BF)
    grad_ref[:, WIDE : 2 * WIDE] = dot_left_t(in_ref[...], low[0]).astype(BF)
    grad_ref[:, 2 * WIDE :] = dot_left_t(in_ref[...], low[1]).astype(BF)
    quad = pl.program_id(0)

    def others(r, carry):
        at = pl.ds(pl.multiple_of(r * WIDE, WIDE), WIDE)
        part = dot_right_t(low[0, at, :], wk_ref[...]) + dot_right_t(low[1, at, :], wv_ref[...])
        so_far = jnp.where(quad == 0, jnp.zeros_like(part), back_sum[at, :]) + part
        back_sum[at, :] = so_far
        others_ref[at, :] = so_far.astype(BF)
        return carry

    lax.fori_loop(0, in_ref.shape[0] // WIDE, others, 0)


SHORT = pl.CostEstimate(flops=1_000_000, bytes_accessed=1_000_000, transcendentals=0)
MESH_ID = pl.DeviceIdType.MESH
CALL_GATHER_FIRST, CALL_GATHER, CALL_REDUCE, CALL_NORMS, CALL_ROWS, CALL_LINE_FFN, CALL_LINE_ATTN, CALL_BOTH = range(8)


def quad_places():
    me = lax.axis_index("quad")
    mate = me + 1 - 2 * (me % 2)
    return me, mate, (me + 2) % QUAD, (mate + 2) % QUAD


def greet(*peers):
    barrier = pltpu.get_barrier_semaphore()
    for peer in peers:
        pl.semaphore_signal(barrier, inc=1, device_id=peer, device_id_type=MESH_ID)
    pl.semaphore_wait(barrier, len(peers))


def block_at(block, size, start=0, rows=None):
    return pl.ds(pl.multiple_of(block * size + start, 16), size if rows is None else rows)


def line_peers(parts):
    plane = lax.axis_index("tensor")
    return [{"tensor": (plane + by) % parts} for by in range(1, parts)]


def lines_start(parts, groups, owns, outs, keep_sem, send_sem, recv_sem):
    peers = line_peers(parts)
    copies, kept, n = [], [], 0
    for count, out in zip(groups, outs):
        for kind in range(count):
            own = owns[n]
            width = own.shape[1]
            kept.append(
                pltpu.make_async_copy(own, out.at[:, pl.ds(kind * parts * width, width)], keep_sem.at[n])
            )
            kept[-1].start()
            for by in range(1, parts):
                copy = pltpu.make_async_remote_copy(
                    src_ref=own,
                    dst_ref=out.at[:, pl.ds((kind * parts + by) * width, width)],
                    send_sem=send_sem.at[n, by - 1],
                    recv_sem=recv_sem.at[n, by - 1],
                    device_id=peers[by - 1],
                    device_id_type=MESH_ID,
                )
                copy.start()
                copies.append(copy)
            n += 1
    return copies, kept


def lines_finish(copies, kept):
    for copy in copies + kept:
        copy.wait()


def lines_shapes(parts, groups):
    owns = [own for group in groups for own in group]
    shapes = [
        jax.ShapeDtypeStruct((group[0].shape[0], parts * len(group) * group[0].shape[1]), BF)
        for group in groups
    ]
    dma, count = pltpu.SemaphoreType.DMA, max(len(owns), 1)
    return owns, shapes, [dma((count,)), dma((count, parts - 1)), dma((count, parts - 1))]


def gather_kernel(pieces, parts_along, groups, *refs):
    count, lines = len(pieces), sum(groups)
    at = [count, count + lines, 2 * count + lines, 2 * count + lines + len(groups)]
    owns, line_owns = refs[: at[0]], refs[at[0] : at[1]]
    outs, line_outs = refs[at[1] : at[2]], refs[at[2] : at[3]]
    keep_sem, mate_send, mate_recv, far_send, far_recv, on_send, on_recv = refs[at[3] : at[3] + 7]
    me, mate, far, cross = quad_places()
    greet({"quad": mate}, {"quad": far}, *(line_peers(parts_along) if groups else []))

    def send(source, target, sends, recvs, at, peer):
        return pltpu.make_async_remote_copy(
            src_ref=source,
            dst_ref=target,
            send_sem=sends.at[at],
            recv_sem=recvs.at[at],
            device_id={"quad": peer},
            device_id_type=MESH_ID,
        )

    parts = []
    for n in range(count):
        size = owns[n].shape[0]
        step = size // pieces[n]
        for p in range(pieces[n]):
            parts.append((n, size, p * step, step))
    to_far = [
        send(owns[n].at[pl.ds(start, step)], outs[n].at[block_at(me, size, start, step)], far_send, far_recv, i, far)
        for i, (n, size, start, step) in enumerate(parts)
    ]
    for copy in to_far:
        copy.start()
    to_mate = [
        send(owns[n], outs[n].at[block_at(me, owns[n].shape[0])], mate_send, mate_recv, n, mate)
        for n in range(count)
    ]
    for copy in to_mate:
        copy.start()
    along = lines_start(parts_along, groups, line_owns, line_outs, *refs[at[3] + 7 :])
    kept = [
        pltpu.make_async_copy(owns[n], outs[n].at[block_at(me, owns[n].shape[0])], keep_sem.at[n])
        for n in range(count)
    ]
    for copy in kept:
        copy.start()
    onward = []
    for i, (n, size, start, step) in enumerate(parts):
        to_far[i].wait_recv()
        came = outs[n].at[block_at(far, size, start, step)]
        copy = send(came, came, on_send, on_recv, i, mate)
        copy.start()
        onward.append(copy)
    for copy in to_mate + onward:
        copy.wait()
    for copy in to_far:
        copy.wait_send()
    for copy in kept:
        copy.wait()
    lines_finish(*along)


def quad_gather(arrays, pieces, call, parts=1, groups=()):
    count, total = len(arrays), sum(pieces)
    sems = [pltpu.SemaphoreType.DMA((k,)) for k in (count, count, count, total, total, total, total)]
    owns, shapes, line_sems = lines_shapes(max(parts, 2), groups)
    return pl.pallas_call(
        functools.partial(gather_kernel, pieces, parts, tuple(len(g) for g in groups)),
        out_shape=[jax.ShapeDtypeStruct((QUAD * x.shape[0],) + x.shape[1:], x.dtype) for x in arrays]
        + shapes,
        in_specs=[pl.BlockSpec(memory_space=pltpu.VMEM)] * (count + len(owns)),
        out_specs=[pl.BlockSpec(memory_space=pl.ANY)] * (count + len(shapes)),
        scratch_shapes=sems + line_sems,
        compiler_params=pltpu.CompilerParams(collective_id=call, has_side_effects=True),
        cost_estimate=SHORT,
        name="quad_gather",
    )(*arrays, *owns)


REDUCE_PIECES = 4


def reduce_kernel(
    parts_ref,
    out_ref,
    near,
    relay,
    beyond,
    mate_send,
    mate_recv,
    own_send,
    own_recv,
    far_send,
    far_recv,
    greeted=False,
):
    me, mate, far, cross = quad_places()
    if not greeted:
        greet({"quad": mate}, {"quad": far})
    size = out_ref.shape[0]
    step = size // REDUCE_PIECES

    def send(source, target, send_sem, recv_sem, peer):
        copy = pltpu.make_async_remote_copy(
            src_ref=source,
            dst_ref=target,
            send_sem=send_sem,
            recv_sem=recv_sem,
            device_id={"quad": peer},
            device_id_type=MESH_ID,
        )
        copy.start()
        return copy

    to_mate = [
        send(
            parts_ref.at[block_at(cross, size, p * step, step)],
            near.at[1, pl.ds(p * step, step)],
            mate_send.at[p],
            mate_recv.at[p],
            mate,
        )
        for p in range(REDUCE_PIECES)
    ]
    own = send(parts_ref.at[block_at(mate, size)], near.at[0], own_send, own_recv, mate)
    to_far = []
    for p in range(REDUCE_PIECES):
        rows = pl.ds(p * step, step)
        to_mate[p].wait_recv()
        mine = parts_ref[block_at(far, size, p * step, step), :].astype(F32)
        relay[rows, :] = (mine + near[1, rows, :].astype(F32)).astype(BF)
        to_far.append(send(relay.at[rows], beyond.at[rows], far_send.at[p], far_recv.at[p], far))
    own.wait_recv()
    for p in range(REDUCE_PIECES):
        rows = pl.ds(p * step, step)
        to_far[p].wait_recv()
        mine = parts_ref[block_at(me, size, p * step, step), :].astype(F32)
        out_ref[rows, :] = mine + near[0, rows, :].astype(F32) + beyond[rows, :].astype(F32)
    for copy in to_mate + [own] + to_far:
        copy.wait_send()


def reduce_scratch(rows, width):
    one, each = pltpu.SemaphoreType.DMA, pltpu.SemaphoreType.DMA((REDUCE_PIECES,))
    low = pltpu.VMEM((rows, width), BF)
    return [pltpu.VMEM((2, rows, width), BF), low, low, each, each, one, one, each, each]


def quad_reduce(parts):
    rows, width = parts.shape[0] // QUAD, parts.shape[1]
    return pl.pallas_call(
        reduce_kernel,
        out_shape=jax.ShapeDtypeStruct((rows, width), F32),
        in_specs=[pl.BlockSpec(memory_space=pltpu.VMEM)],
        out_specs=pl.BlockSpec(memory_space=pltpu.VMEM),
        scratch_shapes=reduce_scratch(rows, width),
        compiler_params=pltpu.CompilerParams(collective_id=CALL_REDUCE, has_side_effects=True),
        cost_estimate=SHORT,
        name="quad_reduce",
    )(parts)


def both_kernel(sizes, planes, parts_ref, x_ref, out_ref, line_ref, *scratch):
    me, mate, far, cross = quad_places()
    greet({"quad": mate}, {"quad": far}, *line_peers(planes))
    held, came, send_sem, recv_sem = scratch[:4]
    copies = line_start(sizes, planes, x_ref, held, came, send_sem, recv_sem)
    reduce_kernel(parts_ref, out_ref, *scratch[4:], greeted=True)
    line_finish(sizes, planes, x_ref, line_ref, came, copies)


def quad_reduce_and_line(parts, lines, sizes, planes):
    rows, width = parts.shape[0] // QUAD, parts.shape[1]
    shape = (lines.shape[0], sum(sizes))
    vmem = pl.BlockSpec(memory_space=pltpu.VMEM)
    return pl.pallas_call(
        functools.partial(both_kernel, sizes, planes),
        out_shape=[jax.ShapeDtypeStruct((rows, width), F32), jax.ShapeDtypeStruct(shape, F32)],
        in_specs=[vmem, vmem],
        out_specs=[vmem, vmem],
        scratch_shapes=line_scratch(shape, planes) + reduce_scratch(rows, width),
        compiler_params=pltpu.CompilerParams(collective_id=CALL_BOTH, has_side_effects=True),
        cost_estimate=SHORT,
        name="quad_reduce_and_line",
    )(parts, lines)


def norms_kernel(hops, x_ref, out_ref, held, came, send_sem, recv_sem):
    peers = []
    for axis, bit in hops:
        at = lax.axis_index(axis)
        peers.append({axis: at + bit - 2 * bit * ((at // bit) % 2)})
    greet(*peers)
    for n, peer in enumerate(peers):
        source = x_ref if n == 0 else held.at[n]
        copy = pltpu.make_async_remote_copy(
            src_ref=source,
            dst_ref=came.at[n],
            send_sem=send_sem.at[n],
            recv_sem=recv_sem.at[n],
            device_id=peer,
            device_id_type=MESH_ID,
        )
        copy.start()
        copy.wait()
        total = source[...] + came[n]
        if n == len(peers) - 1:
            out_ref[...] = total
        else:
            held[n + 1] = total


def sum_everywhere(x):
    hops = []
    for axis in ("quad", "row", "tensor", "hi"):
        bit = 1
        while bit < lax.axis_size(axis):
            hops.append((axis, bit))
            bit *= 2
    vmem = pltpu.VMEM((len(hops),) + x.shape, x.dtype)
    return pl.pallas_call(
        functools.partial(norms_kernel, tuple(hops)),
        out_shape=jax.ShapeDtypeStruct(x.shape, x.dtype),
        in_specs=[pl.BlockSpec(memory_space=pltpu.VMEM)],
        out_specs=pl.BlockSpec(memory_space=pltpu.VMEM),
        scratch_shapes=[
            vmem,
            vmem,
            pltpu.SemaphoreType.DMA((len(hops),)),
            pltpu.SemaphoreType.DMA((len(hops),)),
        ],
        compiler_params=pltpu.CompilerParams(collective_id=CALL_NORMS, has_side_effects=True),
        cost_estimate=SHORT,
        name="sum_everywhere",
    )(x)


def rows_kernel(parts, groups, own_ref, *refs):
    lines = sum(groups)
    line_owns, out_ref, line_outs = refs[:lines], refs[lines], refs[lines + 1 : lines + 1 + len(groups)]
    keep_sem, line_send, line_recv, send_sem, recv_sem = refs[lines + 1 + len(groups) :][:5]
    line_sems = refs[lines + 1 + len(groups) :][5:]
    me, mate, far, cross = quad_places()
    row, plane = lax.axis_index("row"), lax.axis_index("tensor")
    other = 1 - row
    line = [{"tensor": (plane + by) % parts} for by in range(1, parts)]
    to_x, to_y, to_mate = {"quad": far}, {"row": other}, {"quad": mate}
    greet(*line, to_x, to_y, to_mate)
    size, width = own_ref.shape

    def block(at_row, at_quad, part):
        return out_ref.at[block_at(at_row * QUAD + at_quad, size), pl.ds(part * width, width)]

    used = []

    def send(source, target, peer, n):
        copy = pltpu.make_async_remote_copy(
            src_ref=source,
            dst_ref=target,
            send_sem=send_sem.at[n],
            recv_sem=recv_sem.at[n],
            device_id=peer,
            device_id_type=MESH_ID,
        )
        copy.start()
        used.append(copy)
        return copy

    along = []
    for by in range(1, parts):
        copy = pltpu.make_async_remote_copy(
            src_ref=own_ref,
            dst_ref=block(row, me, by),
            send_sem=line_send.at[by - 1],
            recv_sem=line_recv.at[by - 1],
            device_id=line[by - 1],
            device_id_type=MESH_ID,
        )
        copy.start()
        along.append(copy)
    keep = pltpu.make_async_copy(own_ref, block(row, me, 0), keep_sem)
    keep.start()
    only_line = lines_start(parts, groups, line_owns, line_outs, *line_sems)
    near_x, near_y, beyond, mates = [], [], [], []
    for part in range(parts + 1):
        if part < parts:
            if part:
                along[part - 1].wait_recv()
            source = own_ref if part == 0 else block(row, me, part)
            target = block(row, me, part)
            near_x.append(send(source, target, to_x, part))
            near_y.append(send(source, target, to_y, parts + part))
            mates.append(send(source, target, to_mate, 2 * parts + part))
        if part:
            done = part - 1
            from_x, from_y = block(row, far, done), block(other, me, done)
            near_x[done].wait_recv()
            near_y[done].wait_recv()
            if done % 2:
                beyond.append(send(from_y, from_y, to_x, 3 * parts + done))
            else:
                beyond.append(send(from_x, from_x, to_y, 3 * parts + done))
            mates.append(send(from_x, from_x, to_mate, 4 * parts + done))
            mates.append(send(from_y, from_y, to_mate, 5 * parts + done))
    for part in range(parts):
        beyond[part].wait_recv()
        came = block(other, far, part)
        mates.append(send(came, came, to_mate, 6 * parts + part))
    for copy in mates:
        copy.wait_recv()
    for copy in along + used:
        copy.wait_send()
    keep.wait()
    lines_finish(*only_line)


def gather_rows(rows, parts, groups):
    size, width = rows.shape
    dma = pltpu.SemaphoreType.DMA
    owns, shapes, line_sems = lines_shapes(parts, groups)
    return pl.pallas_call(
        functools.partial(rows_kernel, parts, tuple(len(g) for g in groups)),
        out_shape=[jax.ShapeDtypeStruct((ROW * QUAD * size, parts * width), rows.dtype)] + shapes,
        in_specs=[pl.BlockSpec(memory_space=pltpu.VMEM)] * (1 + len(owns)),
        out_specs=[pl.BlockSpec(memory_space=pl.ANY)] * (1 + len(shapes)),
        scratch_shapes=[dma, dma((parts - 1,)), dma((parts - 1,)), dma((7 * parts,)), dma((7 * parts,))]
        + line_sems,
        compiler_params=pltpu.CompilerParams(collective_id=CALL_ROWS, has_side_effects=True),
        cost_estimate=SHORT,
        name="gather_rows",
    )(rows, *owns)


def regroup_kernel(parts, kinds, x_ref, out_ref):
    size = x_ref.shape[1] // (parts * kinds)
    for kind in range(kinds):
        for part in range(parts):
            to, at = (kind * parts + part) * size, (part * kinds + kind) * size
            out_ref[:, to : to + size] = x_ref[:, at : at + size]


def regroup(rows, parts, kinds):
    steps = max(rows.shape[0] // 192, 1)
    block = pl.BlockSpec((rows.shape[0] // steps, rows.shape[1]), lambda i: (i, 0))
    return pl.pallas_call(
        functools.partial(regroup_kernel, parts, kinds),
        out_shape=jax.ShapeDtypeStruct(rows.shape, rows.dtype),
        grid=(steps,),
        in_specs=[block],
        out_specs=block,
        cost_estimate=SHORT,
        name="regroup",
    )(rows)


def line_pick(sizes, parts, x_ref, part):
    columns, start = [], 0
    for size in sizes:
        columns.append(x_ref[:, start + part * size : start + (part + 1) * size])
        start += parts * size
    return jnp.concatenate(columns, axis=1)


def line_start(sizes, parts, x_ref, held, came, send_sem, recv_sem):
    plane = lax.axis_index("tensor")
    copies = []
    for by in range(1, parts):
        held[by - 1] = line_pick(sizes, parts, x_ref, by)
        copy = pltpu.make_async_remote_copy(
            src_ref=held.at[by - 1],
            dst_ref=came.at[by - 1],
            send_sem=send_sem.at[by - 1],
            recv_sem=recv_sem.at[by - 1],
            device_id={"tensor": (plane + parts - by) % parts},
            device_id_type=MESH_ID,
        )
        copy.start()
        copies.append(copy)
    return copies


def line_finish(sizes, parts, x_ref, out_ref, came, copies):
    total = line_pick(sizes, parts, x_ref, 0).astype(F32)
    for by in range(1, parts):
        copies[by - 1].wait_recv()
        total = total + came[by - 1].astype(F32)
    out_ref[...] = total
    for copy in copies:
        copy.wait_send()


def line_scratch(shape, parts):
    dma = pltpu.SemaphoreType.DMA((parts - 1,))
    return [pltpu.VMEM((parts - 1,) + shape, BF), pltpu.VMEM((parts - 1,) + shape, BF), dma, dma]


def parts_kernel(sizes, parts, x_ref, out_ref, held, came, send_sem, recv_sem):
    greet(*line_peers(parts))
    copies = line_start(sizes, parts, x_ref, held, came, send_sem, recv_sem)
    line_finish(sizes, parts, x_ref, out_ref, came, copies)


def sum_line(rows, sizes, parts, call):
    shape = (rows.shape[0], sum(sizes))
    return pl.pallas_call(
        functools.partial(parts_kernel, sizes, parts),
        out_shape=jax.ShapeDtypeStruct(shape, F32),
        in_specs=[pl.BlockSpec(memory_space=pltpu.VMEM)],
        out_specs=pl.BlockSpec(memory_space=pltpu.VMEM),
        scratch_shapes=line_scratch(shape, parts),
        compiler_params=pltpu.CompilerParams(collective_id=call, has_side_effects=True),
        cost_estimate=SHORT,
        name="sum_line",
    )(rows)


def attend_forward(query, keyval, tables):
    keys_at, steps_of, bias = tables
    own, width = query.shape
    quads = width // WIDE
    rows = keyval.shape[0]
    blocks = own // BLK
    return pl.pallas_call(
        forward_kernel,
        grid_spec=pltpu.PrefetchScalarGridSpec(
            num_scalar_prefetch=2,
            grid=(quads,),
            in_specs=[
                pl.BlockSpec((own, WIDE), lambda i, *_: (0, i)),
                pl.BlockSpec((rows, WIDE), lambda i, *_: (0, i)),
                pl.BlockSpec((rows, WIDE), lambda i, *_: (0, i + quads)),
                pl.BlockSpec((blocks, LONGEST, WIDE), lambda i, *_: (0, 0, i)),
            ],
            out_specs=[
                pl.BlockSpec((own, WIDE), lambda i, *_: (0, i)),
                pl.BlockSpec((blocks, 1, WIDE), lambda i, *_: (0, 0, i)),
            ],
        ),
        out_shape=[
            jax.ShapeDtypeStruct((own, width), BF),
            jax.ShapeDtypeStruct((blocks, 1, width), F32),
        ],
        cost_estimate=SHORT,
        name="attend_forward",
    )(keys_at, steps_of, query, keyval, keyval, bias)


def attend_backward(query, keyval, logs, d_mixed, tables, own_inputs, inputs, w_keyval):
    keys_at, steps_of, bias = tables
    own, width = query.shape
    quads = width // WIDE
    rows, depth = inputs.shape
    blocks = own // BLK
    once = pl.Buffered(1)
    return pl.pallas_call(
        backward_kernel,
        grid_spec=pltpu.PrefetchScalarGridSpec(
            num_scalar_prefetch=2,
            grid=(quads,),
            in_specs=[
                pl.BlockSpec((own, WIDE), lambda i, *_: (0, i)),
                pl.BlockSpec((rows, WIDE), lambda i, *_: (0, i)),
                pl.BlockSpec((rows, WIDE), lambda i, *_: (0, i + quads)),
                pl.BlockSpec((blocks, LONGEST, WIDE), lambda i, *_: (0, 0, i)),
                pl.BlockSpec((blocks, 1, WIDE), lambda i, *_: (0, 0, i)),
                pl.BlockSpec((own, WIDE), lambda i, *_: (0, i)),
                pl.BlockSpec((own, depth), lambda i, *_: (0, 0), pipeline_mode=once),
                pl.BlockSpec((rows, depth), lambda i, *_: (0, 0), pipeline_mode=once),
                pl.BlockSpec((depth, WIDE), lambda i, *_: (0, i)),
                pl.BlockSpec((depth, WIDE), lambda i, *_: (0, i + quads)),
            ],
            out_specs=[
                pl.BlockSpec((own, WIDE), lambda i, *_: (0, i)),
                pl.BlockSpec((rows, depth), lambda i, *_: (0, 0)),
                pl.BlockSpec((depth, 3 * WIDE), lambda i, *_: (0, i)),
            ],
            scratch_shapes=[
                pltpu.VMEM((rows, WIDE), F32),
                pltpu.VMEM((rows, WIDE), F32),
                pltpu.VMEM((2, rows, WIDE), BF),
                pltpu.VMEM((rows, depth), F32),
            ],
        ),
        out_shape=[
            jax.ShapeDtypeStruct((own, width), BF),
            jax.ShapeDtypeStruct((rows, depth), BF),
            jax.ShapeDtypeStruct((depth, 3 * width), BF),
        ],
        cost_estimate=SHORT,
        name="attend_backward",
    )(keys_at, steps_of, query, keyval, keyval, bias, logs, d_mixed, own_inputs, inputs, w_keyval, w_keyval)


def attention_tables(doc_lengths, block_deal, random_rows, own_blocks, first_own):
    blocks = block_deal.shape[0]
    doc_ends = jnp.cumsum(doc_lengths)
    doc_starts = doc_ends - doc_lengths
    place = jnp.arange(blocks, dtype=jnp.int32)
    stored_at = jnp.sum(
        jnp.where(block_deal[None, :] == place[:, None], place[None, :], 0), axis=1
    )
    own = lax.dynamic_slice(block_deal, (first_own,), (own_blocks,))
    doc_index = jnp.sum((own[:, None] >= doc_ends[None, :]).astype(jnp.int32), axis=1)
    doc_pick = (
        doc_index[:, None] == jnp.arange(doc_lengths.shape[0], dtype=jnp.int32)[None, :]
    ).astype(jnp.int32)
    first_block = jnp.sum(doc_pick * doc_starts[None, :], axis=1)
    doc_blocks = jnp.sum(doc_pick * doc_lengths[None, :], axis=1)
    local = own - first_block
    other = jnp.arange(LONGEST, dtype=jnp.int32)
    wanted = jnp.minimum(first_block[:, None] + other[None, :], blocks - 1)
    keys_at = jnp.sum(
        jnp.where(wanted[:, :, None] == place[None, None, :], stored_at[None, None, :], 0), axis=2
    )
    own_pick = (own[:, None] == place[None, :]).astype(jnp.int32)
    picks = jnp.sum(own_pick[None, :, :, None] * random_rows[:, None, :, :], axis=2)
    picks = jnp.remainder(picks, doc_blocks[None, :, None])
    random_hit = jnp.any(picks[:, :, :, None] == other[None, None, None, :], axis=2)
    inside = other[None, :] < doc_blocks[:, None]
    near = jnp.abs(local[:, None] - other[None, :]) <= 1
    everywhere = (local[:, None] < 2) | (other[None, :] < 2)
    allowed = inside[None] & ((near | everywhere)[None] | random_hit)
    bias = jnp.where(allowed, 0.0, MASK_VALUE).astype(F32)
    bias = jnp.repeat(bias.transpose(1, 2, 0), BLK, axis=2)
    steps_of = (doc_blocks + STEP - 1) // STEP
    return keys_at, steps_of, bias


def to_home(steps, parts):
    pairs = []
    for hi in range(steps):
        for row in range(ROW):
            for quad in range(QUAD):
                side, core = quad // 2, quad % 2
                plane = parts - 1 - side if core else side
                for part in range(parts):
                    source = ((hi * ROW + row) * QUAD + quad) * parts + part
                    target = ((hi * ROW + row) * QUAD + part) * parts + plane
                    pairs.append((source, target))
    return pairs


def local(
    layer_input,
    w_qkv,
    w_out,
    w_up,
    w_down,
    attn_gain,
    attn_shift,
    ffn_gain,
    ffn_shift,
    out_grad,
    doc_lengths,
    block_deal,
    random_blocks,
):
    own_rows, width = layer_input.shape
    tensor = lax.axis_size("tensor")
    slot = lax.axis_index("quad")
    plane = lax.axis_index("tensor")
    head_local = random_blocks.shape[1]
    chunk = head_local * HD
    depth = w_qkv.shape[1]
    hidden = w_up.shape[2]
    score_scale = HD ** (-0.5)
    moves = to_home(lax.axis_size("hi"), tensor)
    moves_back = [(b, a) for a, b in moves]

    def shifted(x, by):
        return lax.ppermute(x, "tensor", [(i, (i + by) % tensor) for i in range(tensor)])

    def spread(shard):
        return [shard] + [shifted(shard, by) for by in range(1, tensor)]

    def by_kind(parts, kinds):
        rows = jnp.stack([part.reshape(depth, kinds, -1) for part in parts], axis=2)
        return rows.reshape(depth, -1)

    def attn_shard(qkv, back):
        qkv = qkv.reshape(depth, head_local, 3, HD).transpose(0, 2, 1, 3)
        return jnp.concatenate([qkv.reshape(depth, 3 * chunk), back.T], axis=1)

    def over_data(rows):
        return lax.all_gather(rows, DATA, axis=0, tiled=True)

    docs, group_blocks = doc_lengths.shape[1], block_deal.shape[1]
    numbers = jnp.concatenate([doc_lengths[0], block_deal[0], random_blocks[0].reshape(-1)])
    numbers = jnp.stack([numbers // BLK, numbers % BLK]).astype(BF)
    numbers = jnp.pad(numbers, ((0, 14), (0, width - numbers.shape[1])))
    own_numbers = lax.ppermute(numbers, EVERY, moves)
    own_tokens = lax.ppermute(layer_input, EVERY, moves)
    ffn_shards = [w_up[0], w_down[0].T]
    if lax.axis_size("hi") == 1:
        rows, first_rows = gather_rows(attn_shard(w_qkv[0], w_out[0]), tensor, [ffn_shards])
        rows, first_rows, own_tokens, own_numbers = lax.optimization_barrier(
            (rows, first_rows, own_tokens, own_numbers)
        )
        attn_full = [regroup(rows, tensor, 4)]
    else:
        attn_full = [over_data(by_kind(spread(attn_shard(w_qkv[0], w_out[0])), 4))]
        first_rows = by_kind(spread(jnp.concatenate(ffn_shards, axis=1)), 2)
    ffn_full = [over_data(first_rows)]

    groups = []
    for layer in range(1, LAYERS):
        groups += [[attn_shard(w_qkv[layer], w_out[layer])], [w_up[layer], w_down[layer].T]]
    inputs, numbers, *later = quad_gather(
        [own_tokens, own_numbers], [4, 1], CALL_GATHER_FIRST, tensor, groups
    )
    numbers = numbers.reshape(QUAD, 16, width)[:, :2].astype(jnp.int32)
    numbers = numbers[:, 0] * BLK + numbers[:, 1]
    lengths, deal = numbers[0, :docs], numbers[0, docs : docs + group_blocks]
    random_home = numbers[:, docs + group_blocks :][:, : random_blocks.size]
    random_home = random_home.reshape(tensor, head_local, group_blocks, -1)
    part_of = (plane - jnp.arange(tensor, dtype=jnp.int32)) % tensor
    part_pick = (part_of[:, None] == jnp.arange(tensor, dtype=jnp.int32)[None, :]).astype(jnp.int32)
    random_home = jnp.sum(part_pick[:, :, None, None, None] * random_home[None], axis=1)
    random_home = random_home.reshape(tensor * head_local, group_blocks, -1)
    own_blocks = own_rows // BLK
    tables = attention_tables(
        lengths,
        deal,
        random_home,
        own_blocks,
        slot * own_blocks,
    )

    stream = own_tokens.astype(F32)
    stored = []
    for layer in range(LAYERS):
        attn_w, ffn_w = attn_full[layer], ffn_full[layer]
        w_query = attn_w[:, :width]
        w_keyval = attn_w[:, width : 3 * width]
        w_back_t = attn_w[:, 3 * width :]
        w_expand = ffn_w[:, : hidden * tensor]
        w_shrink_t = ffn_w[:, hidden * tensor :]
        own_inputs = stream.astype(BF)
        if layer > 0:
            (inputs,) = quad_gather([own_inputs], [4], CALL_GATHER)
        query = (dot(own_inputs, w_query).astype(BF).astype(F32) * score_scale).astype(BF)
        keyval = dot(inputs, w_keyval).astype(BF)
        if layer < LAYERS - 1:
            attn_full.append(over_data(regroup(later[2 * layer], tensor, 4)))
            ffn_full.append(over_data(later[2 * layer + 1]))
        mixed, logs = attend_forward(query, keyval, tables)
        if layer == 0:
            mixed, own_grad = lax.optimization_barrier((mixed, out_grad))
            own_grad = lax.ppermute(own_grad, EVERY, moves)
        summed_one = stream + dot_right_t(mixed, w_back_t)
        normed = layer_norm(summed_one, attn_gain[layer], attn_shift[layer])
        ffn_in = normed.astype(BF)
        pre_act = dot(ffn_in, w_expand)
        activated = gelu_tanh(pre_act).astype(BF)
        summed_two = normed + dot_right_t(activated, w_shrink_t)
        stored.append(
            (own_inputs, inputs, query, keyval, mixed, logs, summed_one, ffn_in, pre_act, activated, summed_two)
        )
        stream = layer_norm(summed_two, ffn_gain[layer], ffn_shift[layer])
    layer_output = lax.ppermute(stream.astype(BF), EVERY, moves_back)

    def by_piece(rows):
        rows = rows.reshape(depth, -1, 3, WIDE).transpose(0, 2, 1, 3)
        return rows.reshape(depth, 3 * width)

    def sum_data(part):
        return lax.psum_scatter(part, DATA, scatter_dimension=0, tiled=True)

    state_grad = own_grad.astype(F32)
    attn_sums = [None] * LAYERS
    attn_grads = [None] * LAYERS
    ffn_grads = [None] * LAYERS
    norm_parts = [None] * LAYERS
    for layer in reversed(range(LAYERS)):
        (own_inputs, inputs, query, keyval, mixed, logs, summed_one, ffn_in, pre_act, activated, summed_two) = stored[layer]
        attn_w, ffn_w = attn_full[layer], ffn_full[layer]
        w_query = attn_w[:, :width]
        w_keyval = attn_w[:, width : 3 * width]
        w_back_t = attn_w[:, 3 * width :]
        w_expand = ffn_w[:, : hidden * tensor]
        w_shrink_t = ffn_w[:, hidden * tensor :]
        unused_two, ffn_back = jax.vjp(layer_norm, summed_two, ffn_gain[layer], ffn_shift[layer])
        d_two, ffn_gain_part, ffn_shift_part = ffn_back(state_grad)
        d_two_low = d_two.astype(BF)
        shrink_grad_t = dot_left_t(d_two_low, activated)
        unused_act, gelu_back = jax.vjp(gelu_tanh, pre_act)
        d_pre = gelu_back(dot(d_two_low, w_shrink_t))[0].astype(BF)
        expand_grad = dot_left_t(ffn_in, d_pre)
        d_normed = d_two + dot_right_t(d_pre, w_expand)
        unused_one, attn_back = jax.vjp(layer_norm, summed_one, attn_gain[layer], attn_shift[layer])
        d_one, attn_gain_part, attn_shift_part = attn_back(d_normed)
        norm_parts[layer] = (attn_gain_part, attn_shift_part, ffn_gain_part, ffn_shift_part)
        d_one_low = d_one.astype(BF)
        ffn_part = jnp.concatenate(
            [
                expand_grad.astype(BF),
                shrink_grad_t.astype(BF),
                dot_left_t(d_one_low, mixed).astype(BF),
            ],
            axis=1,
        )
        d_one_low, ffn_part = lax.optimization_barrier((d_one_low, ffn_part))
        ffn_sum = sum_data(ffn_part)
        d_mixed = dot(d_one_low, w_back_t).astype(BF)
        if layer < LAYERS - 1:
            d_mixed, attn_sums[layer + 1] = lax.optimization_barrier((d_mixed, attn_sums[layer + 1]))
        d_query, others, attn_part = attend_backward(
            query, keyval, logs, d_mixed, tables, own_inputs, inputs, w_keyval
        )
        if layer == 0:
            others, ffn_last = lax.optimization_barrier((others, ffn_last))
            ffn_grads[1] = sum_line(ffn_last, (hidden, hidden, chunk), tensor, CALL_LINE_FFN)
            attn_sums[1], ffn_grads[1] = lax.optimization_barrier((attn_sums[1], ffn_grads[1]))
            attn_grads[1] = sum_line(by_piece(attn_sums[1]), (chunk,) * 3, tensor, CALL_LINE_ATTN)
            others, ffn_sum, attn_part, ffn_grads[1], attn_grads[1] = lax.optimization_barrier(
                (others, ffn_sum, attn_part, ffn_grads[1], attn_grads[1])
            )
        else:
            others, layer_output = lax.optimization_barrier((others, layer_output))
        if layer == 0:
            summed, ffn_grads[0] = quad_reduce_and_line(others, ffn_sum, (hidden, hidden, chunk), tensor)
        else:
            summed = quad_reduce(others)
            summed, ffn_sum, attn_part = lax.optimization_barrier((summed, ffn_sum, attn_part))
        ffn_last = ffn_sum
        attn_sums[layer] = sum_data(attn_part)
        state_grad = d_one + dot_right_t(d_query, w_query) + summed
    input_grad = lax.ppermute(state_grad.astype(BF), EVERY, moves_back).astype(F32)
    norms = jnp.stack([norm_parts[l][k] for k in range(4) for l in range(LAYERS)])
    norms, state_grad = lax.optimization_barrier((norms, state_grad))
    norm_sums = sum_everywhere(norms)
    attn_sums[0], norm_sums = lax.optimization_barrier((attn_sums[0], norm_sums))
    attn_grads[0] = sum_line(by_piece(attn_sums[0]), (chunk,) * 3, tensor, CALL_LINE_ATTN)

    qkv_grad = jnp.stack(attn_grads).reshape(LAYERS, depth, 3, head_local, HD)
    qkv_grad = qkv_grad.transpose(0, 1, 3, 2, 4).reshape(LAYERS, depth, 3 * chunk)
    ffn_own = jnp.stack(ffn_grads)
    up_grad = ffn_own[:, :, :hidden]
    down_grad = ffn_own[:, :, hidden : 2 * hidden].transpose(0, 2, 1)
    out_w_grad = ffn_own[:, :, 2 * hidden :].transpose(0, 2, 1)
    return (layer_output, input_grad, qkv_grad, out_w_grad, up_grad, down_grad) + tuple(
        norm_sums[k * LAYERS : (k + 1) * LAYERS] for k in range(4)
    )


def solution(mesh):
    devices = mesh.devices
    tensor = devices.shape[1]
    split = jax.sharding.Mesh(
        devices.reshape(devices.shape[0] // (ROW * QUAD), ROW, QUAD, tensor), EVERY
    )
    placed = (
        P(EVERY, None),
        P(None, DATA, "tensor"),
        P(None, "tensor", DATA),
        P(None, DATA, "tensor"),
        P(None, "tensor", DATA),
        P(),
        P(),
        P(),
        P(),
        P(EVERY, None),
        P(DATA, None),
        P(DATA, None),
        P(DATA, "tensor", None, None),
    )
    return jax.shard_map(
        local,
        mesh=split,
        in_specs=placed,
        out_specs=(
            P(EVERY, None),
            P(EVERY, None),
            P(None, DATA, "tensor"),
            P(None, "tensor", DATA),
            P(None, DATA, "tensor"),
            P(None, "tensor", DATA),
            P(),
            P(),
            P(),
            P(),
        ),
        check_vma=False,
    )
```

```python
import functools

import jax
import jax.numpy as jnp
from jax import lax
from jax.experimental import pallas as pl
from jax.experimental.pallas import tpu as pltpu
from jax.sharding import PartitionSpec as P

HD = 64
BLK = 64
LAYERS = 2
LONGEST = 16
QUAD = 4
WIDE = QUAD * HD
STEP = 4
STEPS = LONGEST // STEP

ROW = 2
DATA = ("hi", "row", "quad")
EVERY = DATA + ("tensor",)

NORM_EPSILON = 1e-12
MASK_VALUE = -1e30
BF = jnp.bfloat16
F32 = jnp.float32


def layer_norm(summed, norm_gain, norm_shift):
    row_mean = jnp.mean(summed, axis=-1, keepdims=True)
    centred = summed - row_mean
    row_var = jnp.mean(centred * centred, axis=-1, keepdims=True)
    return centred * lax.rsqrt(row_var + NORM_EPSILON) * norm_gain + norm_shift


def gelu_tanh(values):
    return jax.nn.gelu(values, approximate=True)


def dot(left, right):
    return jnp.dot(left, right, preferred_element_type=F32)


def dot_right_t(left, right):
    return lax.dot_general(left, right, (((1,), (1,)), ((), ())), preferred_element_type=F32)


def dot_left_t(left, right):
    return lax.dot_general(left, right, (((0,), (0,)), ((), ())), preferred_element_type=F32)


def head_diagonal(rows):
    lane_head = lax.broadcasted_iota(jnp.int32, rows.shape, 1) // HD
    return jnp.concatenate(
        [jnp.where(lane_head == h, rows, jnp.zeros_like(rows)) for h in range(QUAD)], axis=0
    )


def diagonal_rows(full):
    lane_head = lax.broadcasted_iota(jnp.int32, (HD, WIDE), 1) // HD
    out = full[:HD]
    for h in range(1, QUAD):
        out = jnp.where(lane_head == h, full[h * HD : (h + 1) * HD], out)
    return out


def key_rows(keys_at, b, count):
    return [pl.ds(pl.multiple_of(keys_at[b, i] * BLK, BLK), BLK) for i in range(count)]


def stacked(ref, places):
    return jnp.concatenate([ref[p, :] for p in places], axis=0)


def row_sums(x):
    return jnp.sum(x.reshape(x.shape[0] // 8, 8, WIDE), axis=0)


def for_steps(steps, body):
    for n in range(1, STEPS + 1):
        pl.when(steps == n)(functools.partial(body, n * STEP))


def forward_kernel(keys_at, steps_of, q_ref, k_ref, v_ref, bias_ref, out_ref, log_ref):
    def one_block(b, carry):
        rows = pl.ds(pl.multiple_of(b * BLK, BLK), BLK)

        def attend(count):
            places = key_rows(keys_at, b, count)
            query = head_diagonal(q_ref[rows, :])
            raw = dot_right_t(stacked(k_ref, places), query)
            scores, peak = [], None
            for i in range(count):
                piece = raw[i * BLK : (i + 1) * BLK] + bias_ref[b, i : i + 1, :]
                scores.append(piece)
                high = jnp.max(piece.reshape(BLK // 8, 8, WIDE), axis=0)
                peak = high if peak is None else jnp.maximum(peak, high)
            peak = jnp.max(peak, axis=0, keepdims=True)
            total, weights = None, []
            for piece in scores:
                exponent = jnp.exp(piece - peak)
                part = row_sums(exponent)
                total = part if total is None else total + part
                weights.append(exponent.astype(BF))
            total = jnp.sum(total, axis=0, keepdims=True)
            mix = dot_left_t(jnp.concatenate(weights, axis=0), stacked(v_ref, places))
            column = jnp.transpose(jnp.broadcast_to(total, (128, WIDE)))
            mix = mix / jnp.concatenate([column, column], axis=1)
            out_ref[rows, :] = diagonal_rows(mix).astype(BF)
            log_ref[b] = peak + jnp.log(total)

        for_steps(steps_of[b], attend)
        return carry

    lax.fori_loop(0, q_ref.shape[0] // BLK, one_block, 0)


def backward_kernel(
    keys_at,
    steps_of,
    q_ref,
    k_ref,
    v_ref,
    bias_ref,
    log_ref,
    d_ref,
    own_ref,
    in_ref,
    wk_ref,
    wv_ref,
    dq_ref,
    others_ref,
    grad_ref,
    dkey,
    dvalue,
    low,
    back_sum,
):
    dkey[...] = jnp.zeros_like(dkey)
    dvalue[...] = jnp.zeros_like(dvalue)

    def one_block(b, carry):
        rows = pl.ds(pl.multiple_of(b * BLK, BLK), BLK)

        def attend(count):
            places = key_rows(keys_at, b, count)
            query = head_diagonal(q_ref[rows, :])
            d_mixed = head_diagonal(d_ref[rows, :])
            logs = log_ref[b]
            keys = stacked(k_ref, places)
            raw = dot_right_t(keys, query)
            back = dot_right_t(stacked(v_ref, places), d_mixed)
            probs, inner = [], None
            for i in range(count):
                at = slice(i * BLK, (i + 1) * BLK)
                prob = jnp.exp(raw[at] + (bias_ref[b, i : i + 1, :] - logs))
                probs.append(prob)
                part = row_sums(prob * back[at])
                inner = part if inner is None else inner + part
            grad = dot(jnp.concatenate([p.astype(BF) for p in probs], axis=0), d_mixed)
            for i, p in enumerate(places):
                dvalue[p, :] += grad[i * BLK : (i + 1) * BLK]
            inner = jnp.sum(inner, axis=0, keepdims=True)
            d_score = jnp.concatenate(
                [
                    (prob * (back[i * BLK : (i + 1) * BLK] - inner)).astype(BF)
                    for i, prob in enumerate(probs)
                ],
                axis=0,
            )
            grad = dot(d_score, query)
            for i, p in enumerate(places):
                dkey[p, :] += grad[i * BLK : (i + 1) * BLK]
            d_query = dot_left_t(d_score, keys)
            dq_ref[rows, :] = (diagonal_rows(d_query) * (HD**-0.5)).astype(BF)

        for_steps(steps_of[b], attend)
        return carry

    lax.fori_loop(0, q_ref.shape[0] // BLK, one_block, 0)

    low[0] = dkey[...].astype(BF)
    low[1] = dvalue[...].astype(BF)
    grad_ref[:, :WIDE] = dot_left_t(own_ref[...], dq_ref[...]).astype(BF)
    grad_ref[:, WIDE : 2 * WIDE] = dot_left_t(in_ref[...], low[0]).astype(BF)
    grad_ref[:, 2 * WIDE :] = dot_left_t(in_ref[...], low[1]).astype(BF)
    quad = pl.program_id(0)

    def others(r, carry):
        at = pl.ds(pl.multiple_of(r * WIDE, WIDE), WIDE)
        part = dot_right_t(low[0, at, :], wk_ref[...]) + dot_right_t(low[1, at, :], wv_ref[...])
        so_far = jnp.where(quad == 0, jnp.zeros_like(part), back_sum[at, :]) + part
        back_sum[at, :] = so_far
        others_ref[at, :] = so_far.astype(BF)
        return carry

    lax.fori_loop(0, in_ref.shape[0] // WIDE, others, 0)


SHORT = pl.CostEstimate(flops=1_000_000, bytes_accessed=1_000_000, transcendentals=0)
MESH_ID = pl.DeviceIdType.MESH
CALL_GATHER_FIRST, CALL_GATHER, CALL_REDUCE, CALL_NORMS, CALL_ROWS, CALL_LINE_FFN, CALL_LINE_ATTN, CALL_BOTH = range(8)


def quad_places():
    me = lax.axis_index("quad")
    mate = me + 1 - 2 * (me % 2)
    return me, mate, (me + 2) % QUAD, (mate + 2) % QUAD


def greet(*peers):
    barrier = pltpu.get_barrier_semaphore()
    for peer in peers:
        pl.semaphore_signal(barrier, inc=1, device_id=peer, device_id_type=MESH_ID)
    pl.semaphore_wait(barrier, len(peers))


def block_at(block, size, start=0, rows=None):
    return pl.ds(pl.multiple_of(block * size + start, 16), size if rows is None else rows)


def line_peers(parts):
    plane = lax.axis_index("tensor")
    return [{"tensor": (plane + by) % parts} for by in range(1, parts)]


def lines_start(parts, groups, owns, outs, keep_sem, send_sem, recv_sem):
    peers = line_peers(parts)
    copies, kept, n = [], [], 0
    for count, out in zip(groups, outs):
        for kind in range(count):
            own = owns[n]
            width = own.shape[1]
            kept.append(
                pltpu.make_async_copy(own, out.at[:, pl.ds(kind * parts * width, width)], keep_sem.at[n])
            )
            kept[-1].start()
            for by in range(1, parts):
                copy = pltpu.make_async_remote_copy(
                    src_ref=own,
                    dst_ref=out.at[:, pl.ds((kind * parts + by) * width, width)],
                    send_sem=send_sem.at[n, by - 1],
                    recv_sem=recv_sem.at[n, by - 1],
                    device_id=peers[by - 1],
                    device_id_type=MESH_ID,
                )
                copy.start()
                copies.append(copy)
            n += 1
    return copies, kept


def lines_finish(copies, kept):
    for copy in copies + kept:
        copy.wait()


def lines_shapes(parts, groups):
    owns = [own for group in groups for own in group]
    shapes = [
        jax.ShapeDtypeStruct((group[0].shape[0], parts * len(group) * group[0].shape[1]), BF)
        for group in groups
    ]
    dma, count = pltpu.SemaphoreType.DMA, max(len(owns), 1)
    return owns, shapes, [dma((count,)), dma((count, parts - 1)), dma((count, parts - 1))]


def gather_kernel(pieces, parts_along, groups, *refs):
    count, lines = len(pieces), sum(groups)
    at = [count, count + lines, 2 * count + lines, 2 * count + lines + len(groups)]
    owns, line_owns = refs[: at[0]], refs[at[0] : at[1]]
    outs, line_outs = refs[at[1] : at[2]], refs[at[2] : at[3]]
    keep_sem, mate_send, mate_recv, far_send, far_recv, on_send, on_recv = refs[at[3] : at[3] + 7]
    me, mate, far, cross = quad_places()
    greet({"quad": mate}, {"quad": far}, *(line_peers(parts_along) if groups else []))

    def send(source, target, sends, recvs, at, peer):
        return pltpu.make_async_remote_copy(
            src_ref=source,
            dst_ref=target,
            send_sem=sends.at[at],
            recv_sem=recvs.at[at],
            device_id={"quad": peer},
            device_id_type=MESH_ID,
        )

    parts = []
    for n in range(count):
        size = owns[n].shape[0]
        step = size // pieces[n]
        for p in range(pieces[n]):
            parts.append((n, size, p * step, step))
    to_far = [
        send(owns[n].at[pl.ds(start, step)], outs[n].at[block_at(me, size, start, step)], far_send, far_recv, i, far)
        for i, (n, size, start, step) in enumerate(parts)
    ]
    for copy in to_far:
        copy.start()
    to_mate = [
        send(owns[n], outs[n].at[block_at(me, owns[n].shape[0])], mate_send, mate_recv, n, mate)
        for n in range(count)
    ]
    for copy in to_mate:
        copy.start()
    along = lines_start(parts_along, groups, line_owns, line_outs, *refs[at[3] + 7 :])
    kept = [
        pltpu.make_async_copy(owns[n], outs[n].at[block_at(me, owns[n].shape[0])], keep_sem.at[n])
        for n in range(count)
    ]
    for copy in kept:
        copy.start()
    onward = []
    for i, (n, size, start, step) in enumerate(parts):
        to_far[i].wait_recv()
        came = outs[n].at[block_at(far, size, start, step)]
        copy = send(came, came, on_send, on_recv, i, mate)
        copy.start()
        onward.append(copy)
    for copy in to_mate + onward:
        copy.wait()
    for copy in to_far:
        copy.wait_send()
    for copy in kept:
        copy.wait()
    lines_finish(*along)


def quad_gather(arrays, pieces, call, parts=1, groups=()):
    count, total = len(arrays), sum(pieces)
    sems = [pltpu.SemaphoreType.DMA((k,)) for k in (count, count, count, total, total, total, total)]
    owns, shapes, line_sems = lines_shapes(max(parts, 2), groups)
    return pl.pallas_call(
        functools.partial(gather_kernel, pieces, parts, tuple(len(g) for g in groups)),
        out_shape=[jax.ShapeDtypeStruct((QUAD * x.shape[0],) + x.shape[1:], x.dtype) for x in arrays]
        + shapes,
        in_specs=[pl.BlockSpec(memory_space=pltpu.VMEM)] * (count + len(owns)),
        out_specs=[pl.BlockSpec(memory_space=pl.ANY)] * (count + len(shapes)),
        scratch_shapes=sems + line_sems,
        compiler_params=pltpu.CompilerParams(collective_id=call, has_side_effects=True),
        cost_estimate=SHORT,
        name="quad_gather",
    )(*arrays, *owns)


REDUCE_PIECES = 4


def reduce_kernel(
    parts_ref,
    out_ref,
    near,
    relay,
    beyond,
    mate_send,
    mate_recv,
    own_send,
    own_recv,
    far_send,
    far_recv,
    greeted=False,
):
    me, mate, far, cross = quad_places()
    if not greeted:
        greet({"quad": mate}, {"quad": far})
    size = out_ref.shape[0]
    step = size // REDUCE_PIECES

    def send(source, target, send_sem, recv_sem, peer):
        copy = pltpu.make_async_remote_copy(
            src_ref=source,
            dst_ref=target,
            send_sem=send_sem,
            recv_sem=recv_sem,
            device_id={"quad": peer},
            device_id_type=MESH_ID,
        )
        copy.start()
        return copy

    to_mate = [
        send(
            parts_ref.at[block_at(cross, size, p * step, step)],
            near.at[1, pl.ds(p * step, step)],
            mate_send.at[p],
            mate_recv.at[p],
            mate,
        )
        for p in range(REDUCE_PIECES)
    ]
    own = send(parts_ref.at[block_at(mate, size)], near.at[0], own_send, own_recv, mate)
    to_far = []
    for p in range(REDUCE_PIECES):
        rows = pl.ds(p * step, step)
        to_mate[p].wait_recv()
        mine = parts_ref[block_at(far, size, p * step, step), :].astype(F32)
        relay[rows, :] = (mine + near[1, rows, :].astype(F32)).astype(BF)
        to_far.append(send(relay.at[rows], beyond.at[rows], far_send.at[p], far_recv.at[p], far))
    own.wait_recv()
    for p in range(REDUCE_PIECES):
        rows = pl.ds(p * step, step)
        to_far[p].wait_recv()
        mine = parts_ref[block_at(me, size, p * step, step), :].astype(F32)
        out_ref[rows, :] = mine + near[0, rows, :].astype(F32) + beyond[rows, :].astype(F32)
    for copy in to_mate + [own] + to_far:
        copy.wait_send()


def reduce_scratch(rows, width):
    one, each = pltpu.SemaphoreType.DMA, pltpu.SemaphoreType.DMA((REDUCE_PIECES,))
    low = pltpu.VMEM((rows, width), BF)
    return [pltpu.VMEM((2, rows, width), BF), low, low, each, each, one, one, each, each]


def quad_reduce(parts):
    rows, width = parts.shape[0] // QUAD, parts.shape[1]
    return pl.pallas_call(
        reduce_kernel,
        out_shape=jax.ShapeDtypeStruct((rows, width), F32),
        in_specs=[pl.BlockSpec(memory_space=pltpu.VMEM)],
        out_specs=pl.BlockSpec(memory_space=pltpu.VMEM),
        scratch_shapes=reduce_scratch(rows, width),
        compiler_params=pltpu.CompilerParams(collective_id=CALL_REDUCE, has_side_effects=True),
        cost_estimate=SHORT,
        name="quad_reduce",
    )(parts)


def both_kernel(sizes, planes, parts_ref, *refs):
    count = len(sizes)
    x_refs, out_ref, line_refs, scratch = refs[:count], refs[count], refs[count + 1 :][:count], refs[2 * count + 1 :]
    me, mate, far, cross = quad_places()
    greet({"quad": mate}, {"quad": far}, *line_peers(planes))
    lines = []
    for n in range(count):
        held, came, send_sem, recv_sem = scratch[4 * n : 4 * n + 4]
        lines.append((came, line_start(sizes[n], planes, x_refs[n], held, came, send_sem, recv_sem)))
    reduce_kernel(parts_ref, out_ref, *scratch[4 * count :], greeted=True)
    for n in range(count):
        line_finish(sizes[n], planes, x_refs[n], line_refs[n], *lines[n])


def quad_reduce_and_lines(parts, lines, sizes, planes):
    rows, width = parts.shape[0] // QUAD, parts.shape[1]
    shapes = [(x.shape[0], sum(own)) for x, own in zip(lines, sizes)]
    vmem, count = pl.BlockSpec(memory_space=pltpu.VMEM), len(lines)
    return pl.pallas_call(
        functools.partial(both_kernel, tuple(sizes), planes),
        out_shape=[jax.ShapeDtypeStruct((rows, width), F32)]
        + [jax.ShapeDtypeStruct(shape, F32) for shape in shapes],
        in_specs=[vmem] * (1 + count),
        out_specs=[vmem] * (1 + count),
        scratch_shapes=sum([line_scratch(shape, planes) for shape in shapes], [])
        + reduce_scratch(rows, width),
        compiler_params=pltpu.CompilerParams(collective_id=CALL_BOTH, has_side_effects=True),
        cost_estimate=SHORT,
        name="quad_reduce_and_lines",
    )(parts, *lines)


def norms_kernel(hops, x_ref, out_ref, held, came, send_sem, recv_sem):
    peers = []
    for axis, bit in hops:
        at = lax.axis_index(axis)
        peers.append({axis: at + bit - 2 * bit * ((at // bit) % 2)})
    greet(*peers)
    for n, peer in enumerate(peers):
        source = x_ref if n == 0 else held.at[n]
        copy = pltpu.make_async_remote_copy(
            src_ref=source,
            dst_ref=came.at[n],
            send_sem=send_sem.at[n],
            recv_sem=recv_sem.at[n],
            device_id=peer,
            device_id_type=MESH_ID,
        )
        copy.start()
        copy.wait()
        total = source[...] + came[n]
        if n == len(peers) - 1:
            out_ref[...] = total
        else:
            held[n + 1] = total


def sum_everywhere(x):
    hops = []
    for axis in ("quad", "row", "tensor", "hi"):
        bit = 1
        while bit < lax.axis_size(axis):
            hops.append((axis, bit))
            bit *= 2
    vmem = pltpu.VMEM((len(hops),) + x.shape, x.dtype)
    return pl.pallas_call(
        functools.partial(norms_kernel, tuple(hops)),
        out_shape=jax.ShapeDtypeStruct(x.shape, x.dtype),
        in_specs=[pl.BlockSpec(memory_space=pltpu.VMEM)],
        out_specs=pl.BlockSpec(memory_space=pltpu.VMEM),
        scratch_shapes=[
            vmem,
            vmem,
            pltpu.SemaphoreType.DMA((len(hops),)),
            pltpu.SemaphoreType.DMA((len(hops),)),
        ],
        compiler_params=pltpu.CompilerParams(collective_id=CALL_NORMS, has_side_effects=True),
        cost_estimate=SHORT,
        name="sum_everywhere",
    )(x)


def rows_kernel(parts, groups, own_ref, *refs):
    lines = sum(groups)
    line_owns, out_ref, line_outs = refs[:lines], refs[lines], refs[lines + 1 : lines + 1 + len(groups)]
    keep_sem, line_send, line_recv, send_sem, recv_sem = refs[lines + 1 + len(groups) :][:5]
    line_sems = refs[lines + 1 + len(groups) :][5:]
    me, mate, far, cross = quad_places()
    row, plane = lax.axis_index("row"), lax.axis_index("tensor")
    other = 1 - row
    line = [{"tensor": (plane + by) % parts} for by in range(1, parts)]
    to_x, to_y, to_mate = {"quad": far}, {"row": other}, {"quad": mate}
    greet(*line, to_x, to_y, to_mate)
    size, width = own_ref.shape

    def block(at_row, at_quad, part):
        return out_ref.at[block_at(at_row * QUAD + at_quad, size), pl.ds(part * width, width)]

    used = []

    def send(source, target, peer, n):
        copy = pltpu.make_async_remote_copy(
            src_ref=source,
            dst_ref=target,
            send_sem=send_sem.at[n],
            recv_sem=recv_sem.at[n],
            device_id=peer,
            device_id_type=MESH_ID,
        )
        copy.start()
        used.append(copy)
        return copy

    along = []
    for by in range(1, parts):
        copy = pltpu.make_async_remote_copy(
            src_ref=own_ref,
            dst_ref=block(row, me, by),
            send_sem=line_send.at[by - 1],
            recv_sem=line_recv.at[by - 1],
            device_id=line[by - 1],
            device_id_type=MESH_ID,
        )
        copy.start()
        along.append(copy)
    keep = pltpu.make_async_copy(own_ref, block(row, me, 0), keep_sem)
    keep.start()
    only_line = lines_start(parts, groups, line_owns, line_outs, *line_sems)
    near_x, near_y, beyond, mates = [], [], [], []
    for part in range(parts + 1):
        if part < parts:
            if part:
                along[part - 1].wait_recv()
            source = own_ref if part == 0 else block(row, me, part)
            target = block(row, me, part)
            near_x.append(send(source, target, to_x, part))
            near_y.append(send(source, target, to_y, parts + part))
            mates.append(send(source, target, to_mate, 2 * parts + part))
        if part:
            done = part - 1
            from_x, from_y = block(row, far, done), block(other, me, done)
            near_x[done].wait_recv()
            near_y[done].wait_recv()
            if done % 2:
                beyond.append(send(from_y, from_y, to_x, 3 * parts + done))
            else:
                beyond.append(send(from_x, from_x, to_y, 3 * parts + done))
            mates.append(send(from_x, from_x, to_mate, 4 * parts + done))
            mates.append(send(from_y, from_y, to_mate, 5 * parts + done))
    for part in range(parts):
        beyond[part].wait_recv()
        came = block(other, far, part)
        mates.append(send(came, came, to_mate, 6 * parts + part))
    for copy in mates:
        copy.wait_recv()
    for copy in along + used:
        copy.wait_send()
    keep.wait()
    lines_finish(*only_line)


def gather_rows(rows, parts, groups):
    size, width = rows.shape
    dma = pltpu.SemaphoreType.DMA
    owns, shapes, line_sems = lines_shapes(parts, groups)
    return pl.pallas_call(
        functools.partial(rows_kernel, parts, tuple(len(g) for g in groups)),
        out_shape=[jax.ShapeDtypeStruct((ROW * QUAD * size, parts * width), rows.dtype)] + shapes,
        in_specs=[pl.BlockSpec(memory_space=pltpu.VMEM)] * (1 + len(owns)),
        out_specs=[pl.BlockSpec(memory_space=pl.ANY)] * (1 + len(shapes)),
        scratch_shapes=[dma, dma((parts - 1,)), dma((parts - 1,)), dma((7 * parts,)), dma((7 * parts,))]
        + line_sems,
        compiler_params=pltpu.CompilerParams(collective_id=CALL_ROWS, has_side_effects=True),
        cost_estimate=SHORT,
        name="gather_rows",
    )(rows, *owns)


def regroup_kernel(parts, kinds, x_ref, out_ref):
    size = x_ref.shape[1] // (parts * kinds)
    for kind in range(kinds):
        for part in range(parts):
            to, at = (kind * parts + part) * size, (part * kinds + kind) * size
            out_ref[:, to : to + size] = x_ref[:, at : at + size]


def regroup(rows, parts, kinds):
    steps = max(rows.shape[0] // 192, 1)
    block = pl.BlockSpec((rows.shape[0] // steps, rows.shape[1]), lambda i: (i, 0))
    return pl.pallas_call(
        functools.partial(regroup_kernel, parts, kinds),
        out_shape=jax.ShapeDtypeStruct(rows.shape, rows.dtype),
        grid=(steps,),
        in_specs=[block],
        out_specs=block,
        cost_estimate=SHORT,
        name="regroup",
    )(rows)


def line_pick(sizes, parts, x_ref, part):
    columns, start = [], 0
    for size in sizes:
        columns.append(x_ref[:, start + part * size : start + (part + 1) * size])
        start += parts * size
    return jnp.concatenate(columns, axis=1)


def line_start(sizes, parts, x_ref, held, came, send_sem, recv_sem):
    plane = lax.axis_index("tensor")
    copies = []
    for by in range(1, parts):
        held[by - 1] = line_pick(sizes, parts, x_ref, by)
        copy = pltpu.make_async_remote_copy(
            src_ref=held.at[by - 1],
            dst_ref=came.at[by - 1],
            send_sem=send_sem.at[by - 1],
            recv_sem=recv_sem.at[by - 1],
            device_id={"tensor": (plane + parts - by) % parts},
            device_id_type=MESH_ID,
        )
        copy.start()
        copies.append(copy)
    return copies


def line_finish(sizes, parts, x_ref, out_ref, came, copies):
    total = line_pick(sizes, parts, x_ref, 0).astype(F32)
    for by in range(1, parts):
        copies[by - 1].wait_recv()
        total = total + came[by - 1].astype(F32)
    out_ref[...] = total
    for copy in copies:
        copy.wait_send()


def line_scratch(shape, parts):
    dma = pltpu.SemaphoreType.DMA((parts - 1,))
    return [pltpu.VMEM((parts - 1,) + shape, BF), pltpu.VMEM((parts - 1,) + shape, BF), dma, dma]


def parts_kernel(sizes, parts, x_ref, out_ref, held, came, send_sem, recv_sem):
    greet(*line_peers(parts))
    copies = line_start(sizes, parts, x_ref, held, came, send_sem, recv_sem)
    line_finish(sizes, parts, x_ref, out_ref, came, copies)


def sum_line(rows, sizes, parts, call):
    shape = (rows.shape[0], sum(sizes))
    return pl.pallas_call(
        functools.partial(parts_kernel, sizes, parts),
        out_shape=jax.ShapeDtypeStruct(shape, F32),
        in_specs=[pl.BlockSpec(memory_space=pltpu.VMEM)],
        out_specs=pl.BlockSpec(memory_space=pltpu.VMEM),
        scratch_shapes=line_scratch(shape, parts),
        compiler_params=pltpu.CompilerParams(collective_id=call, has_side_effects=True),
        cost_estimate=SHORT,
        name="sum_line",
    )(rows)


def attend_forward(query, keyval, tables):
    keys_at, steps_of, bias = tables
    own, width = query.shape
    quads = width // WIDE
    rows = keyval.shape[0]
    blocks = own // BLK
    return pl.pallas_call(
        forward_kernel,
        grid_spec=pltpu.PrefetchScalarGridSpec(
            num_scalar_prefetch=2,
            grid=(quads,),
            in_specs=[
                pl.BlockSpec((own, WIDE), lambda i, *_: (0, i)),
                pl.BlockSpec((rows, WIDE), lambda i, *_: (0, i)),
                pl.BlockSpec((rows, WIDE), lambda i, *_: (0, i + quads)),
                pl.BlockSpec((blocks, LONGEST, WIDE), lambda i, *_: (0, 0, i)),
            ],
            out_specs=[
                pl.BlockSpec((own, WIDE), lambda i, *_: (0, i)),
                pl.BlockSpec((blocks, 1, WIDE), lambda i, *_: (0, 0, i)),
            ],
        ),
        out_shape=[
            jax.ShapeDtypeStruct((own, width), BF),
            jax.ShapeDtypeStruct((blocks, 1, width), F32),
        ],
        cost_estimate=SHORT,
        name="attend_forward",
    )(keys_at, steps_of, query, keyval, keyval, bias)


def attend_backward(query, keyval, logs, d_mixed, tables, own_inputs, inputs, w_keyval):
    keys_at, steps_of, bias = tables
    own, width = query.shape
    quads = width // WIDE
    rows, depth = inputs.shape
    blocks = own // BLK
    once = pl.Buffered(1)
    return pl.pallas_call(
        backward_kernel,
        grid_spec=pltpu.PrefetchScalarGridSpec(
            num_scalar_prefetch=2,
            grid=(quads,),
            in_specs=[
                pl.BlockSpec((own, WIDE), lambda i, *_: (0, i)),
                pl.BlockSpec((rows, WIDE), lambda i, *_: (0, i)),
                pl.BlockSpec((rows, WIDE), lambda i, *_: (0, i + quads)),
                pl.BlockSpec((blocks, LONGEST, WIDE), lambda i, *_: (0, 0, i)),
                pl.BlockSpec((blocks, 1, WIDE), lambda i, *_: (0, 0, i)),
                pl.BlockSpec((own, WIDE), lambda i, *_: (0, i)),
                pl.BlockSpec((own, depth), lambda i, *_: (0, 0), pipeline_mode=once),
                pl.BlockSpec((rows, depth), lambda i, *_: (0, 0), pipeline_mode=once),
                pl.BlockSpec((depth, WIDE), lambda i, *_: (0, i)),
                pl.BlockSpec((depth, WIDE), lambda i, *_: (0, i + quads)),
            ],
            out_specs=[
                pl.BlockSpec((own, WIDE), lambda i, *_: (0, i)),
                pl.BlockSpec((rows, depth), lambda i, *_: (0, 0)),
                pl.BlockSpec((depth, 3 * WIDE), lambda i, *_: (0, i)),
            ],
            scratch_shapes=[
                pltpu.VMEM((rows, WIDE), F32),
                pltpu.VMEM((rows, WIDE), F32),
                pltpu.VMEM((2, rows, WIDE), BF),
                pltpu.VMEM((rows, depth), F32),
            ],
        ),
        out_shape=[
            jax.ShapeDtypeStruct((own, width), BF),
            jax.ShapeDtypeStruct((rows, depth), BF),
            jax.ShapeDtypeStruct((depth, 3 * width), BF),
        ],
        cost_estimate=SHORT,
        name="attend_backward",
    )(keys_at, steps_of, query, keyval, keyval, bias, logs, d_mixed, own_inputs, inputs, w_keyval, w_keyval)


def weights_kernel(steps, ffn_ref, two_ref, one_ref, pre_ref, act_ref, mixed_ref, out_ref, left):
    i = pl.program_id(0)
    for start, ref in ((0, ffn_ref), (steps, two_ref), (2 * steps, one_ref)):

        @pl.when(i == start)
        def _():
            left[...] = jnp.transpose(ref[...])

    for start, ref in ((0, pre_ref), (steps, act_ref), (2 * steps, mixed_ref)):

        @pl.when((i >= start) & (i < start + steps))
        def _():
            out_ref[...] = dot(left[...], ref[...]).astype(BF)


def weight_grads(ffn_in, d_two, d_one, d_pre, activated, mixed):
    own, depth = ffn_in.shape
    steps = d_pre.shape[1] // depth
    last = steps - 1
    whole = pl.BlockSpec((own, depth), lambda i: (0, 0), pipeline_mode=pl.Buffered(1))
    return pl.pallas_call(
        functools.partial(weights_kernel, steps),
        grid=(2 * steps + 1,),
        in_specs=[
            whole,
            whole,
            whole,
            pl.BlockSpec((own, depth), lambda i: (0, jnp.minimum(i, last))),
            pl.BlockSpec((own, depth), lambda i: (0, jnp.clip(i - steps, 0, last))),
            whole,
        ],
        out_specs=pl.BlockSpec((depth, depth), lambda i: (0, i)),
        out_shape=jax.ShapeDtypeStruct((depth, (2 * steps + 1) * depth), BF),
        scratch_shapes=[pltpu.VMEM((depth, own), BF)],
        cost_estimate=SHORT,
        name="weight_grads",
    )(ffn_in, d_two, d_one, d_pre, activated, mixed)


def attention_tables(doc_lengths, block_deal, random_rows, own_blocks, first_own):
    blocks = block_deal.shape[0]
    doc_ends = jnp.cumsum(doc_lengths)
    doc_starts = doc_ends - doc_lengths
    place = jnp.arange(blocks, dtype=jnp.int32)
    stored_at = jnp.sum(
        jnp.where(block_deal[None, :] == place[:, None], place[None, :], 0), axis=1
    )
    own = lax.dynamic_slice(block_deal, (first_own,), (own_blocks,))
    doc_index = jnp.sum((own[:, None] >= doc_ends[None, :]).astype(jnp.int32), axis=1)
    doc_pick = (
        doc_index[:, None] == jnp.arange(doc_lengths.shape[0], dtype=jnp.int32)[None, :]
    ).astype(jnp.int32)
    first_block = jnp.sum(doc_pick * doc_starts[None, :], axis=1)
    doc_blocks = jnp.sum(doc_pick * doc_lengths[None, :], axis=1)
    local = own - first_block
    other = jnp.arange(LONGEST, dtype=jnp.int32)
    wanted = jnp.minimum(first_block[:, None] + other[None, :], blocks - 1)
    keys_at = jnp.sum(
        jnp.where(wanted[:, :, None] == place[None, None, :], stored_at[None, None, :], 0), axis=2
    )
    own_pick = (own[:, None] == place[None, :]).astype(jnp.int32)
    picks = jnp.sum(own_pick[None, :, :, None] * random_rows[:, None, :, :], axis=2)
    picks = jnp.remainder(picks, doc_blocks[None, :, None])
    random_hit = jnp.any(picks[:, :, :, None] == other[None, None, None, :], axis=2)
    inside = other[None, :] < doc_blocks[:, None]
    near = jnp.abs(local[:, None] - other[None, :]) <= 1
    everywhere = (local[:, None] < 2) | (other[None, :] < 2)
    allowed = inside[None] & ((near | everywhere)[None] | random_hit)
    bias = jnp.where(allowed, 0.0, MASK_VALUE).astype(F32)
    bias = jnp.repeat(bias.transpose(1, 2, 0), BLK, axis=2)
    steps_of = (doc_blocks + STEP - 1) // STEP
    return keys_at, steps_of, bias


def to_home(steps, parts):
    pairs = []
    for hi in range(steps):
        for row in range(ROW):
            for quad in range(QUAD):
                side, core = quad // 2, quad % 2
                plane = parts - 1 - side if core else side
                for part in range(parts):
                    source = ((hi * ROW + row) * QUAD + quad) * parts + part
                    target = ((hi * ROW + row) * QUAD + part) * parts + plane
                    pairs.append((source, target))
    return pairs


def local(
    layer_input,
    w_qkv,
    w_out,
    w_up,
    w_down,
    attn_gain,
    attn_shift,
    ffn_gain,
    ffn_shift,
    out_grad,
    doc_lengths,
    block_deal,
    random_blocks,
):
    own_rows, width = layer_input.shape
    tensor = lax.axis_size("tensor")
    slot = lax.axis_index("quad")
    plane = lax.axis_index("tensor")
    head_local = random_blocks.shape[1]
    chunk = head_local * HD
    depth = w_qkv.shape[1]
    hidden = w_up.shape[2]
    score_scale = HD ** (-0.5)
    moves = to_home(lax.axis_size("hi"), tensor)
    moves_back = [(b, a) for a, b in moves]

    def shifted(x, by):
        return lax.ppermute(x, "tensor", [(i, (i + by) % tensor) for i in range(tensor)])

    def spread(shard):
        return [shard] + [shifted(shard, by) for by in range(1, tensor)]

    def by_kind(parts, kinds):
        rows = jnp.stack([part.reshape(depth, kinds, -1) for part in parts], axis=2)
        return rows.reshape(depth, -1)

    def attn_shard(qkv, back):
        qkv = qkv.reshape(depth, head_local, 3, HD).transpose(0, 2, 1, 3)
        return jnp.concatenate([qkv.reshape(depth, 3 * chunk), back.T], axis=1)

    def over_data(rows):
        return lax.all_gather(rows, DATA, axis=0, tiled=True)

    docs, group_blocks = doc_lengths.shape[1], block_deal.shape[1]
    numbers = jnp.concatenate([doc_lengths[0], block_deal[0], random_blocks[0].reshape(-1)])
    numbers = jnp.stack([numbers // BLK, numbers % BLK]).astype(BF)
    numbers = jnp.pad(numbers, ((0, 14), (0, width - numbers.shape[1])))
    own_numbers = lax.ppermute(numbers, EVERY, moves)
    own_tokens = lax.ppermute(layer_input, EVERY, moves)
    ffn_shards = [w_up[0], w_down[0].T]
    if lax.axis_size("hi") == 1:
        rows, first_rows = gather_rows(attn_shard(w_qkv[0], w_out[0]), tensor, [ffn_shards])
        rows, first_rows, own_tokens, own_numbers = lax.optimization_barrier(
            (rows, first_rows, own_tokens, own_numbers)
        )
        attn_full = [regroup(rows, tensor, 4)]
    else:
        attn_full = [over_data(by_kind(spread(attn_shard(w_qkv[0], w_out[0])), 4))]
        first_rows = by_kind(spread(jnp.concatenate(ffn_shards, axis=1)), 2)
    ffn_full = [over_data(first_rows)]

    groups = []
    for layer in range(1, LAYERS):
        groups += [[attn_shard(w_qkv[layer], w_out[layer])], [w_up[layer], w_down[layer].T]]
    inputs, numbers, *later = quad_gather(
        [own_tokens, own_numbers], [4, 1], CALL_GATHER_FIRST, tensor, groups
    )
    numbers = numbers.reshape(QUAD, 16, width)[:, :2].astype(jnp.int32)
    numbers = numbers[:, 0] * BLK + numbers[:, 1]
    lengths, deal = numbers[0, :docs], numbers[0, docs : docs + group_blocks]
    random_home = numbers[:, docs + group_blocks :][:, : random_blocks.size]
    random_home = random_home.reshape(tensor, head_local, group_blocks, -1)
    part_of = (plane - jnp.arange(tensor, dtype=jnp.int32)) % tensor
    part_pick = (part_of[:, None] == jnp.arange(tensor, dtype=jnp.int32)[None, :]).astype(jnp.int32)
    random_home = jnp.sum(part_pick[:, :, None, None, None] * random_home[None], axis=1)
    random_home = random_home.reshape(tensor * head_local, group_blocks, -1)
    own_blocks = own_rows // BLK
    tables = attention_tables(
        lengths,
        deal,
        random_home,
        own_blocks,
        slot * own_blocks,
    )

    stream = own_tokens.astype(F32)
    stored = []
    for layer in range(LAYERS):
        attn_w, ffn_w = attn_full[layer], ffn_full[layer]
        w_query = attn_w[:, :width]
        w_keyval = attn_w[:, width : 3 * width]
        w_back_t = attn_w[:, 3 * width :]
        w_expand = ffn_w[:, : hidden * tensor]
        w_shrink_t = ffn_w[:, hidden * tensor :]
        own_inputs = stream.astype(BF)
        if layer > 0:
            (inputs,) = quad_gather([own_inputs], [4], CALL_GATHER)
        query = (dot(own_inputs, w_query).astype(BF).astype(F32) * score_scale).astype(BF)
        keyval = dot(inputs, w_keyval).astype(BF)
        if layer < LAYERS - 1:
            attn_full.append(over_data(regroup(later[2 * layer], tensor, 4)))
            ffn_full.append(over_data(later[2 * layer + 1]))
        mixed, logs = attend_forward(query, keyval, tables)
        if layer == 0:
            mixed, own_grad = lax.optimization_barrier((mixed, out_grad))
            own_grad = lax.ppermute(own_grad, EVERY, moves)
        summed_one = stream + dot_right_t(mixed, w_back_t)
        normed = layer_norm(summed_one, attn_gain[layer], attn_shift[layer])
        ffn_in = normed.astype(BF)
        pre_act = dot(ffn_in, w_expand)
        activated = gelu_tanh(pre_act).astype(BF)
        summed_two = normed + dot_right_t(activated, w_shrink_t)
        stored.append(
            (own_inputs, inputs, query, keyval, mixed, logs, summed_one, ffn_in, pre_act, activated, summed_two)
        )
        stream = layer_norm(summed_two, ffn_gain[layer], ffn_shift[layer])
    layer_output = lax.ppermute(stream.astype(BF), EVERY, moves_back)

    def by_piece(rows):
        rows = rows.reshape(depth, -1, 3, WIDE).transpose(0, 2, 1, 3)
        return rows.reshape(depth, 3 * width)

    def sum_data(part):
        return lax.psum_scatter(part, DATA, scatter_dimension=0, tiled=True)

    state_grad = own_grad.astype(F32)
    attn_sums = [None] * LAYERS
    attn_grads = [None] * LAYERS
    ffn_grads = [None] * LAYERS
    norm_parts = [None] * LAYERS
    for layer in reversed(range(LAYERS)):
        (own_inputs, inputs, query, keyval, mixed, logs, summed_one, ffn_in, pre_act, activated, summed_two) = stored[layer]
        attn_w, ffn_w = attn_full[layer], ffn_full[layer]
        w_query = attn_w[:, :width]
        w_keyval = attn_w[:, width : 3 * width]
        w_back_t = attn_w[:, 3 * width :]
        w_expand = ffn_w[:, : hidden * tensor]
        w_shrink_t = ffn_w[:, hidden * tensor :]
        unused_two, ffn_back = jax.vjp(layer_norm, summed_two, ffn_gain[layer], ffn_shift[layer])
        d_two, ffn_gain_part, ffn_shift_part = ffn_back(state_grad)
        d_two_low = d_two.astype(BF)
        unused_act, gelu_back = jax.vjp(gelu_tanh, pre_act)
        d_pre = gelu_back(dot(d_two_low, w_shrink_t))[0].astype(BF)
        d_normed = d_two + dot_right_t(d_pre, w_expand)
        unused_one, attn_back = jax.vjp(layer_norm, summed_one, attn_gain[layer], attn_shift[layer])
        d_one, attn_gain_part, attn_shift_part = attn_back(d_normed)
        norm_parts[layer] = (attn_gain_part, attn_shift_part, ffn_gain_part, ffn_shift_part)
        d_one_low = d_one.astype(BF)
        ffn_part = weight_grads(ffn_in, d_two_low, d_one_low, d_pre, activated, mixed)
        d_one_low, ffn_part = lax.optimization_barrier((d_one_low, ffn_part))
        ffn_sum = sum_data(ffn_part)
        d_mixed = dot(d_one_low, w_back_t).astype(BF)
        if layer < LAYERS - 1:
            norms = jnp.stack([norm_parts[l][k] for k in range(4) for l in range(LAYERS)])
            d_mixed, norms = lax.optimization_barrier((d_mixed, norms))
            norm_sums = sum_everywhere(norms)
            d_mixed, norm_sums, attn_sums[layer + 1] = lax.optimization_barrier(
                (d_mixed, norm_sums, attn_sums[layer + 1])
            )
        d_query, others, attn_part = attend_backward(
            query, keyval, logs, d_mixed, tables, own_inputs, inputs, w_keyval
        )
        if layer == 0:
            others, ffn_last = lax.optimization_barrier((others, ffn_last))
            ffn_grads[1] = sum_line(ffn_last, (hidden, hidden, chunk), tensor, CALL_LINE_FFN)
            others, ffn_sum, attn_part, ffn_grads[1] = lax.optimization_barrier(
                (others, ffn_sum, attn_part, ffn_grads[1])
            )
        else:
            others, layer_output = lax.optimization_barrier((others, layer_output))
        if layer == 0:
            summed, ffn_grads[0], attn_grads[1] = quad_reduce_and_lines(
                others,
                [ffn_sum, by_piece(attn_sums[1])],
                [(hidden, hidden, chunk), (chunk,) * 3],
                tensor,
            )
        else:
            summed = quad_reduce(others)
            summed, ffn_sum, attn_part = lax.optimization_barrier((summed, ffn_sum, attn_part))
        ffn_last = ffn_sum
        attn_sums[layer] = sum_data(attn_part)
        state_grad = d_one + dot_right_t(d_query, w_query) + summed
    input_grad = lax.ppermute(state_grad.astype(BF), EVERY, moves_back)
    attn_grads[0] = sum_line(by_piece(attn_sums[0]), (chunk,) * 3, tensor, CALL_LINE_ATTN)
    input_grad, attn_grads = lax.optimization_barrier((input_grad, attn_grads))
    input_grad = input_grad.astype(F32)

    qkv_grad = jnp.stack(attn_grads).reshape(LAYERS, depth, 3, head_local, HD)
    qkv_grad = qkv_grad.transpose(0, 1, 3, 2, 4).reshape(LAYERS, depth, 3 * chunk)
    ffn_own = jnp.stack(ffn_grads)
    up_grad = ffn_own[:, :, :hidden]
    down_grad = ffn_own[:, :, hidden : 2 * hidden].transpose(0, 2, 1)
    out_w_grad = ffn_own[:, :, 2 * hidden :].transpose(0, 2, 1)
    return (layer_output, input_grad, qkv_grad, out_w_grad, up_grad, down_grad) + tuple(
        norm_sums[k * LAYERS : (k + 1) * LAYERS] for k in range(4)
    )


def solution(mesh):
    devices = mesh.devices
    tensor = devices.shape[1]
    split = jax.sharding.Mesh(
        devices.reshape(devices.shape[0] // (ROW * QUAD), ROW, QUAD, tensor), EVERY
    )
    placed = (
        P(EVERY, None),
        P(None, DATA, "tensor"),
        P(None, "tensor", DATA),
        P(None, DATA, "tensor"),
        P(None, "tensor", DATA),
        P(),
        P(),
        P(),
        P(),
        P(EVERY, None),
        P(DATA, None),
        P(DATA, None),
        P(DATA, "tensor", None, None),
    )
    return jax.shard_map(
        local,
        mesh=split,
        in_specs=placed,
        out_specs=(
            P(EVERY, None),
            P(EVERY, None),
            P(None, DATA, "tensor"),
            P(None, "tensor", DATA),
            P(None, DATA, "tensor"),
            P(None, "tensor", DATA),
            P(),
            P(),
            P(),
            P(),
        ),
        check_vma=False,
    )
```

```python
import functools

import jax
import jax.numpy as jnp
from jax import lax
from jax.experimental import pallas as pl
from jax.experimental.pallas import tpu as pltpu
from jax.sharding import PartitionSpec as P

HD = 64
BLK = 64
LAYERS = 2
LONGEST = 16
QUAD = 4
WIDE = QUAD * HD
STEP = 4
STEPS = LONGEST // STEP

ROW = 2
DATA = ("hi", "row", "quad")
EVERY = DATA + ("tensor",)

NORM_EPSILON = 1e-12
MASK_VALUE = -1e30
BF = jnp.bfloat16
F32 = jnp.float32


def layer_norm(summed, norm_gain, norm_shift):
    row_mean = jnp.mean(summed, axis=-1, keepdims=True)
    centred = summed - row_mean
    row_var = jnp.mean(centred * centred, axis=-1, keepdims=True)
    return centred * lax.rsqrt(row_var + NORM_EPSILON) * norm_gain + norm_shift


def gelu_tanh(values):
    return jax.nn.gelu(values, approximate=True)


def dot(left, right):
    return jnp.dot(left, right, preferred_element_type=F32)


def dot_right_t(left, right):
    return lax.dot_general(left, right, (((1,), (1,)), ((), ())), preferred_element_type=F32)


def dot_left_t(left, right):
    return lax.dot_general(left, right, (((0,), (0,)), ((), ())), preferred_element_type=F32)


def head_diagonal(rows):
    lane_head = lax.broadcasted_iota(jnp.int32, rows.shape, 1) // HD
    return jnp.concatenate(
        [jnp.where(lane_head == h, rows, jnp.zeros_like(rows)) for h in range(QUAD)], axis=0
    )


def diagonal_rows(full):
    lane_head = lax.broadcasted_iota(jnp.int32, (HD, WIDE), 1) // HD
    out = full[:HD]
    for h in range(1, QUAD):
        out = jnp.where(lane_head == h, full[h * HD : (h + 1) * HD], out)
    return out


def key_rows(keys_at, b, count):
    return [pl.ds(pl.multiple_of(keys_at[b, i] * BLK, BLK), BLK) for i in range(count)]


def stacked(ref, places):
    return jnp.concatenate([ref[p, :] for p in places], axis=0)


def row_sums(x):
    return jnp.sum(x.reshape(x.shape[0] // 8, 8, WIDE), axis=0)


def for_steps(steps, body):
    for n in range(1, STEPS + 1):
        pl.when(steps == n)(functools.partial(body, n * STEP))


def forward_kernel(keys_at, steps_of, q_ref, k_ref, v_ref, bias_ref, out_ref, log_ref):
    def one_block(b, carry):
        rows = pl.ds(pl.multiple_of(b * BLK, BLK), BLK)

        def attend(count):
            places = key_rows(keys_at, b, count)
            query = head_diagonal(q_ref[rows, :])
            raw = dot_right_t(stacked(k_ref, places), query)
            scores, peak = [], None
            for i in range(count):
                piece = raw[i * BLK : (i + 1) * BLK] + bias_ref[b, i : i + 1, :]
                scores.append(piece)
                high = jnp.max(piece.reshape(BLK // 8, 8, WIDE), axis=0)
                peak = high if peak is None else jnp.maximum(peak, high)
            peak = jnp.max(peak, axis=0, keepdims=True)
            total, weights = None, []
            for piece in scores:
                exponent = jnp.exp(piece - peak)
                part = row_sums(exponent)
                total = part if total is None else total + part
                weights.append(exponent.astype(BF))
            total = jnp.sum(total, axis=0, keepdims=True)
            mix = dot_left_t(jnp.concatenate(weights, axis=0), stacked(v_ref, places))
            column = jnp.transpose(jnp.broadcast_to(total, (128, WIDE)))
            mix = mix / jnp.concatenate([column, column], axis=1)
            out_ref[rows, :] = diagonal_rows(mix).astype(BF)
            log_ref[b] = peak + jnp.log(total)

        for_steps(steps_of[b], attend)
        return carry

    lax.fori_loop(0, q_ref.shape[0] // BLK, one_block, 0)


def backward_kernel(
    keys_at,
    steps_of,
    q_ref,
    k_ref,
    v_ref,
    bias_ref,
    log_ref,
    d_ref,
    own_ref,
    in_ref,
    wk_ref,
    wv_ref,
    dq_ref,
    others_ref,
    grad_ref,
    dkey,
    dvalue,
    low,
    back_sum,
):
    dkey[...] = jnp.zeros_like(dkey)
    dvalue[...] = jnp.zeros_like(dvalue)

    def one_block(b, carry):
        rows = pl.ds(pl.multiple_of(b * BLK, BLK), BLK)

        def attend(count):
            places = key_rows(keys_at, b, count)
            query = head_diagonal(q_ref[rows, :])
            d_mixed = head_diagonal(d_ref[rows, :])
            logs = log_ref[b]
            keys = stacked(k_ref, places)
            raw = dot_right_t(keys, query)
            back = dot_right_t(stacked(v_ref, places), d_mixed)
            probs, inner = [], None
            for i in range(count):
                at = slice(i * BLK, (i + 1) * BLK)
                prob = jnp.exp(raw[at] + (bias_ref[b, i : i + 1, :] - logs))
                probs.append(prob)
                part = row_sums(prob * back[at])
                inner = part if inner is None else inner + part
            grad = dot(jnp.concatenate([p.astype(BF) for p in probs], axis=0), d_mixed)
            for i, p in enumerate(places):
                dvalue[p, :] += grad[i * BLK : (i + 1) * BLK]
            inner = jnp.sum(inner, axis=0, keepdims=True)
            d_score = jnp.concatenate(
                [
                    (prob * (back[i * BLK : (i + 1) * BLK] - inner)).astype(BF)
                    for i, prob in enumerate(probs)
                ],
                axis=0,
            )
            grad = dot(d_score, query)
            for i, p in enumerate(places):
                dkey[p, :] += grad[i * BLK : (i + 1) * BLK]
            d_query = dot_left_t(d_score, keys)
            dq_ref[rows, :] = (diagonal_rows(d_query) * (HD**-0.5)).astype(BF)

        for_steps(steps_of[b], attend)
        return carry

    lax.fori_loop(0, q_ref.shape[0] // BLK, one_block, 0)

    low[0] = dkey[...].astype(BF)
    low[1] = dvalue[...].astype(BF)
    grad_ref[:, :WIDE] = dot_left_t(own_ref[...], dq_ref[...]).astype(BF)
    grad_ref[:, WIDE : 2 * WIDE] = dot_left_t(in_ref[...], low[0]).astype(BF)
    grad_ref[:, 2 * WIDE :] = dot_left_t(in_ref[...], low[1]).astype(BF)
    quad = pl.program_id(0)

    def others(r, carry):
        at = pl.ds(pl.multiple_of(r * WIDE, WIDE), WIDE)
        part = dot_right_t(low[0, at, :], wk_ref[...]) + dot_right_t(low[1, at, :], wv_ref[...])
        so_far = jnp.where(quad == 0, jnp.zeros_like(part), back_sum[at, :]) + part
        back_sum[at, :] = so_far
        others_ref[at, :] = so_far.astype(BF)
        return carry

    lax.fori_loop(0, in_ref.shape[0] // WIDE, others, 0)


SHORT = pl.CostEstimate(flops=1_000_000, bytes_accessed=1_000_000, transcendentals=0)
MESH_ID = pl.DeviceIdType.MESH
CALL_GATHER_FIRST, CALL_GATHER, CALL_REDUCE, CALL_NORMS, CALL_ROWS, CALL_LINE_FFN, CALL_LINE_ATTN, CALL_BOTH = range(8)


def quad_places():
    me = lax.axis_index("quad")
    mate = me + 1 - 2 * (me % 2)
    return me, mate, (me + 2) % QUAD, (mate + 2) % QUAD


def greet(*peers):
    barrier = pltpu.get_barrier_semaphore()
    for peer in peers:
        pl.semaphore_signal(barrier, inc=1, device_id=peer, device_id_type=MESH_ID)
    pl.semaphore_wait(barrier, len(peers))


def block_at(block, size, start=0, rows=None):
    return pl.ds(pl.multiple_of(block * size + start, 16), size if rows is None else rows)


def line_peers(parts):
    plane = lax.axis_index("tensor")
    return [{"tensor": (plane + by) % parts} for by in range(1, parts)]


def lines_start(parts, groups, owns, outs, keep_sem, send_sem, recv_sem):
    peers = line_peers(parts)
    copies, kept, n = [], [], 0
    for count, out in zip(groups, outs):
        for kind in range(count):
            own = owns[n]
            width = own.shape[1]
            kept.append(
                pltpu.make_async_copy(own, out.at[:, pl.ds(kind * parts * width, width)], keep_sem.at[n])
            )
            kept[-1].start()
            for by in range(1, parts):
                copy = pltpu.make_async_remote_copy(
                    src_ref=own,
                    dst_ref=out.at[:, pl.ds((kind * parts + by) * width, width)],
                    send_sem=send_sem.at[n, by - 1],
                    recv_sem=recv_sem.at[n, by - 1],
                    device_id=peers[by - 1],
                    device_id_type=MESH_ID,
                )
                copy.start()
                copies.append(copy)
            n += 1
    return copies, kept


def lines_finish(copies, kept):
    for copy in copies + kept:
        copy.wait()


def lines_shapes(parts, groups):
    owns = [own for group in groups for own in group]
    shapes = [
        jax.ShapeDtypeStruct((group[0].shape[0], parts * len(group) * group[0].shape[1]), BF)
        for group in groups
    ]
    dma, count = pltpu.SemaphoreType.DMA, max(len(owns), 1)
    return owns, shapes, [dma((count,)), dma((count, parts - 1)), dma((count, parts - 1))]


def gather_kernel(pieces, parts_along, groups, *refs):
    count, lines = len(pieces), sum(groups)
    at = [count, count + lines, 2 * count + lines, 2 * count + lines + len(groups)]
    owns, line_owns = refs[: at[0]], refs[at[0] : at[1]]
    outs, line_outs = refs[at[1] : at[2]], refs[at[2] : at[3]]
    keep_sem, mate_send, mate_recv, far_send, far_recv, on_send, on_recv = refs[at[3] : at[3] + 7]
    me, mate, far, cross = quad_places()
    greet({"quad": mate}, {"quad": far}, *(line_peers(parts_along) if groups else []))

    def send(source, target, sends, recvs, at, peer):
        return pltpu.make_async_remote_copy(
            src_ref=source,
            dst_ref=target,
            send_sem=sends.at[at],
            recv_sem=recvs.at[at],
            device_id={"quad": peer},
            device_id_type=MESH_ID,
        )

    parts = []
    for n in range(count):
        size = owns[n].shape[0]
        step = size // pieces[n]
        for p in range(pieces[n]):
            parts.append((n, size, p * step, step))
    to_far = [
        send(owns[n].at[pl.ds(start, step)], outs[n].at[block_at(me, size, start, step)], far_send, far_recv, i, far)
        for i, (n, size, start, step) in enumerate(parts)
    ]
    for copy in to_far:
        copy.start()
    to_mate = [
        send(owns[n], outs[n].at[block_at(me, owns[n].shape[0])], mate_send, mate_recv, n, mate)
        for n in range(count)
    ]
    for copy in to_mate:
        copy.start()
    along = lines_start(parts_along, groups, line_owns, line_outs, *refs[at[3] + 7 :])
    kept = [
        pltpu.make_async_copy(owns[n], outs[n].at[block_at(me, owns[n].shape[0])], keep_sem.at[n])
        for n in range(count)
    ]
    for copy in kept:
        copy.start()
    onward = []
    for i, (n, size, start, step) in enumerate(parts):
        to_far[i].wait_recv()
        came = outs[n].at[block_at(far, size, start, step)]
        copy = send(came, came, on_send, on_recv, i, mate)
        copy.start()
        onward.append(copy)
    for copy in to_mate + onward:
        copy.wait()
    for copy in to_far:
        copy.wait_send()
    for copy in kept:
        copy.wait()
    lines_finish(*along)


def quad_gather(arrays, pieces, call, parts=1, groups=()):
    count, total = len(arrays), sum(pieces)
    sems = [pltpu.SemaphoreType.DMA((k,)) for k in (count, count, count, total, total, total, total)]
    owns, shapes, line_sems = lines_shapes(max(parts, 2), groups)
    return pl.pallas_call(
        functools.partial(gather_kernel, pieces, parts, tuple(len(g) for g in groups)),
        out_shape=[jax.ShapeDtypeStruct((QUAD * x.shape[0],) + x.shape[1:], x.dtype) for x in arrays]
        + shapes,
        in_specs=[pl.BlockSpec(memory_space=pltpu.VMEM)] * (count + len(owns)),
        out_specs=[pl.BlockSpec(memory_space=pl.ANY)] * (count + len(shapes)),
        scratch_shapes=sems + line_sems,
        compiler_params=pltpu.CompilerParams(collective_id=call, has_side_effects=True),
        cost_estimate=SHORT,
        name="quad_gather",
    )(*arrays, *owns)


REDUCE_PIECES = 4


def reduce_kernel(
    parts_ref,
    out_ref,
    near,
    relay,
    beyond,
    mate_send,
    mate_recv,
    own_send,
    own_recv,
    far_send,
    far_recv,
    greeted=False,
):
    me, mate, far, cross = quad_places()
    if not greeted:
        greet({"quad": mate}, {"quad": far})
    size = out_ref.shape[0]
    step = size // REDUCE_PIECES

    def send(source, target, send_sem, recv_sem, peer):
        copy = pltpu.make_async_remote_copy(
            src_ref=source,
            dst_ref=target,
            send_sem=send_sem,
            recv_sem=recv_sem,
            device_id={"quad": peer},
            device_id_type=MESH_ID,
        )
        copy.start()
        return copy

    to_mate = [
        send(
            parts_ref.at[block_at(cross, size, p * step, step)],
            near.at[1, pl.ds(p * step, step)],
            mate_send.at[p],
            mate_recv.at[p],
            mate,
        )
        for p in range(REDUCE_PIECES)
    ]
    own = send(parts_ref.at[block_at(mate, size)], near.at[0], own_send, own_recv, mate)
    to_far = []
    for p in range(REDUCE_PIECES):
        rows = pl.ds(p * step, step)
        to_mate[p].wait_recv()
        mine = parts_ref[block_at(far, size, p * step, step), :].astype(F32)
        relay[rows, :] = (mine + near[1, rows, :].astype(F32)).astype(BF)
        to_far.append(send(relay.at[rows], beyond.at[rows], far_send.at[p], far_recv.at[p], far))
    own.wait_recv()
    for p in range(REDUCE_PIECES):
        rows = pl.ds(p * step, step)
        to_far[p].wait_recv()
        mine = parts_ref[block_at(me, size, p * step, step), :].astype(F32)
        out_ref[rows, :] = mine + near[0, rows, :].astype(F32) + beyond[rows, :].astype(F32)
    for copy in to_mate + [own] + to_far:
        copy.wait_send()


def reduce_scratch(rows, width):
    one, each = pltpu.SemaphoreType.DMA, pltpu.SemaphoreType.DMA((REDUCE_PIECES,))
    low = pltpu.VMEM((rows, width), BF)
    return [pltpu.VMEM((2, rows, width), BF), low, low, each, each, one, one, each, each]


def quad_reduce(parts):
    rows, width = parts.shape[0] // QUAD, parts.shape[1]
    return pl.pallas_call(
        reduce_kernel,
        out_shape=jax.ShapeDtypeStruct((rows, width), F32),
        in_specs=[pl.BlockSpec(memory_space=pltpu.VMEM)],
        out_specs=pl.BlockSpec(memory_space=pltpu.VMEM),
        scratch_shapes=reduce_scratch(rows, width),
        compiler_params=pltpu.CompilerParams(collective_id=CALL_REDUCE, has_side_effects=True),
        cost_estimate=SHORT,
        name="quad_reduce",
    )(parts)


def both_kernel(sizes, planes, parts_ref, *refs):
    count = len(sizes)
    x_refs, out_ref, line_refs, scratch = refs[:count], refs[count], refs[count + 1 :][:count], refs[2 * count + 1 :]
    me, mate, far, cross = quad_places()
    greet({"quad": mate}, {"quad": far}, *line_peers(planes))
    lines = []
    for n in range(count):
        held, came, send_sem, recv_sem = scratch[4 * n : 4 * n + 4]
        lines.append((came, line_start(sizes[n], planes, x_refs[n], held, came, send_sem, recv_sem)))
    reduce_kernel(parts_ref, out_ref, *scratch[4 * count :], greeted=True)
    for n in range(count):
        line_finish(sizes[n], planes, x_refs[n], line_refs[n], *lines[n])


def quad_reduce_and_lines(parts, lines, sizes, planes):
    rows, width = parts.shape[0] // QUAD, parts.shape[1]
    shapes = [(x.shape[0], sum(own)) for x, own in zip(lines, sizes)]
    vmem, count = pl.BlockSpec(memory_space=pltpu.VMEM), len(lines)
    return pl.pallas_call(
        functools.partial(both_kernel, tuple(sizes), planes),
        out_shape=[jax.ShapeDtypeStruct((rows, width), F32)]
        + [jax.ShapeDtypeStruct(shape, F32) for shape in shapes],
        in_specs=[vmem] * (1 + count),
        out_specs=[vmem] * (1 + count),
        scratch_shapes=sum([line_scratch(shape, planes) for shape in shapes], [])
        + reduce_scratch(rows, width),
        compiler_params=pltpu.CompilerParams(collective_id=CALL_BOTH, has_side_effects=True),
        cost_estimate=SHORT,
        name="quad_reduce_and_lines",
    )(parts, *lines)


def norms_kernel(hops, x_ref, out_ref, held, came, send_sem, recv_sem):
    peers = []
    for axis, bit in hops:
        at = lax.axis_index(axis)
        peers.append({axis: at + bit - 2 * bit * ((at // bit) % 2)})
    greet(*peers)
    for n, peer in enumerate(peers):
        source = x_ref if n == 0 else held.at[n]
        copy = pltpu.make_async_remote_copy(
            src_ref=source,
            dst_ref=came.at[n],
            send_sem=send_sem.at[n],
            recv_sem=recv_sem.at[n],
            device_id=peer,
            device_id_type=MESH_ID,
        )
        copy.start()
        copy.wait()
        total = source[...] + came[n]
        if n == len(peers) - 1:
            out_ref[...] = total
        else:
            held[n + 1] = total


def sum_everywhere(x):
    hops = []
    for axis in ("quad", "row", "tensor", "hi"):
        bit = 1
        while bit < lax.axis_size(axis):
            hops.append((axis, bit))
            bit *= 2
    vmem = pltpu.VMEM((len(hops),) + x.shape, x.dtype)
    return pl.pallas_call(
        functools.partial(norms_kernel, tuple(hops)),
        out_shape=jax.ShapeDtypeStruct(x.shape, x.dtype),
        in_specs=[pl.BlockSpec(memory_space=pltpu.VMEM)],
        out_specs=pl.BlockSpec(memory_space=pltpu.VMEM),
        scratch_shapes=[
            vmem,
            vmem,
            pltpu.SemaphoreType.DMA((len(hops),)),
            pltpu.SemaphoreType.DMA((len(hops),)),
        ],
        compiler_params=pltpu.CompilerParams(collective_id=CALL_NORMS, has_side_effects=True),
        cost_estimate=SHORT,
        name="sum_everywhere",
    )(x)


def rows_kernel(parts, groups, own_ref, *refs):
    lines = sum(groups)
    line_owns, out_ref, line_outs = refs[:lines], refs[lines], refs[lines + 1 : lines + 1 + len(groups)]
    keep_sem, line_send, line_recv, send_sem, recv_sem = refs[lines + 1 + len(groups) :][:5]
    line_sems = refs[lines + 1 + len(groups) :][5:]
    me, mate, far, cross = quad_places()
    row, plane = lax.axis_index("row"), lax.axis_index("tensor")
    other = 1 - row
    line = [{"tensor": (plane + by) % parts} for by in range(1, parts)]
    to_x, to_y, to_mate = {"quad": far}, {"row": other}, {"quad": mate}
    greet(*line, to_x, to_y, to_mate)
    size, width = own_ref.shape

    def block(at_row, at_quad, part):
        return out_ref.at[block_at(at_row * QUAD + at_quad, size), pl.ds(part * width, width)]

    used = []

    def send(source, target, peer, n):
        copy = pltpu.make_async_remote_copy(
            src_ref=source,
            dst_ref=target,
            send_sem=send_sem.at[n],
            recv_sem=recv_sem.at[n],
            device_id=peer,
            device_id_type=MESH_ID,
        )
        copy.start()
        used.append(copy)
        return copy

    along = []
    for by in range(1, parts):
        copy = pltpu.make_async_remote_copy(
            src_ref=own_ref,
            dst_ref=block(row, me, by),
            send_sem=line_send.at[by - 1],
            recv_sem=line_recv.at[by - 1],
            device_id=line[by - 1],
            device_id_type=MESH_ID,
        )
        copy.start()
        along.append(copy)
    keep = pltpu.make_async_copy(own_ref, block(row, me, 0), keep_sem)
    keep.start()
    only_line = lines_start(parts, groups, line_owns, line_outs, *line_sems)
    near_x, near_y, beyond, mates = [], [], [], []
    for part in range(parts + 1):
        if part < parts:
            if part:
                along[part - 1].wait_recv()
            source = own_ref if part == 0 else block(row, me, part)
            target = block(row, me, part)
            near_x.append(send(source, target, to_x, part))
            near_y.append(send(source, target, to_y, parts + part))
            mates.append(send(source, target, to_mate, 2 * parts + part))
        if part:
            done = part - 1
            from_x, from_y = block(row, far, done), block(other, me, done)
            near_x[done].wait_recv()
            near_y[done].wait_recv()
            if done % 2:
                beyond.append(send(from_y, from_y, to_x, 3 * parts + done))
            else:
                beyond.append(send(from_x, from_x, to_y, 3 * parts + done))
            mates.append(send(from_x, from_x, to_mate, 4 * parts + done))
            mates.append(send(from_y, from_y, to_mate, 5 * parts + done))
    for part in range(parts):
        beyond[part].wait_recv()
        came = block(other, far, part)
        mates.append(send(came, came, to_mate, 6 * parts + part))
    for copy in mates:
        copy.wait_recv()
    for copy in along + used:
        copy.wait_send()
    keep.wait()
    lines_finish(*only_line)


def gather_rows(rows, parts, groups):
    size, width = rows.shape
    dma = pltpu.SemaphoreType.DMA
    owns, shapes, line_sems = lines_shapes(parts, groups)
    return pl.pallas_call(
        functools.partial(rows_kernel, parts, tuple(len(g) for g in groups)),
        out_shape=[jax.ShapeDtypeStruct((ROW * QUAD * size, parts * width), rows.dtype)] + shapes,
        in_specs=[pl.BlockSpec(memory_space=pltpu.VMEM)] * (1 + len(owns)),
        out_specs=[pl.BlockSpec(memory_space=pl.ANY)] * (1 + len(shapes)),
        scratch_shapes=[dma, dma((parts - 1,)), dma((parts - 1,)), dma((7 * parts,)), dma((7 * parts,))]
        + line_sems,
        compiler_params=pltpu.CompilerParams(collective_id=CALL_ROWS, has_side_effects=True),
        cost_estimate=SHORT,
        name="gather_rows",
    )(rows, *owns)


def regroup_kernel(parts, kinds, x_ref, out_ref):
    size = x_ref.shape[1] // (parts * kinds)
    for kind in range(kinds):
        for part in range(parts):
            to, at = (kind * parts + part) * size, (part * kinds + kind) * size
            out_ref[:, to : to + size] = x_ref[:, at : at + size]


def regroup(rows, parts, kinds):
    steps = max(rows.shape[0] // 192, 1)
    block = pl.BlockSpec((rows.shape[0] // steps, rows.shape[1]), lambda i: (i, 0))
    return pl.pallas_call(
        functools.partial(regroup_kernel, parts, kinds),
        out_shape=jax.ShapeDtypeStruct(rows.shape, rows.dtype),
        grid=(steps,),
        in_specs=[block],
        out_specs=block,
        cost_estimate=SHORT,
        name="regroup",
    )(rows)


def line_pick(sizes, parts, x_ref, part):
    columns, start = [], 0
    for size in sizes:
        columns.append(x_ref[:, start + part * size : start + (part + 1) * size])
        start += parts * size
    return jnp.concatenate(columns, axis=1)


def line_start(sizes, parts, x_ref, held, came, send_sem, recv_sem):
    plane = lax.axis_index("tensor")
    copies = []
    for by in range(1, parts):
        held[by - 1] = line_pick(sizes, parts, x_ref, by)
        copy = pltpu.make_async_remote_copy(
            src_ref=held.at[by - 1],
            dst_ref=came.at[by - 1],
            send_sem=send_sem.at[by - 1],
            recv_sem=recv_sem.at[by - 1],
            device_id={"tensor": (plane + parts - by) % parts},
            device_id_type=MESH_ID,
        )
        copy.start()
        copies.append(copy)
    return copies


def line_finish(sizes, parts, x_ref, out_ref, came, copies):
    total = line_pick(sizes, parts, x_ref, 0).astype(F32)
    for by in range(1, parts):
        copies[by - 1].wait_recv()
        total = total + came[by - 1].astype(F32)
    out_ref[...] = total
    for copy in copies:
        copy.wait_send()


def line_scratch(shape, parts):
    dma = pltpu.SemaphoreType.DMA((parts - 1,))
    return [pltpu.VMEM((parts - 1,) + shape, BF), pltpu.VMEM((parts - 1,) + shape, BF), dma, dma]


def parts_kernel(sizes, parts, x_ref, out_ref, held, came, send_sem, recv_sem):
    greet(*line_peers(parts))
    copies = line_start(sizes, parts, x_ref, held, came, send_sem, recv_sem)
    line_finish(sizes, parts, x_ref, out_ref, came, copies)


def sum_line(rows, sizes, parts, call):
    shape = (rows.shape[0], sum(sizes))
    return pl.pallas_call(
        functools.partial(parts_kernel, sizes, parts),
        out_shape=jax.ShapeDtypeStruct(shape, F32),
        in_specs=[pl.BlockSpec(memory_space=pltpu.VMEM)],
        out_specs=pl.BlockSpec(memory_space=pltpu.VMEM),
        scratch_shapes=line_scratch(shape, parts),
        compiler_params=pltpu.CompilerParams(collective_id=call, has_side_effects=True),
        cost_estimate=SHORT,
        name="sum_line",
    )(rows)


def attend_forward(query, keyval, tables):
    keys_at, steps_of, bias = tables
    own, width = query.shape
    quads = width // WIDE
    rows = keyval.shape[0]
    blocks = own // BLK
    return pl.pallas_call(
        forward_kernel,
        grid_spec=pltpu.PrefetchScalarGridSpec(
            num_scalar_prefetch=2,
            grid=(quads,),
            in_specs=[
                pl.BlockSpec((own, WIDE), lambda i, *_: (0, i)),
                pl.BlockSpec((rows, WIDE), lambda i, *_: (0, i)),
                pl.BlockSpec((rows, WIDE), lambda i, *_: (0, i + quads)),
                pl.BlockSpec((blocks, LONGEST, WIDE), lambda i, *_: (0, 0, i)),
            ],
            out_specs=[
                pl.BlockSpec((own, WIDE), lambda i, *_: (0, i)),
                pl.BlockSpec((blocks, 1, WIDE), lambda i, *_: (0, 0, i)),
            ],
        ),
        out_shape=[
            jax.ShapeDtypeStruct((own, width), BF),
            jax.ShapeDtypeStruct((blocks, 1, width), F32),
        ],
        cost_estimate=SHORT,
        name="attend_forward",
    )(keys_at, steps_of, query, keyval, keyval, bias)


def attend_backward(query, keyval, logs, d_mixed, tables, own_inputs, inputs, attn_w):
    keys_at, steps_of, bias = tables
    own, width = query.shape
    quads = width // WIDE
    rows, depth = inputs.shape
    blocks = own // BLK
    once = pl.Buffered(1)
    return pl.pallas_call(
        backward_kernel,
        grid_spec=pltpu.PrefetchScalarGridSpec(
            num_scalar_prefetch=2,
            grid=(quads,),
            in_specs=[
                pl.BlockSpec((own, WIDE), lambda i, *_: (0, i)),
                pl.BlockSpec((rows, WIDE), lambda i, *_: (0, i)),
                pl.BlockSpec((rows, WIDE), lambda i, *_: (0, i + quads)),
                pl.BlockSpec((blocks, LONGEST, WIDE), lambda i, *_: (0, 0, i)),
                pl.BlockSpec((blocks, 1, WIDE), lambda i, *_: (0, 0, i)),
                pl.BlockSpec((own, WIDE), lambda i, *_: (0, i)),
                pl.BlockSpec((own, depth), lambda i, *_: (0, 0), pipeline_mode=once),
                pl.BlockSpec((rows, depth), lambda i, *_: (0, 0), pipeline_mode=once),
                pl.BlockSpec((depth, WIDE), lambda i, *_: (0, i + quads)),
                pl.BlockSpec((depth, WIDE), lambda i, *_: (0, i + 2 * quads)),
            ],
            out_specs=[
                pl.BlockSpec((own, WIDE), lambda i, *_: (0, i)),
                pl.BlockSpec((rows, depth), lambda i, *_: (0, 0)),
                pl.BlockSpec((depth, 3 * WIDE), lambda i, *_: (0, i)),
            ],
            scratch_shapes=[
                pltpu.VMEM((rows, WIDE), F32),
                pltpu.VMEM((rows, WIDE), F32),
                pltpu.VMEM((2, rows, WIDE), BF),
                pltpu.VMEM((rows, depth), F32),
            ],
        ),
        out_shape=[
            jax.ShapeDtypeStruct((own, width), BF),
            jax.ShapeDtypeStruct((rows, depth), BF),
            jax.ShapeDtypeStruct((depth, 3 * width), BF),
        ],
        cost_estimate=SHORT,
        name="attend_backward",
    )(keys_at, steps_of, query, keyval, keyval, bias, logs, d_mixed, own_inputs, inputs, attn_w, attn_w)


def weights_kernel(steps, ffn_ref, two_ref, one_ref, pre_ref, act_ref, mixed_ref, out_ref, left):
    i = pl.program_id(0)
    for start, ref in ((0, ffn_ref), (steps, two_ref), (2 * steps, one_ref)):

        @pl.when(i == start)
        def _():
            left[...] = jnp.transpose(ref[...])

    for start, ref in ((0, pre_ref), (steps, act_ref), (2 * steps, mixed_ref)):

        @pl.when((i >= start) & (i < start + steps))
        def _():
            out_ref[...] = dot(left[...], ref[...]).astype(BF)


def weight_grads(ffn_in, d_two, d_one, d_pre, activated, mixed):
    own, depth = ffn_in.shape
    steps = d_pre.shape[1] // depth
    last = steps - 1
    whole = pl.BlockSpec((own, depth), lambda i: (0, 0), pipeline_mode=pl.Buffered(1))
    return pl.pallas_call(
        functools.partial(weights_kernel, steps),
        grid=(2 * steps + 1,),
        in_specs=[
            whole,
            whole,
            whole,
            pl.BlockSpec((own, depth), lambda i: (0, jnp.minimum(i, last))),
            pl.BlockSpec((own, depth), lambda i: (0, jnp.clip(i - steps, 0, last))),
            whole,
        ],
        out_specs=pl.BlockSpec((depth, depth), lambda i: (0, i)),
        out_shape=jax.ShapeDtypeStruct((depth, (2 * steps + 1) * depth), BF),
        scratch_shapes=[pltpu.VMEM((depth, own), BF)],
        cost_estimate=SHORT,
        name="weight_grads",
    )(ffn_in, d_two, d_one, d_pre, activated, mixed)


def attention_tables(doc_lengths, block_deal, random_rows, own_blocks, first_own):
    blocks = block_deal.shape[0]
    doc_ends = jnp.cumsum(doc_lengths)
    doc_starts = doc_ends - doc_lengths
    place = jnp.arange(blocks, dtype=jnp.int32)
    stored_at = jnp.sum(
        jnp.where(block_deal[None, :] == place[:, None], place[None, :], 0), axis=1
    )
    own = lax.dynamic_slice(block_deal, (first_own,), (own_blocks,))
    doc_index = jnp.sum((own[:, None] >= doc_ends[None, :]).astype(jnp.int32), axis=1)
    doc_pick = (
        doc_index[:, None] == jnp.arange(doc_lengths.shape[0], dtype=jnp.int32)[None, :]
    ).astype(jnp.int32)
    first_block = jnp.sum(doc_pick * doc_starts[None, :], axis=1)
    doc_blocks = jnp.sum(doc_pick * doc_lengths[None, :], axis=1)
    local = own - first_block
    other = jnp.arange(LONGEST, dtype=jnp.int32)
    wanted = jnp.minimum(first_block[:, None] + other[None, :], blocks - 1)
    keys_at = jnp.sum(
        jnp.where(wanted[:, :, None] == place[None, None, :], stored_at[None, None, :], 0), axis=2
    )
    own_pick = (own[:, None] == place[None, :]).astype(jnp.int32)
    picks = jnp.sum(own_pick[None, :, :, None] * random_rows[:, None, :, :], axis=2)
    picks = jnp.remainder(picks, doc_blocks[None, :, None])
    random_hit = jnp.any(picks[:, :, :, None] == other[None, None, None, :], axis=2)
    inside = other[None, :] < doc_blocks[:, None]
    near = jnp.abs(local[:, None] - other[None, :]) <= 1
    everywhere = (local[:, None] < 2) | (other[None, :] < 2)
    allowed = inside[None] & ((near | everywhere)[None] | random_hit)
    bias = jnp.where(allowed, 0.0, MASK_VALUE).astype(F32)
    bias = jnp.repeat(bias.transpose(1, 2, 0), BLK, axis=2)
    steps_of = (doc_blocks + STEP - 1) // STEP
    return keys_at, steps_of, bias


def to_home(steps, parts):
    pairs = []
    for hi in range(steps):
        for row in range(ROW):
            for quad in range(QUAD):
                side, core = quad // 2, quad % 2
                plane = parts - 1 - side if core else side
                for part in range(parts):
                    source = ((hi * ROW + row) * QUAD + quad) * parts + part
                    target = ((hi * ROW + row) * QUAD + part) * parts + plane
                    pairs.append((source, target))
    return pairs


def local(
    layer_input,
    w_qkv,
    w_out,
    w_up,
    w_down,
    attn_gain,
    attn_shift,
    ffn_gain,
    ffn_shift,
    out_grad,
    doc_lengths,
    block_deal,
    random_blocks,
):
    own_rows, width = layer_input.shape
    tensor = lax.axis_size("tensor")
    slot = lax.axis_index("quad")
    plane = lax.axis_index("tensor")
    head_local = random_blocks.shape[1]
    chunk = head_local * HD
    depth = w_qkv.shape[1]
    hidden = w_up.shape[2]
    score_scale = HD ** (-0.5)
    moves = to_home(lax.axis_size("hi"), tensor)
    moves_back = [(b, a) for a, b in moves]

    def shifted(x, by):
        return lax.ppermute(x, "tensor", [(i, (i + by) % tensor) for i in range(tensor)])

    def spread(shard):
        return [shard] + [shifted(shard, by) for by in range(1, tensor)]

    def by_kind(parts, kinds):
        rows = jnp.stack([part.reshape(depth, kinds, -1) for part in parts], axis=2)
        return rows.reshape(depth, -1)

    def attn_shard(qkv, back):
        qkv = qkv.reshape(depth, head_local, 3, HD).transpose(0, 2, 1, 3)
        return jnp.concatenate([qkv.reshape(depth, 3 * chunk), back.T], axis=1)

    def over_data(rows):
        return lax.all_gather(rows, DATA, axis=0, tiled=True)

    docs, group_blocks = doc_lengths.shape[1], block_deal.shape[1]
    numbers = jnp.concatenate([doc_lengths[0], block_deal[0], random_blocks[0].reshape(-1)])
    numbers = jnp.stack([numbers // BLK, numbers % BLK]).astype(BF)
    numbers = jnp.pad(numbers, ((0, 14), (0, width - numbers.shape[1])))
    own_numbers = lax.ppermute(numbers, EVERY, moves)
    own_tokens = lax.ppermute(layer_input, EVERY, moves)
    ffn_shards = [w_up[0], w_down[0].T]
    if lax.axis_size("hi") == 1:
        rows, first_rows = gather_rows(attn_shard(w_qkv[0], w_out[0]), tensor, [ffn_shards])
        rows, first_rows, own_tokens, own_numbers = lax.optimization_barrier(
            (rows, first_rows, own_tokens, own_numbers)
        )
        attn_full = [regroup(rows, tensor, 4)]
    else:
        attn_full = [over_data(by_kind(spread(attn_shard(w_qkv[0], w_out[0])), 4))]
        first_rows = by_kind(spread(jnp.concatenate(ffn_shards, axis=1)), 2)
    ffn_full = [over_data(first_rows)]

    groups = []
    for layer in range(1, LAYERS):
        groups += [[attn_shard(w_qkv[layer], w_out[layer])], [w_up[layer], w_down[layer].T]]
    inputs, numbers, *later = quad_gather(
        [own_tokens, own_numbers], [4, 1], CALL_GATHER_FIRST, tensor, groups
    )
    numbers = numbers.reshape(QUAD, 16, width)[:, :2].astype(jnp.int32)
    numbers = numbers[:, 0] * BLK + numbers[:, 1]
    lengths, deal = numbers[0, :docs], numbers[0, docs : docs + group_blocks]
    random_home = numbers[:, docs + group_blocks :][:, : random_blocks.size]
    random_home = random_home.reshape(tensor, head_local, group_blocks, -1)
    part_of = (plane - jnp.arange(tensor, dtype=jnp.int32)) % tensor
    part_pick = (part_of[:, None] == jnp.arange(tensor, dtype=jnp.int32)[None, :]).astype(jnp.int32)
    random_home = jnp.sum(part_pick[:, :, None, None, None] * random_home[None], axis=1)
    random_home = random_home.reshape(tensor * head_local, group_blocks, -1)
    own_blocks = own_rows // BLK
    tables = attention_tables(
        lengths,
        deal,
        random_home,
        own_blocks,
        slot * own_blocks,
    )

    stream = own_tokens.astype(F32)
    stored = []
    for layer in range(LAYERS):
        attn_w, ffn_w = attn_full[layer], ffn_full[layer]
        w_query = attn_w[:, :width]
        w_keyval = attn_w[:, width : 3 * width]
        w_back_t = attn_w[:, 3 * width :]
        w_expand = ffn_w[:, : hidden * tensor]
        w_shrink_t = ffn_w[:, hidden * tensor :]
        own_inputs = stream.astype(BF)
        if layer > 0:
            (inputs,) = quad_gather([own_inputs], [4], CALL_GATHER)
        query = (dot(own_inputs, w_query).astype(BF).astype(F32) * score_scale).astype(BF)
        keyval = dot(inputs, w_keyval).astype(BF)
        if layer < LAYERS - 1:
            attn_full.append(over_data(regroup(later[2 * layer], tensor, 4)))
            ffn_full.append(over_data(later[2 * layer + 1]))
        mixed, logs = attend_forward(query, keyval, tables)
        if layer == 0:
            mixed, own_grad = lax.optimization_barrier((mixed, out_grad))
            own_grad = lax.ppermute(own_grad, EVERY, moves)
        summed_one = stream + dot_right_t(mixed, w_back_t)
        normed = layer_norm(summed_one, attn_gain[layer], attn_shift[layer])
        ffn_in = normed.astype(BF)
        pre_act = dot(ffn_in, w_expand)
        activated = gelu_tanh(pre_act).astype(BF)
        summed_two = normed + dot_right_t(activated, w_shrink_t)
        stored.append(
            (own_inputs, inputs, query, keyval, mixed, logs, summed_one, ffn_in, pre_act, activated, summed_two)
        )
        stream = layer_norm(summed_two, ffn_gain[layer], ffn_shift[layer])
    layer_output = lax.ppermute(stream.astype(BF), EVERY, moves_back)

    def line_parts(rows, sizes):
        pieces, start = [], 0
        for size in sizes:
            pieces.append(rows[:, start : start + tensor * size].reshape(depth, tensor, size))
            start += tensor * size
        parts = [jnp.concatenate([p[:, by] for p in pieces], axis=1) for by in range(tensor)]
        return parts[:1] + [shifted(parts[by], tensor - by) for by in range(1, tensor)]

    def by_piece(rows):
        rows = rows.reshape(depth, -1, 3, WIDE).transpose(0, 2, 1, 3)
        return rows.reshape(depth, 3 * width)

    def sum_data(part):
        return lax.psum_scatter(part, DATA, scatter_dimension=0, tiled=True)

    state_grad = own_grad.astype(F32)
    attn_sums = [None] * LAYERS
    attn_grads = [None] * LAYERS
    ffn_grads = [None] * LAYERS
    norm_parts = [None] * LAYERS
    for layer in reversed(range(LAYERS)):
        (own_inputs, inputs, query, keyval, mixed, logs, summed_one, ffn_in, pre_act, activated, summed_two) = stored[layer]
        attn_w, ffn_w = attn_full[layer], ffn_full[layer]
        w_query = attn_w[:, :width]
        w_keyval = attn_w[:, width : 3 * width]
        w_back_t = attn_w[:, 3 * width :]
        w_expand = ffn_w[:, : hidden * tensor]
        w_shrink_t = ffn_w[:, hidden * tensor :]
        unused_two, ffn_back = jax.vjp(layer_norm, summed_two, ffn_gain[layer], ffn_shift[layer])
        d_two, ffn_gain_part, ffn_shift_part = ffn_back(state_grad)
        d_two_low = d_two.astype(BF)
        unused_act, gelu_back = jax.vjp(gelu_tanh, pre_act)
        d_pre = gelu_back(dot(d_two_low, w_shrink_t))[0].astype(BF)
        d_normed = d_two + dot_right_t(d_pre, w_expand)
        unused_one, attn_back = jax.vjp(layer_norm, summed_one, attn_gain[layer], attn_shift[layer])
        d_one, attn_gain_part, attn_shift_part = attn_back(d_normed)
        norm_parts[layer] = (attn_gain_part, attn_shift_part, ffn_gain_part, ffn_shift_part)
        d_one_low = d_one.astype(BF)
        ffn_part = weight_grads(ffn_in, d_two_low, d_one_low, d_pre, activated, mixed)
        d_one_low, ffn_part = lax.optimization_barrier((d_one_low, ffn_part))
        ffn_sum = sum_data(ffn_part)
        d_mixed = dot(d_one_low, w_back_t).astype(BF)
        if layer < LAYERS - 1:
            norms = jnp.stack([norm_parts[l][k] for k in range(4) for l in range(LAYERS)])
            d_mixed, norms = lax.optimization_barrier((d_mixed, norms))
            norm_sums = sum_everywhere(norms)
            d_mixed, norm_sums, attn_sums[layer + 1] = lax.optimization_barrier(
                (d_mixed, norm_sums, attn_sums[layer + 1])
            )
        if layer == 0:
            d_mixed, ffn_last = lax.optimization_barrier((d_mixed, ffn_last))
            moving = line_parts(ffn_last, (hidden, hidden, chunk))
        d_query, others, attn_part = attend_backward(
            query, keyval, logs, d_mixed, tables, own_inputs, inputs, attn_w
        )
        if layer == 0:
            others, attn_sums[1] = lax.optimization_barrier((others, attn_sums[1]))
            attn_grads[1] = sum_line(by_piece(attn_sums[1]), (chunk,) * 3, tensor, CALL_LINE_ATTN)
            others, ffn_sum, attn_part, attn_grads[1], moving = lax.optimization_barrier(
                (others, ffn_sum, attn_part, attn_grads[1], moving)
            )
            ffn_grads[1] = sum(part.astype(F32) for part in moving)
        else:
            others, layer_output = lax.optimization_barrier((others, layer_output))
        if layer == 0:
            summed, ffn_grads[0] = quad_reduce_and_lines(
                others, [ffn_sum], [(hidden, hidden, chunk)], tensor
            )
        else:
            summed = quad_reduce(others)
            summed, ffn_sum, attn_part = lax.optimization_barrier((summed, ffn_sum, attn_part))
        ffn_last = ffn_sum
        attn_sums[layer] = sum_data(attn_part)
        state_grad = d_one + dot_right_t(d_query, w_query) + summed
    input_grad = lax.ppermute(state_grad.astype(BF), EVERY, moves_back)
    attn_grads[0] = sum_line(by_piece(attn_sums[0]), (chunk,) * 3, tensor, CALL_LINE_ATTN)
    input_grad, attn_grads = lax.optimization_barrier((input_grad, attn_grads))
    input_grad = input_grad.astype(F32)

    qkv_grad = jnp.stack(attn_grads).reshape(LAYERS, depth, 3, head_local, HD)
    qkv_grad = qkv_grad.transpose(0, 1, 3, 2, 4).reshape(LAYERS, depth, 3 * chunk)
    ffn_own = jnp.stack(ffn_grads)
    up_grad = ffn_own[:, :, :hidden]
    down_grad = ffn_own[:, :, hidden : 2 * hidden].transpose(0, 2, 1)
    out_w_grad = ffn_own[:, :, 2 * hidden :].transpose(0, 2, 1)
    return (layer_output, input_grad, qkv_grad, out_w_grad, up_grad, down_grad) + tuple(
        norm_sums[k * LAYERS : (k + 1) * LAYERS] for k in range(4)
    )


def solution(mesh):
    devices = mesh.devices
    tensor = devices.shape[1]
    split = jax.sharding.Mesh(
        devices.reshape(devices.shape[0] // (ROW * QUAD), ROW, QUAD, tensor), EVERY
    )
    placed = (
        P(EVERY, None),
        P(None, DATA, "tensor"),
        P(None, "tensor", DATA),
        P(None, DATA, "tensor"),
        P(None, "tensor", DATA),
        P(),
        P(),
        P(),
        P(),
        P(EVERY, None),
        P(DATA, None),
        P(DATA, None),
        P(DATA, "tensor", None, None),
    )
    return jax.shard_map(
        local,
        mesh=split,
        in_specs=placed,
        out_specs=(
            P(EVERY, None),
            P(EVERY, None),
            P(None, DATA, "tensor"),
            P(None, "tensor", DATA),
            P(None, DATA, "tensor"),
            P(None, "tensor", DATA),
            P(),
            P(),
            P(),
            P(),
        ),
        check_vma=False,
    )
```

```python
import functools

import jax
import jax.numpy as jnp
from jax import lax
from jax.experimental import pallas as pl
from jax.experimental.pallas import tpu as pltpu
from jax.sharding import PartitionSpec as P

HD = 64
BLK = 64
LAYERS = 2
LONGEST = 16
QUAD = 4
WIDE = QUAD * HD
STEP = 4
STEPS = LONGEST // STEP

ROW = 2
DATA = ("hi", "row", "quad")
EVERY = DATA + ("tensor",)

NORM_EPSILON = 1e-12
MASK_VALUE = -1e30
BF = jnp.bfloat16
F32 = jnp.float32


def layer_norm(summed, norm_gain, norm_shift):
    row_mean = jnp.mean(summed, axis=-1, keepdims=True)
    centred = summed - row_mean
    row_var = jnp.mean(centred * centred, axis=-1, keepdims=True)
    return centred * lax.rsqrt(row_var + NORM_EPSILON) * norm_gain + norm_shift


def gelu_tanh(values):
    return jax.nn.gelu(values, approximate=True)


def dot(left, right):
    return jnp.dot(left, right, preferred_element_type=F32)


def dot_right_t(left, right):
    return lax.dot_general(left, right, (((1,), (1,)), ((), ())), preferred_element_type=F32)


def dot_left_t(left, right):
    return lax.dot_general(left, right, (((0,), (0,)), ((), ())), preferred_element_type=F32)


def head_diagonal(rows):
    lane_head = lax.broadcasted_iota(jnp.int32, rows.shape, 1) // HD
    return jnp.concatenate(
        [jnp.where(lane_head == h, rows, jnp.zeros_like(rows)) for h in range(QUAD)], axis=0
    )


def diagonal_rows(full):
    lane_head = lax.broadcasted_iota(jnp.int32, (HD, WIDE), 1) // HD
    out = full[:HD]
    for h in range(1, QUAD):
        out = jnp.where(lane_head == h, full[h * HD : (h + 1) * HD], out)
    return out


def key_rows(keys_at, b, count):
    return [pl.ds(pl.multiple_of(keys_at[b, i] * BLK, BLK), BLK) for i in range(count)]


def stacked(ref, places):
    return jnp.concatenate([ref[p, :] for p in places], axis=0)


def row_sums(x):
    return jnp.sum(x.reshape(x.shape[0] // 8, 8, WIDE), axis=0)


def for_steps(steps, body):
    for n in range(1, STEPS + 1):
        pl.when(steps == n)(functools.partial(body, n * STEP))


def forward_kernel(keys_at, steps_of, q_ref, k_ref, v_ref, bias_ref, out_ref, log_ref):
    def one_block(b, carry):
        rows = pl.ds(pl.multiple_of(b * BLK, BLK), BLK)

        def attend(count):
            places = key_rows(keys_at, b, count)
            query = head_diagonal(q_ref[rows, :])
            raw = dot_right_t(stacked(k_ref, places), query)
            scores, peak = [], None
            for i in range(count):
                piece = raw[i * BLK : (i + 1) * BLK] + bias_ref[b, i : i + 1, :]
                scores.append(piece)
                high = jnp.max(piece.reshape(BLK // 8, 8, WIDE), axis=0)
                peak = high if peak is None else jnp.maximum(peak, high)
            peak = jnp.max(peak, axis=0, keepdims=True)
            total, weights = None, []
            for piece in scores:
                exponent = jnp.exp(piece - peak)
                part = row_sums(exponent)
                total = part if total is None else total + part
                weights.append(exponent.astype(BF))
            total = jnp.sum(total, axis=0, keepdims=True)
            mix = dot_left_t(jnp.concatenate(weights, axis=0), stacked(v_ref, places))
            column = jnp.transpose(jnp.broadcast_to(total, (128, WIDE)))
            mix = mix / jnp.concatenate([column, column], axis=1)
            out_ref[rows, :] = diagonal_rows(mix).astype(BF)
            log_ref[b] = peak + jnp.log(total)

        for_steps(steps_of[b], attend)
        return carry

    lax.fori_loop(0, q_ref.shape[0] // BLK, one_block, 0)


def backward_kernel(
    keys_at,
    steps_of,
    q_ref,
    k_ref,
    v_ref,
    bias_ref,
    log_ref,
    d_ref,
    own_ref,
    in_ref,
    wk_ref,
    wv_ref,
    dq_ref,
    others_ref,
    grad_ref,
    dkey,
    dvalue,
    low,
    back_sum,
):
    dkey[...] = jnp.zeros_like(dkey)
    dvalue[...] = jnp.zeros_like(dvalue)

    def one_block(b, carry):
        rows = pl.ds(pl.multiple_of(b * BLK, BLK), BLK)

        def attend(count):
            places = key_rows(keys_at, b, count)
            query = head_diagonal(q_ref[rows, :])
            d_mixed = head_diagonal(d_ref[rows, :])
            logs = log_ref[b]
            keys = stacked(k_ref, places)
            raw = dot_right_t(keys, query)
            back = dot_right_t(stacked(v_ref, places), d_mixed)
            probs, inner = [], None
            for i in range(count):
                at = slice(i * BLK, (i + 1) * BLK)
                prob = jnp.exp(raw[at] + (bias_ref[b, i : i + 1, :] - logs))
                probs.append(prob)
                part = row_sums(prob * back[at])
                inner = part if inner is None else inner + part
            grad = dot(jnp.concatenate([p.astype(BF) for p in probs], axis=0), d_mixed)
            for i, p in enumerate(places):
                dvalue[p, :] += grad[i * BLK : (i + 1) * BLK]
            inner = jnp.sum(inner, axis=0, keepdims=True)
            d_score = jnp.concatenate(
                [
                    (prob * (back[i * BLK : (i + 1) * BLK] - inner)).astype(BF)
                    for i, prob in enumerate(probs)
                ],
                axis=0,
            )
            grad = dot(d_score, query)
            for i, p in enumerate(places):
                dkey[p, :] += grad[i * BLK : (i + 1) * BLK]
            d_query = dot_left_t(d_score, keys)
            dq_ref[rows, :] = (diagonal_rows(d_query) * (HD**-0.5)).astype(BF)

        for_steps(steps_of[b], attend)
        return carry

    lax.fori_loop(0, q_ref.shape[0] // BLK, one_block, 0)

    low[0] = dkey[...].astype(BF)
    low[1] = dvalue[...].astype(BF)
    grad_ref[:, :WIDE] = dot_left_t(own_ref[...], dq_ref[...]).astype(BF)
    grad_ref[:, WIDE : 2 * WIDE] = dot_left_t(in_ref[...], low[0]).astype(BF)
    grad_ref[:, 2 * WIDE :] = dot_left_t(in_ref[...], low[1]).astype(BF)
    quad = pl.program_id(0)

    def others(r, carry):
        at = pl.ds(pl.multiple_of(r * WIDE, WIDE), WIDE)
        part = dot_right_t(low[0, at, :], wk_ref[...]) + dot_right_t(low[1, at, :], wv_ref[...])
        so_far = jnp.where(quad == 0, jnp.zeros_like(part), back_sum[at, :]) + part
        back_sum[at, :] = so_far
        others_ref[at, :] = so_far.astype(BF)
        return carry

    lax.fori_loop(0, in_ref.shape[0] // WIDE, others, 0)


SHORT = pl.CostEstimate(flops=1_000_000, bytes_accessed=1_000_000, transcendentals=0)
MESH_ID = pl.DeviceIdType.MESH
CALL_GATHER_FIRST, CALL_GATHER, CALL_REDUCE, CALL_NORMS, CALL_ROWS, CALL_LINE_FFN, CALL_LINE_ATTN, CALL_BOTH = range(8)


def quad_places():
    me = lax.axis_index("quad")
    mate = me + 1 - 2 * (me % 2)
    return me, mate, (me + 2) % QUAD, (mate + 2) % QUAD


def greet(*peers):
    barrier = pltpu.get_barrier_semaphore()
    for peer in peers:
        pl.semaphore_signal(barrier, inc=1, device_id=peer, device_id_type=MESH_ID)
    pl.semaphore_wait(barrier, len(peers))


def block_at(block, size, start=0, rows=None):
    return pl.ds(pl.multiple_of(block * size + start, 16), size if rows is None else rows)


def line_peers(parts):
    plane = lax.axis_index("tensor")
    return [{"tensor": (plane + by) % parts} for by in range(1, parts)]


def lines_start(parts, groups, owns, outs, keep_sem, send_sem, recv_sem):
    peers = line_peers(parts)
    copies, kept, n = [], [], 0
    for count, out in zip(groups, outs):
        for kind in range(count):
            own = owns[n]
            width = own.shape[1]
            kept.append(
                pltpu.make_async_copy(own, out.at[:, pl.ds(kind * parts * width, width)], keep_sem.at[n])
            )
            kept[-1].start()
            for by in range(1, parts):
                copy = pltpu.make_async_remote_copy(
                    src_ref=own,
                    dst_ref=out.at[:, pl.ds((kind * parts + by) * width, width)],
                    send_sem=send_sem.at[n, by - 1],
                    recv_sem=recv_sem.at[n, by - 1],
                    device_id=peers[by - 1],
                    device_id_type=MESH_ID,
                )
                copy.start()
                copies.append(copy)
            n += 1
    return copies, kept


def lines_finish(copies, kept):
    for copy in copies + kept:
        copy.wait()


def lines_shapes(parts, groups):
    owns = [own for group in groups for own in group]
    shapes = [
        jax.ShapeDtypeStruct((group[0].shape[0], parts * len(group) * group[0].shape[1]), BF)
        for group in groups
    ]
    dma, count = pltpu.SemaphoreType.DMA, max(len(owns), 1)
    return owns, shapes, [dma((count,)), dma((count, parts - 1)), dma((count, parts - 1))]


def gather_kernel(pieces, parts_along, groups, *refs):
    count, lines = len(pieces), sum(groups)
    at = [count, count + lines, 2 * count + lines, 2 * count + lines + len(groups)]
    owns, line_owns = refs[: at[0]], refs[at[0] : at[1]]
    outs, line_outs = refs[at[1] : at[2]], refs[at[2] : at[3]]
    keep_sem, mate_send, mate_recv, far_send, far_recv, on_send, on_recv = refs[at[3] : at[3] + 7]
    me, mate, far, cross = quad_places()
    greet({"quad": mate}, {"quad": far}, *(line_peers(parts_along) if groups else []))

    def send(source, target, sends, recvs, at, peer):
        return pltpu.make_async_remote_copy(
            src_ref=source,
            dst_ref=target,
            send_sem=sends.at[at],
            recv_sem=recvs.at[at],
            device_id={"quad": peer},
            device_id_type=MESH_ID,
        )

    parts = []
    for n in range(count):
        size = owns[n].shape[0]
        step = size // pieces[n]
        for p in range(pieces[n]):
            parts.append((n, size, p * step, step))
    to_far = [
        send(owns[n].at[pl.ds(start, step)], outs[n].at[block_at(me, size, start, step)], far_send, far_recv, i, far)
        for i, (n, size, start, step) in enumerate(parts)
    ]
    for copy in to_far:
        copy.start()
    to_mate = [
        send(owns[n], outs[n].at[block_at(me, owns[n].shape[0])], mate_send, mate_recv, n, mate)
        for n in range(count)
    ]
    for copy in to_mate:
        copy.start()
    along = lines_start(parts_along, groups, line_owns, line_outs, *refs[at[3] + 7 :])
    kept = [
        pltpu.make_async_copy(owns[n], outs[n].at[block_at(me, owns[n].shape[0])], keep_sem.at[n])
        for n in range(count)
    ]
    for copy in kept:
        copy.start()
    onward = []
    for i, (n, size, start, step) in enumerate(parts):
        to_far[i].wait_recv()
        came = outs[n].at[block_at(far, size, start, step)]
        copy = send(came, came, on_send, on_recv, i, mate)
        copy.start()
        onward.append(copy)
    for copy in to_mate + onward:
        copy.wait()
    for copy in to_far:
        copy.wait_send()
    for copy in kept:
        copy.wait()
    lines_finish(*along)


def quad_gather(arrays, pieces, call, parts=1, groups=()):
    count, total = len(arrays), sum(pieces)
    sems = [pltpu.SemaphoreType.DMA((k,)) for k in (count, count, count, total, total, total, total)]
    owns, shapes, line_sems = lines_shapes(max(parts, 2), groups)
    return pl.pallas_call(
        functools.partial(gather_kernel, pieces, parts, tuple(len(g) for g in groups)),
        out_shape=[jax.ShapeDtypeStruct((QUAD * x.shape[0],) + x.shape[1:], x.dtype) for x in arrays]
        + shapes,
        in_specs=[pl.BlockSpec(memory_space=pltpu.VMEM)] * (count + len(owns)),
        out_specs=[pl.BlockSpec(memory_space=pl.ANY)] * (count + len(shapes)),
        scratch_shapes=sems + line_sems,
        compiler_params=pltpu.CompilerParams(collective_id=call, has_side_effects=True),
        cost_estimate=SHORT,
        name="quad_gather",
    )(*arrays, *owns)


REDUCE_PIECES = 8


def reduce_kernel(
    parts_ref,
    out_ref,
    near,
    relay,
    beyond,
    mate_send,
    mate_recv,
    own_send,
    own_recv,
    far_send,
    far_recv,
    greeted=False,
):
    me, mate, far, cross = quad_places()
    if not greeted:
        greet({"quad": mate}, {"quad": far})
    size = out_ref.shape[0]
    step = size // REDUCE_PIECES

    def send(source, target, send_sem, recv_sem, peer):
        copy = pltpu.make_async_remote_copy(
            src_ref=source,
            dst_ref=target,
            send_sem=send_sem,
            recv_sem=recv_sem,
            device_id={"quad": peer},
            device_id_type=MESH_ID,
        )
        copy.start()
        return copy

    to_mate = [
        send(
            parts_ref.at[block_at(cross, size, p * step, step)],
            near.at[1, pl.ds(p * step, step)],
            mate_send.at[p],
            mate_recv.at[p],
            mate,
        )
        for p in range(REDUCE_PIECES)
    ]
    own = send(parts_ref.at[block_at(mate, size)], near.at[0], own_send, own_recv, mate)
    to_far = []
    for p in range(REDUCE_PIECES):
        rows = pl.ds(p * step, step)
        to_mate[p].wait_recv()
        mine = parts_ref[block_at(far, size, p * step, step), :].astype(F32)
        relay[rows, :] = (mine + near[1, rows, :].astype(F32)).astype(BF)
        to_far.append(send(relay.at[rows], beyond.at[rows], far_send.at[p], far_recv.at[p], far))
    own.wait_recv()
    for p in range(REDUCE_PIECES):
        rows = pl.ds(p * step, step)
        to_far[p].wait_recv()
        mine = parts_ref[block_at(me, size, p * step, step), :].astype(F32)
        out_ref[rows, :] = mine + near[0, rows, :].astype(F32) + beyond[rows, :].astype(F32)
    for copy in to_mate + [own] + to_far:
        copy.wait_send()


def reduce_scratch(rows, width):
    one, each = pltpu.SemaphoreType.DMA, pltpu.SemaphoreType.DMA((REDUCE_PIECES,))
    low = pltpu.VMEM((rows, width), BF)
    return [pltpu.VMEM((2, rows, width), BF), low, low, each, each, one, one, each, each]


def quad_reduce(parts):
    rows, width = parts.shape[0] // QUAD, parts.shape[1]
    return pl.pallas_call(
        reduce_kernel,
        out_shape=jax.ShapeDtypeStruct((rows, width), F32),
        in_specs=[pl.BlockSpec(memory_space=pltpu.VMEM)],
        out_specs=pl.BlockSpec(memory_space=pltpu.VMEM),
        scratch_shapes=reduce_scratch(rows, width),
        compiler_params=pltpu.CompilerParams(collective_id=CALL_REDUCE, has_side_effects=True),
        cost_estimate=SHORT,
        name="quad_reduce",
    )(parts)


def both_kernel(sizes, planes, parts_ref, *refs):
    count = len(sizes)
    x_refs, out_ref, line_refs, scratch = refs[:count], refs[count], refs[count + 1 :][:count], refs[2 * count + 1 :]
    me, mate, far, cross = quad_places()
    greet({"quad": mate}, {"quad": far}, *line_peers(planes))
    lines = []
    for n in range(count):
        held, came, send_sem, recv_sem = scratch[4 * n : 4 * n + 4]
        lines.append((came, line_start(sizes[n], planes, x_refs[n], held, came, send_sem, recv_sem)))
    reduce_kernel(parts_ref, out_ref, *scratch[4 * count :], greeted=True)
    for n in range(count):
        line_finish(sizes[n], planes, x_refs[n], line_refs[n], *lines[n])


def quad_reduce_and_lines(parts, lines, sizes, planes):
    rows, width = parts.shape[0] // QUAD, parts.shape[1]
    shapes = [(x.shape[0], sum(own)) for x, own in zip(lines, sizes)]
    vmem, count = pl.BlockSpec(memory_space=pltpu.VMEM), len(lines)
    return pl.pallas_call(
        functools.partial(both_kernel, tuple(sizes), planes),
        out_shape=[jax.ShapeDtypeStruct((rows, width), F32)]
        + [jax.ShapeDtypeStruct(shape, F32) for shape in shapes],
        in_specs=[vmem] * (1 + count),
        out_specs=[vmem] * (1 + count),
        scratch_shapes=sum([line_scratch(shape, planes) for shape in shapes], [])
        + reduce_scratch(rows, width),
        compiler_params=pltpu.CompilerParams(collective_id=CALL_BOTH, has_side_effects=True),
        cost_estimate=SHORT,
        name="quad_reduce_and_lines",
    )(parts, *lines)


def norms_kernel(hops, x_ref, out_ref, held, came, send_sem, recv_sem):
    peers = []
    for axis, bit in hops:
        at = lax.axis_index(axis)
        peers.append({axis: at + bit - 2 * bit * ((at // bit) % 2)})
    greet(*peers)
    for n, peer in enumerate(peers):
        source = x_ref if n == 0 else held.at[n]
        copy = pltpu.make_async_remote_copy(
            src_ref=source,
            dst_ref=came.at[n],
            send_sem=send_sem.at[n],
            recv_sem=recv_sem.at[n],
            device_id=peer,
            device_id_type=MESH_ID,
        )
        copy.start()
        copy.wait()
        total = source[...] + came[n]
        if n == len(peers) - 1:
            out_ref[...] = total
        else:
            held[n + 1] = total


def sum_everywhere(x):
    hops = []
    for axis in ("quad", "row", "tensor", "hi"):
        bit = 1
        while bit < lax.axis_size(axis):
            hops.append((axis, bit))
            bit *= 2
    vmem = pltpu.VMEM((len(hops),) + x.shape, x.dtype)
    return pl.pallas_call(
        functools.partial(norms_kernel, tuple(hops)),
        out_shape=jax.ShapeDtypeStruct(x.shape, x.dtype),
        in_specs=[pl.BlockSpec(memory_space=pltpu.VMEM)],
        out_specs=pl.BlockSpec(memory_space=pltpu.VMEM),
        scratch_shapes=[
            vmem,
            vmem,
            pltpu.SemaphoreType.DMA((len(hops),)),
            pltpu.SemaphoreType.DMA((len(hops),)),
        ],
        compiler_params=pltpu.CompilerParams(collective_id=CALL_NORMS, has_side_effects=True),
        cost_estimate=SHORT,
        name="sum_everywhere",
    )(x)


def rows_kernel(parts, groups, own_ref, *refs):
    lines = sum(groups)
    line_owns, out_ref, line_outs = refs[:lines], refs[lines], refs[lines + 1 : lines + 1 + len(groups)]
    keep_sem, line_send, line_recv, send_sem, recv_sem = refs[lines + 1 + len(groups) :][:5]
    line_sems = refs[lines + 1 + len(groups) :][5:]
    me, mate, far, cross = quad_places()
    row, plane = lax.axis_index("row"), lax.axis_index("tensor")
    other = 1 - row
    line = [{"tensor": (plane + by) % parts} for by in range(1, parts)]
    to_x, to_y, to_mate = {"quad": far}, {"row": other}, {"quad": mate}
    greet(*line, to_x, to_y, to_mate)
    size, width = own_ref.shape

    def block(at_row, at_quad, part):
        return out_ref.at[block_at(at_row * QUAD + at_quad, size), pl.ds(part * width, width)]

    used = []

    def send(source, target, peer, n):
        copy = pltpu.make_async_remote_copy(
            src_ref=source,
            dst_ref=target,
            send_sem=send_sem.at[n],
            recv_sem=recv_sem.at[n],
            device_id=peer,
            device_id_type=MESH_ID,
        )
        copy.start()
        used.append(copy)
        return copy

    along = []
    for by in range(1, parts):
        copy = pltpu.make_async_remote_copy(
            src_ref=own_ref,
            dst_ref=block(row, me, by),
            send_sem=line_send.at[by - 1],
            recv_sem=line_recv.at[by - 1],
            device_id=line[by - 1],
            device_id_type=MESH_ID,
        )
        copy.start()
        along.append(copy)
    keep = pltpu.make_async_copy(own_ref, block(row, me, 0), keep_sem)
    keep.start()
    only_line = lines_start(parts, groups, line_owns, line_outs, *line_sems)
    near_x, near_y, beyond, mates = [], [], [], []
    for part in range(parts + 1):
        if part < parts:
            if part:
                along[part - 1].wait_recv()
            source = own_ref if part == 0 else block(row, me, part)
            target = block(row, me, part)
            near_x.append(send(source, target, to_x, part))
            near_y.append(send(source, target, to_y, parts + part))
            mates.append(send(source, target, to_mate, 2 * parts + part))
        if part:
            done = part - 1
            from_x, from_y = block(row, far, done), block(other, me, done)
            near_x[done].wait_recv()
            near_y[done].wait_recv()
            if done % 2:
                beyond.append(send(from_y, from_y, to_x, 3 * parts + done))
            else:
                beyond.append(send(from_x, from_x, to_y, 3 * parts + done))
            mates.append(send(from_x, from_x, to_mate, 4 * parts + done))
            mates.append(send(from_y, from_y, to_mate, 5 * parts + done))
    for part in range(parts):
        beyond[part].wait_recv()
        came = block(other, far, part)
        mates.append(send(came, came, to_mate, 6 * parts + part))
    for copy in mates:
        copy.wait_recv()
    for copy in along + used:
        copy.wait_send()
    keep.wait()
    lines_finish(*only_line)


def gather_rows(rows, parts, groups):
    size, width = rows.shape
    dma = pltpu.SemaphoreType.DMA
    owns, shapes, line_sems = lines_shapes(parts, groups)
    return pl.pallas_call(
        functools.partial(rows_kernel, parts, tuple(len(g) for g in groups)),
        out_shape=[jax.ShapeDtypeStruct((ROW * QUAD * size, parts * width), rows.dtype)] + shapes,
        in_specs=[pl.BlockSpec(memory_space=pltpu.VMEM)] * (1 + len(owns)),
        out_specs=[pl.BlockSpec(memory_space=pl.ANY)] * (1 + len(shapes)),
        scratch_shapes=[dma, dma((parts - 1,)), dma((parts - 1,)), dma((7 * parts,)), dma((7 * parts,))]
        + line_sems,
        compiler_params=pltpu.CompilerParams(collective_id=CALL_ROWS, has_side_effects=True),
        cost_estimate=SHORT,
        name="gather_rows",
    )(rows, *owns)


def regroup_kernel(parts, kinds, x_ref, out_ref):
    size = x_ref.shape[1] // (parts * kinds)
    for kind in range(kinds):
        for part in range(parts):
            to, at = (kind * parts + part) * size, (part * kinds + kind) * size
            out_ref[:, to : to + size] = x_ref[:, at : at + size]


def regroup(rows, parts, kinds):
    steps = max(rows.shape[0] // 192, 1)
    block = pl.BlockSpec((rows.shape[0] // steps, rows.shape[1]), lambda i: (i, 0))
    return pl.pallas_call(
        functools.partial(regroup_kernel, parts, kinds),
        out_shape=jax.ShapeDtypeStruct(rows.shape, rows.dtype),
        grid=(steps,),
        in_specs=[block],
        out_specs=block,
        cost_estimate=SHORT,
        name="regroup",
    )(rows)


def line_pick(sizes, parts, x_ref, part):
    columns, start = [], 0
    for size in sizes:
        columns.append(x_ref[:, start + part * size : start + (part + 1) * size])
        start += parts * size
    return jnp.concatenate(columns, axis=1)


def line_start(sizes, parts, x_ref, held, came, send_sem, recv_sem):
    plane = lax.axis_index("tensor")
    copies = []
    for by in range(1, parts):
        held[by - 1] = line_pick(sizes, parts, x_ref, by)
        copy = pltpu.make_async_remote_copy(
            src_ref=held.at[by - 1],
            dst_ref=came.at[by - 1],
            send_sem=send_sem.at[by - 1],
            recv_sem=recv_sem.at[by - 1],
            device_id={"tensor": (plane + parts - by) % parts},
            device_id_type=MESH_ID,
        )
        copy.start()
        copies.append(copy)
    return copies


def line_finish(sizes, parts, x_ref, out_ref, came, copies):
    total = line_pick(sizes, parts, x_ref, 0).astype(F32)
    for by in range(1, parts):
        copies[by - 1].wait_recv()
        total = total + came[by - 1].astype(F32)
    out_ref[...] = total
    for copy in copies:
        copy.wait_send()


def line_scratch(shape, parts):
    dma = pltpu.SemaphoreType.DMA((parts - 1,))
    return [pltpu.VMEM((parts - 1,) + shape, BF), pltpu.VMEM((parts - 1,) + shape, BF), dma, dma]


def parts_kernel(sizes, parts, x_ref, out_ref, held, came, send_sem, recv_sem):
    greet(*line_peers(parts))
    copies = line_start(sizes, parts, x_ref, held, came, send_sem, recv_sem)
    line_finish(sizes, parts, x_ref, out_ref, came, copies)


def sum_line(rows, sizes, parts, call):
    shape = (rows.shape[0], sum(sizes))
    return pl.pallas_call(
        functools.partial(parts_kernel, sizes, parts),
        out_shape=jax.ShapeDtypeStruct(shape, F32),
        in_specs=[pl.BlockSpec(memory_space=pltpu.VMEM)],
        out_specs=pl.BlockSpec(memory_space=pltpu.VMEM),
        scratch_shapes=line_scratch(shape, parts),
        compiler_params=pltpu.CompilerParams(collective_id=call, has_side_effects=True),
        cost_estimate=SHORT,
        name="sum_line",
    )(rows)


def attend_forward(query, keyval, tables):
    keys_at, steps_of, bias = tables
    own, width = query.shape
    quads = width // WIDE
    rows = keyval.shape[0]
    blocks = own // BLK
    return pl.pallas_call(
        forward_kernel,
        grid_spec=pltpu.PrefetchScalarGridSpec(
            num_scalar_prefetch=2,
            grid=(quads,),
            in_specs=[
                pl.BlockSpec((own, WIDE), lambda i, *_: (0, i)),
                pl.BlockSpec((rows, WIDE), lambda i, *_: (0, i)),
                pl.BlockSpec((rows, WIDE), lambda i, *_: (0, i + quads)),
                pl.BlockSpec((blocks, LONGEST, WIDE), lambda i, *_: (0, 0, i)),
            ],
            out_specs=[
                pl.BlockSpec((own, WIDE), lambda i, *_: (0, i)),
                pl.BlockSpec((blocks, 1, WIDE), lambda i, *_: (0, 0, i)),
            ],
        ),
        out_shape=[
            jax.ShapeDtypeStruct((own, width), BF),
            jax.ShapeDtypeStruct((blocks, 1, width), F32),
        ],
        cost_estimate=SHORT,
        name="attend_forward",
    )(keys_at, steps_of, query, keyval, keyval, bias)


def attend_backward(query, keyval, logs, d_mixed, tables, own_inputs, inputs, attn_w):
    keys_at, steps_of, bias = tables
    own, width = query.shape
    quads = width // WIDE
    rows, depth = inputs.shape
    blocks = own // BLK
    once = pl.Buffered(1)
    return pl.pallas_call(
        backward_kernel,
        grid_spec=pltpu.PrefetchScalarGridSpec(
            num_scalar_prefetch=2,
            grid=(quads,),
            in_specs=[
                pl.BlockSpec((own, WIDE), lambda i, *_: (0, i)),
                pl.BlockSpec((rows, WIDE), lambda i, *_: (0, i)),
                pl.BlockSpec((rows, WIDE), lambda i, *_: (0, i + quads)),
                pl.BlockSpec((blocks, LONGEST, WIDE), lambda i, *_: (0, 0, i)),
                pl.BlockSpec((blocks, 1, WIDE), lambda i, *_: (0, 0, i)),
                pl.BlockSpec((own, WIDE), lambda i, *_: (0, i)),
                pl.BlockSpec((own, depth), lambda i, *_: (0, 0), pipeline_mode=once),
                pl.BlockSpec((rows, depth), lambda i, *_: (0, 0), pipeline_mode=once),
                pl.BlockSpec((depth, WIDE), lambda i, *_: (0, i + quads)),
                pl.BlockSpec((depth, WIDE), lambda i, *_: (0, i + 2 * quads)),
            ],
            out_specs=[
                pl.BlockSpec((own, WIDE), lambda i, *_: (0, i)),
                pl.BlockSpec((rows, depth), lambda i, *_: (0, 0)),
                pl.BlockSpec((depth, 3 * WIDE), lambda i, *_: (0, i)),
            ],
            scratch_shapes=[
                pltpu.VMEM((rows, WIDE), F32),
                pltpu.VMEM((rows, WIDE), F32),
                pltpu.VMEM((2, rows, WIDE), BF),
                pltpu.VMEM((rows, depth), F32),
            ],
        ),
        out_shape=[
            jax.ShapeDtypeStruct((own, width), BF),
            jax.ShapeDtypeStruct((rows, depth), BF),
            jax.ShapeDtypeStruct((depth, 3 * width), BF),
        ],
        cost_estimate=SHORT,
        name="attend_backward",
    )(keys_at, steps_of, query, keyval, keyval, bias, logs, d_mixed, own_inputs, inputs, attn_w, attn_w)


def weights_kernel(steps, ffn_ref, two_ref, one_ref, pre_ref, act_ref, mixed_ref, out_ref, left):
    i = pl.program_id(0)
    for start, ref in ((0, ffn_ref), (steps, two_ref), (2 * steps, one_ref)):

        @pl.when(i == start)
        def _():
            left[...] = jnp.transpose(ref[...])

    for start, ref in ((0, pre_ref), (steps, act_ref), (2 * steps, mixed_ref)):

        @pl.when((i >= start) & (i < start + steps))
        def _():
            out_ref[...] = dot(left[...], ref[...]).astype(BF)


def weight_grads(ffn_in, d_two, d_one, d_pre, activated, mixed):
    own, depth = ffn_in.shape
    steps = d_pre.shape[1] // depth
    last = steps - 1
    whole = pl.BlockSpec((own, depth), lambda i: (0, 0), pipeline_mode=pl.Buffered(1))
    return pl.pallas_call(
        functools.partial(weights_kernel, steps),
        grid=(2 * steps + 1,),
        in_specs=[
            whole,
            whole,
            whole,
            pl.BlockSpec((own, depth), lambda i: (0, jnp.minimum(i, last))),
            pl.BlockSpec((own, depth), lambda i: (0, jnp.clip(i - steps, 0, last))),
            whole,
        ],
        out_specs=pl.BlockSpec((depth, depth), lambda i: (0, i)),
        out_shape=jax.ShapeDtypeStruct((depth, (2 * steps + 1) * depth), BF),
        scratch_shapes=[pltpu.VMEM((depth, own), BF)],
        cost_estimate=SHORT,
        name="weight_grads",
    )(ffn_in, d_two, d_one, d_pre, activated, mixed)


def attention_tables(doc_lengths, block_deal, random_rows, own_blocks, first_own):
    blocks = block_deal.shape[0]
    doc_ends = jnp.cumsum(doc_lengths)
    doc_starts = doc_ends - doc_lengths
    place = jnp.arange(blocks, dtype=jnp.int32)
    stored_at = jnp.sum(
        jnp.where(block_deal[None, :] == place[:, None], place[None, :], 0), axis=1
    )
    own = lax.dynamic_slice(block_deal, (first_own,), (own_blocks,))
    doc_index = jnp.sum((own[:, None] >= doc_ends[None, :]).astype(jnp.int32), axis=1)
    doc_pick = (
        doc_index[:, None] == jnp.arange(doc_lengths.shape[0], dtype=jnp.int32)[None, :]
    ).astype(jnp.int32)
    first_block = jnp.sum(doc_pick * doc_starts[None, :], axis=1)
    doc_blocks = jnp.sum(doc_pick * doc_lengths[None, :], axis=1)
    local = own - first_block
    other = jnp.arange(LONGEST, dtype=jnp.int32)
    wanted = jnp.minimum(first_block[:, None] + other[None, :], blocks - 1)
    keys_at = jnp.sum(
        jnp.where(wanted[:, :, None] == place[None, None, :], stored_at[None, None, :], 0), axis=2
    )
    own_pick = (own[:, None] == place[None, :]).astype(jnp.int32)
    picks = jnp.sum(own_pick[None, :, :, None] * random_rows[:, None, :, :], axis=2)
    picks = jnp.remainder(picks, doc_blocks[None, :, None])
    random_hit = jnp.any(picks[:, :, :, None] == other[None, None, None, :], axis=2)
    inside = other[None, :] < doc_blocks[:, None]
    near = jnp.abs(local[:, None] - other[None, :]) <= 1
    everywhere = (local[:, None] < 2) | (other[None, :] < 2)
    allowed = inside[None] & ((near | everywhere)[None] | random_hit)
    bias = jnp.where(allowed, 0.0, MASK_VALUE).astype(F32)
    bias = jnp.repeat(bias.transpose(1, 2, 0), BLK, axis=2)
    steps_of = (doc_blocks + STEP - 1) // STEP
    return keys_at, steps_of, bias


def to_home(steps, parts):
    pairs = []
    for hi in range(steps):
        for row in range(ROW):
            for quad in range(QUAD):
                side, core = quad // 2, quad % 2
                plane = parts - 1 - side if core else side
                for part in range(parts):
                    source = ((hi * ROW + row) * QUAD + quad) * parts + part
                    target = ((hi * ROW + row) * QUAD + part) * parts + plane
                    pairs.append((source, target))
    return pairs


def local(
    layer_input,
    w_qkv,
    w_out,
    w_up,
    w_down,
    attn_gain,
    attn_shift,
    ffn_gain,
    ffn_shift,
    out_grad,
    doc_lengths,
    block_deal,
    random_blocks,
):
    own_rows, width = layer_input.shape
    tensor = lax.axis_size("tensor")
    slot = lax.axis_index("quad")
    plane = lax.axis_index("tensor")
    head_local = random_blocks.shape[1]
    chunk = head_local * HD
    depth = w_qkv.shape[1]
    hidden = w_up.shape[2]
    score_scale = HD ** (-0.5)
    moves = to_home(lax.axis_size("hi"), tensor)
    moves_back = [(b, a) for a, b in moves]

    def shifted(x, by):
        return lax.ppermute(x, "tensor", [(i, (i + by) % tensor) for i in range(tensor)])

    def spread(shard):
        return [shard] + [shifted(shard, by) for by in range(1, tensor)]

    def by_kind(parts, kinds):
        rows = jnp.stack([part.reshape(depth, kinds, -1) for part in parts], axis=2)
        return rows.reshape(depth, -1)

    def attn_shard(qkv, back):
        qkv = qkv.reshape(depth, head_local, 3, HD).transpose(0, 2, 1, 3)
        return jnp.concatenate([qkv.reshape(depth, 3 * chunk), back.T], axis=1)

    def over_data(rows):
        return lax.all_gather(rows, DATA, axis=0, tiled=True)

    docs, group_blocks = doc_lengths.shape[1], block_deal.shape[1]
    numbers = jnp.concatenate([doc_lengths[0], block_deal[0], random_blocks[0].reshape(-1)])
    numbers = jnp.stack([numbers // BLK, numbers % BLK]).astype(BF)
    numbers = jnp.pad(numbers, ((0, 14), (0, width - numbers.shape[1])))
    own_numbers = lax.ppermute(numbers, EVERY, moves)
    own_tokens = lax.ppermute(layer_input, EVERY, moves)
    ffn_shards = [w_up[0], w_down[0].T]
    if lax.axis_size("hi") == 1:
        rows, first_rows = gather_rows(attn_shard(w_qkv[0], w_out[0]), tensor, [ffn_shards])
        rows, first_rows, own_tokens, own_numbers = lax.optimization_barrier(
            (rows, first_rows, own_tokens, own_numbers)
        )
        attn_full = [regroup(rows, tensor, 4)]
    else:
        attn_full = [over_data(by_kind(spread(attn_shard(w_qkv[0], w_out[0])), 4))]
        first_rows = by_kind(spread(jnp.concatenate(ffn_shards, axis=1)), 2)
    ffn_full = [over_data(first_rows)]

    groups = []
    for layer in range(1, LAYERS):
        groups += [[attn_shard(w_qkv[layer], w_out[layer])], [w_up[layer], w_down[layer].T]]
    inputs, numbers, *later = quad_gather(
        [own_tokens, own_numbers], [8, 1], CALL_GATHER_FIRST, tensor, groups
    )
    numbers = numbers.reshape(QUAD, 16, width)[:, :2].astype(jnp.int32)
    numbers = numbers[:, 0] * BLK + numbers[:, 1]
    lengths, deal = numbers[0, :docs], numbers[0, docs : docs + group_blocks]
    random_home = numbers[:, docs + group_blocks :][:, : random_blocks.size]
    random_home = random_home.reshape(tensor, head_local, group_blocks, -1)
    part_of = (plane - jnp.arange(tensor, dtype=jnp.int32)) % tensor
    part_pick = (part_of[:, None] == jnp.arange(tensor, dtype=jnp.int32)[None, :]).astype(jnp.int32)
    random_home = jnp.sum(part_pick[:, :, None, None, None] * random_home[None], axis=1)
    random_home = random_home.reshape(tensor * head_local, group_blocks, -1)
    own_blocks = own_rows // BLK
    tables = attention_tables(
        lengths,
        deal,
        random_home,
        own_blocks,
        slot * own_blocks,
    )

    stream = own_tokens.astype(F32)
    stored = []
    for layer in range(LAYERS):
        attn_w, ffn_w = attn_full[layer], ffn_full[layer]
        w_query = attn_w[:, :width]
        w_keyval = attn_w[:, width : 3 * width]
        w_back_t = attn_w[:, 3 * width :]
        w_expand = ffn_w[:, : hidden * tensor]
        w_shrink_t = ffn_w[:, hidden * tensor :]
        own_inputs = stream.astype(BF)
        if layer > 0:
            (inputs,) = quad_gather([own_inputs], [8], CALL_GATHER)
        query = (dot(own_inputs, w_query).astype(BF).astype(F32) * score_scale).astype(BF)
        keyval = dot(inputs, w_keyval).astype(BF)
        if layer < LAYERS - 1:
            attn_full.append(over_data(regroup(later[2 * layer], tensor, 4)))
            ffn_full.append(over_data(later[2 * layer + 1]))
        mixed, logs = attend_forward(query, keyval, tables)
        if layer == 0:
            mixed, own_grad = lax.optimization_barrier((mixed, out_grad))
            own_grad = lax.ppermute(own_grad, EVERY, moves)
        summed_one = stream + dot_right_t(mixed, w_back_t)
        normed = layer_norm(summed_one, attn_gain[layer], attn_shift[layer])
        ffn_in = normed.astype(BF)
        pre_act = dot(ffn_in, w_expand)
        activated = gelu_tanh(pre_act).astype(BF)
        summed_two = normed + dot_right_t(activated, w_shrink_t)
        stored.append(
            (own_inputs, inputs, query, keyval, mixed, logs, summed_one, ffn_in, pre_act, activated, summed_two)
        )
        stream = layer_norm(summed_two, ffn_gain[layer], ffn_shift[layer])
    layer_output = lax.ppermute(stream.astype(BF), EVERY, moves_back)

    def line_parts(rows, sizes):
        pieces, start = [], 0
        for size in sizes:
            pieces.append(rows[:, start : start + tensor * size].reshape(depth, tensor, size))
            start += tensor * size
        parts = [jnp.concatenate([p[:, by] for p in pieces], axis=1) for by in range(tensor)]
        return parts[:1] + [shifted(parts[by], tensor - by) for by in range(1, tensor)]

    def by_piece(rows):
        rows = rows.reshape(depth, -1, 3, WIDE).transpose(0, 2, 1, 3)
        return rows.reshape(depth, 3 * width)

    def sum_data(part):
        return lax.psum_scatter(part, DATA, scatter_dimension=0, tiled=True)

    state_grad = own_grad.astype(F32)
    attn_sums = [None] * LAYERS
    attn_grads = [None] * LAYERS
    ffn_grads = [None] * LAYERS
    norm_parts = [None] * LAYERS
    for layer in reversed(range(LAYERS)):
        (own_inputs, inputs, query, keyval, mixed, logs, summed_one, ffn_in, pre_act, activated, summed_two) = stored[layer]
        attn_w, ffn_w = attn_full[layer], ffn_full[layer]
        w_query = attn_w[:, :width]
        w_keyval = attn_w[:, width : 3 * width]
        w_back_t = attn_w[:, 3 * width :]
        w_expand = ffn_w[:, : hidden * tensor]
        w_shrink_t = ffn_w[:, hidden * tensor :]
        unused_two, ffn_back = jax.vjp(layer_norm, summed_two, ffn_gain[layer], ffn_shift[layer])
        d_two, ffn_gain_part, ffn_shift_part = ffn_back(state_grad)
        d_two_low = d_two.astype(BF)
        unused_act, gelu_back = jax.vjp(gelu_tanh, pre_act)
        d_pre = gelu_back(dot(d_two_low, w_shrink_t))[0].astype(BF)
        d_normed = d_two + dot_right_t(d_pre, w_expand)
        unused_one, attn_back = jax.vjp(layer_norm, summed_one, attn_gain[layer], attn_shift[layer])
        d_one, attn_gain_part, attn_shift_part = attn_back(d_normed)
        norm_parts[layer] = (attn_gain_part, attn_shift_part, ffn_gain_part, ffn_shift_part)
        d_one_low = d_one.astype(BF)
        ffn_part = weight_grads(ffn_in, d_two_low, d_one_low, d_pre, activated, mixed)
        d_one_low, ffn_part = lax.optimization_barrier((d_one_low, ffn_part))
        ffn_sum = sum_data(ffn_part)
        d_mixed = dot(d_one_low, w_back_t).astype(BF)
        if layer < LAYERS - 1:
            norms = jnp.stack([norm_parts[l][k] for k in range(4) for l in range(LAYERS)])
            d_mixed, norms = lax.optimization_barrier((d_mixed, norms))
            norm_sums = sum_everywhere(norms)
            d_mixed, norm_sums, attn_sums[layer + 1] = lax.optimization_barrier(
                (d_mixed, norm_sums, attn_sums[layer + 1])
            )
        if layer == 0:
            d_mixed, ffn_last = lax.optimization_barrier((d_mixed, ffn_last))
            moving = line_parts(ffn_last, (hidden, hidden, chunk))
        d_query, others, attn_part = attend_backward(
            query, keyval, logs, d_mixed, tables, own_inputs, inputs, attn_w
        )
        if layer == 0:
            others, attn_sums[1] = lax.optimization_barrier((others, attn_sums[1]))
            attn_grads[1] = sum_line(by_piece(attn_sums[1]), (chunk,) * 3, tensor, CALL_LINE_ATTN)
            others, ffn_sum, attn_part, attn_grads[1], moving = lax.optimization_barrier(
                (others, ffn_sum, attn_part, attn_grads[1], moving)
            )
            ffn_grads[1] = sum(part.astype(F32) for part in moving)
        else:
            others, layer_output = lax.optimization_barrier((others, layer_output))
        if layer == 0:
            summed, ffn_grads[0] = quad_reduce_and_lines(
                others, [ffn_sum], [(hidden, hidden, chunk)], tensor
            )
        else:
            summed = quad_reduce(others)
            summed, ffn_sum, attn_part = lax.optimization_barrier((summed, ffn_sum, attn_part))
        ffn_last = ffn_sum
        attn_sums[layer] = sum_data(attn_part)
        state_grad = d_one + dot_right_t(d_query, w_query) + summed
    input_grad = lax.ppermute(state_grad.astype(BF), EVERY, moves_back)
    attn_grads[0] = sum_line(by_piece(attn_sums[0]), (chunk,) * 3, tensor, CALL_LINE_ATTN)
    input_grad, attn_grads = lax.optimization_barrier((input_grad, attn_grads))
    input_grad = input_grad.astype(F32)

    qkv_grad = jnp.stack(attn_grads).reshape(LAYERS, depth, 3, head_local, HD)
    qkv_grad = qkv_grad.transpose(0, 1, 3, 2, 4).reshape(LAYERS, depth, 3 * chunk)
    ffn_own = jnp.stack(ffn_grads)
    up_grad = ffn_own[:, :, :hidden]
    down_grad = ffn_own[:, :, hidden : 2 * hidden].transpose(0, 2, 1)
    out_w_grad = ffn_own[:, :, 2 * hidden :].transpose(0, 2, 1)
    return (layer_output, input_grad, qkv_grad, out_w_grad, up_grad, down_grad) + tuple(
        norm_sums[k * LAYERS : (k + 1) * LAYERS] for k in range(4)
    )


def solution(mesh):
    devices = mesh.devices
    tensor = devices.shape[1]
    split = jax.sharding.Mesh(
        devices.reshape(devices.shape[0] // (ROW * QUAD), ROW, QUAD, tensor), EVERY
    )
    placed = (
        P(EVERY, None),
        P(None, DATA, "tensor"),
        P(None, "tensor", DATA),
        P(None, DATA, "tensor"),
        P(None, "tensor", DATA),
        P(),
        P(),
        P(),
        P(),
        P(EVERY, None),
        P(DATA, None),
        P(DATA, None),
        P(DATA, "tensor", None, None),
    )
    return jax.shard_map(
        local,
        mesh=split,
        in_specs=placed,
        out_specs=(
            P(EVERY, None),
            P(EVERY, None),
            P(None, DATA, "tensor"),
            P(None, "tensor", DATA),
            P(None, DATA, "tensor"),
            P(None, "tensor", DATA),
            P(),
            P(),
            P(),
            P(),
        ),
        check_vma=False,
    )
```
